32 devices in a mesh: groups: 2 (over y), row: 8 (over z, x), col: 2 (over core).
Axes of the slice: x: 2, y: 2, z: 4, core: 2. Of those that a mesh axis runs over, the one named last changes fastest.
Arguments:
- wavenumber: float32 [2], P('groups'), parts along dimension 0, may hold values from 30 to 90
- tgt_geom: float32 [6, 4096], P(None, ('groups', 'row')), parts along dimension 1, may hold values from -2 to 8, as said below
- src_geom: float32 [4, 512], P(None, ('groups', 'row', 'col')), parts along dimension 1, may hold values from -2 to 8, as said below
- excite: bfloat16 [128, 512], P(None, ('groups', 'row', 'col')), parts along dimension 1, may hold values from -6 to 6
- tgt_nodes: float32 [3, 6144], P(None, ('groups', 'row')), parts along dimension 1, may hold values from -2 to 8, as said below
- src_nodes: float32 [3, 3072], P(None, ('groups', 'row')), parts along dimension 1, may hold values from -2 to 8, as said below
- tgt_weights: bfloat16 [2, 192, 4096], P(None, None, ('groups', 'row')), parts along dimension 2, may hold values from -0.109375 to 0.109375
- src_weights: bfloat16 [2, 192, 512], P(None, None, ('groups', 'row', 'col')), parts along dimension 2, may hold values from -1 to 1
- near_order: int32 [32, 9], P(('groups', 'row')), parts along dimension 0, may hold values from 0 to 3
Outputs:
- responses: float32 [4096, 128], P(('groups', 'row', 'col')), parts along dimension 0
The draws below stay inside these ranges and needn't reach their ends.
There are 2 independent parts, one for each index of `groups`. The reference program is written for one: setup_inputs(seed, part) draws one part's arguments, and reference() takes and returns one part's arrays. A program takes and returns all parts, laid end to end along the dimension named above; each array names one. Nothing has to cross between parts.
Inputs may be any that keep to these rules, and one draw needn't show every extreme that they name: `tgt_geom`: rows 0 to 2 are points, rows 3 to 5 unit normals. `src_geom`: rows 0 to 2 are points, row 3 positive areas. `tgt_nodes`: Points. `src_nodes`: Points. `near_order`: 0 marks a pair that is not near.
All inputs are finite; a program needn't handle non-finite values.
Results may differ from the reference program's by a relative error of at most 0.0011.
Values may be sent and summed in bfloat16 or wider, within the bound.
A program may use at most 64 MiB of HBM per device.

```python
import jax
import jax.numpy as jnp
from jax import lax

BLK = 128
RBD = 2
CPD = 16
NEXC = 64
QSTEP = 64
ORDERS = 3
NEARW = 4
QN = 192
NBAND = 9
NROWS = 2048
NCOL = 256
N_ROW = 8


ACROSS = 2.0


def line_positions(key, count, per_unit):
    first, second = jax.random.split(key)
    along = (jnp.arange(count, dtype=jnp.float32) + jax.random.uniform(first, (count,), jnp.float32)) / per_unit
    across = jax.random.uniform(second, (2, count), jnp.float32, -ACROSS, ACROSS)
    return jnp.concatenate([along[None, :], across], 0)


def draw_tgt_geom(key, part):
    place_key, normal_key = jax.random.split(jax.random.fold_in(key, 11))
    points = line_positions(place_key, NROWS, BLK * RBD)
    raw = jax.random.normal(normal_key, (3, NROWS), jnp.float32)
    length = jnp.sqrt(jnp.sum(raw * raw, 0, keepdims=True))
    return jnp.concatenate([points, raw / jnp.maximum(length, 0.001)], 0)


def draw_src_geom(key, part):
    place_key, area_key = jax.random.split(jax.random.fold_in(key, 23))
    points = line_positions(place_key, NCOL, NCOL * BLK * RBD // NROWS)
    areas = jnp.exp(jax.random.uniform(area_key, (1, NCOL), jnp.float32, jnp.log(0.1), jnp.log(0.4)))
    return jnp.concatenate([points, areas], 0)


def draw_tgt_nodes(key, part):
    return line_positions(jax.random.fold_in(key, 37), QN * NROWS // BLK, QN * RBD)


def draw_src_nodes(key, part):
    return line_positions(jax.random.fold_in(key, 41), QN * NROWS // (BLK * RBD), QN)


def plant(values, key, smallest, largest):
    extent = values.shape
    index_at = [jax.random.randint(jax.random.fold_in(key, axis), (), 0, extent[axis]) for axis in range(len(extent))]
    values = values.at[tuple(index_at)].set(smallest)
    longest = extent.index(max(extent))
    index_at[longest] = (index_at[longest] + 1) % extent[longest]
    return values.at[tuple(index_at)].set(largest)


def levels(rng, shape, shards, low, largest):
    loudness, own = 1.0, jax.random.fold_in(rng, 6)
    for position, shards_of in shards:
        steps = jnp.exp(jax.random.uniform(jax.random.fold_in(own, position), (shards_of,), jnp.float32, low / len(shards), largest / len(shards)))
        loudness = loudness * jnp.repeat(steps, shape[position] // shards_of).reshape([-1 if axis == position else 1 for axis in range(len(shape))])
    return loudness


def noise(rng, extent, deviation, most, pieces=(), kind=jnp.bfloat16):
    array = deviation * jax.random.normal(rng, extent, jnp.float32)
    if pieces:
        array = array * levels(rng, extent, pieces, -0.22, 0.18)
    return jnp.clip(array, -most, most).astype(kind)


def setup_inputs(seed: int = 0, part: int = 0) -> dict:
    seeds = jax.random.split(jax.random.key(seed), 10)
    part_splits = jax.random.split(jax.random.fold_in(seeds[9], part), 10)
    return {
        "wavenumber": jnp.clip(jax.random.uniform(part_splits[0], (1,), jnp.float32, 30.0, 90.0), 30.0, 90.0),
        "tgt_geom": draw_tgt_geom(jax.random.fold_in(jax.random.fold_in(seeds[9], part), 71), part),
        "src_geom": draw_src_geom(jax.random.fold_in(jax.random.fold_in(seeds[9], part), 71), part),
        "excite": noise(part_splits[3], (2 * NEXC, NCOL), 1.0, 6.0, ((1, 16),)),
        "tgt_nodes": draw_tgt_nodes(jax.random.fold_in(jax.random.fold_in(seeds[9], part), 71), part),
        "src_nodes": draw_src_nodes(jax.random.fold_in(jax.random.fold_in(seeds[9], part), 71), part),
        "tgt_weights": noise(part_splits[6], (2, QN, NROWS), (16 * QN) ** -0.5, 0.109375, ((2, 8),)),
        "src_weights": noise(part_splits[7], (2, QN, NCOL), (2 * CPD) ** -0.5, 1.0, ((2, 16),)),
        "near_order": plant(jax.random.randint(part_splits[8], (N_ROW * RBD, NBAND), 0, ORDERS + 1), jax.random.fold_in(part_splits[8], 1), 0, ORDERS).astype(jnp.int32),
    }


SOFT = 0.05
FOUR_PI = 4.0 * 3.141592653589793
HIGH = lax.Precision.HIGHEST

def far_block(targets, sources, excite_cols, wave_number):
    delta_x = targets[0][:, None] - sources[0][None, :]
    delta_y = targets[1][:, None] - sources[1][None, :]
    delta_z = targets[2][:, None] - sources[2][None, :]
    radius = jnp.sqrt(delta_x * delta_x + delta_y * delta_y + delta_z * delta_z + SOFT * SOFT)
    cosine = (targets[3][:, None] * delta_x + targets[4][:, None] * delta_y + targets[5][:, None] * delta_z) / radius
    scale = sources[3][None, :] / (FOUR_PI * radius)
    phase = wave_number * radius
    green_re = scale * jnp.cos(phase)
    green_im = scale * jnp.sin(phase)
    factor_re = 1.0 - cosine
    factor_im = -cosine / phase
    kern_re = (green_re * factor_re - green_im * factor_im).astype(jnp.bfloat16)
    kern_im = (green_re * factor_im + green_im * factor_re).astype(jnp.bfloat16)
    dims = (((1,), (1,)), ((), ()))
    first = lax.dot_general(kern_re, excite_cols, dims, preferred_element_type=jnp.float32)
    second = lax.dot_general(kern_im, excite_cols, dims, preferred_element_type=jnp.float32)
    half = excite_cols.shape[0] // 2
    return jnp.concatenate([first[:, :half] - second[:, half:], first[:, half:] + second[:, :half]], 1)

def near_term(tnodes, snodes, moments, unodes, order_val, wave_number):
    delta_x = tnodes[0][:, None] - snodes[0][None, :]
    delta_y = tnodes[1][:, None] - snodes[1][None, :]
    delta_z = tnodes[2][:, None] - snodes[2][None, :]
    radius = jnp.sqrt(delta_x * delta_x + delta_y * delta_y + delta_z * delta_z + SOFT * SOFT)
    scale = 1.0 / (FOUR_PI * radius)
    node_live = (jnp.arange(QN, dtype=jnp.int32) < order_val * QSTEP).astype(jnp.float32)
    node_mask = node_live[:, None] * node_live[None, :]
    green_re = scale * jnp.cos(wave_number * radius) * node_mask
    green_im = scale * jnp.sin(wave_number * radius) * node_mask
    half = moments.shape[1] // 2
    mom_re = moments[:, :half]
    mom_im = moments[:, half:]
    inner_re = jnp.dot(green_re, mom_re, precision=HIGH) - jnp.dot(green_im, mom_im, precision=HIGH)
    inner_im = jnp.dot(green_re, mom_im, precision=HIGH) + jnp.dot(green_im, mom_re, precision=HIGH)
    test_re = unodes[0].astype(jnp.float32)
    test_im = unodes[1].astype(jnp.float32)
    dims = (((0,), (0,)), ((), ()))
    out_re = lax.dot_general(test_re, inner_re, dims, precision=HIGH) - lax.dot_general(test_im, inner_im, dims, precision=HIGH)
    out_im = lax.dot_general(test_re, inner_im, dims, precision=HIGH) + lax.dot_general(test_im, inner_re, dims, precision=HIGH)
    return jnp.concatenate([out_re, out_im], 1)

def reference(wavenumber, tgt_geom, src_geom, excite, tgt_nodes, src_nodes, tgt_weights, src_weights, near_order):
    wave_number = wavenumber[0]
    row_blocks = NROWS // BLK
    col_blocks = row_blocks // RBD
    cols_block = NCOL // col_blocks
    half = excite.shape[0] // 2

    def moment(index):
        start = (index * cols_block).astype(jnp.int32)
        weights = lax.dynamic_slice_in_dim(src_weights, start, cols_block, 2)
        cols = lax.dynamic_slice_in_dim(excite, start, cols_block, 1)
        dims = (((1,), (1,)), ((), ()))
        first = lax.dot_general(weights[0], cols, dims, preferred_element_type=jnp.float32)
        second = lax.dot_general(weights[1], cols, dims, preferred_element_type=jnp.float32)
        return jnp.concatenate([first[:, :half] - second[:, half:], first[:, half:] + second[:, :half]], 1)
    moments = lax.map(moment, jnp.arange(col_blocks, dtype=jnp.int32))

    def row_block(index):
        targets = lax.dynamic_slice_in_dim(tgt_geom, (index * BLK).astype(jnp.int32), BLK, 1)
        total = far_block(targets, src_geom, excite, wave_number)
        tnodes = lax.dynamic_slice_in_dim(tgt_nodes, (index * QN).astype(jnp.int32), QN, 1)
        unodes = lax.dynamic_slice_in_dim(tgt_weights, (index * BLK).astype(jnp.int32), BLK, 2)
        home = index // RBD
        for offset in range(NBAND):
            other = home + offset - NEARW
            valid = jnp.logical_and(other >= 0, other < col_blocks).astype(jnp.float32)
            clipped = jnp.clip(other, 0, col_blocks - 1).astype(jnp.int32)
            snodes = lax.dynamic_slice_in_dim(src_nodes, clipped * QN, QN, 1) * valid
            there = moments[clipped] * valid
            total = total + near_term(tnodes, snodes, there, unodes, near_order[index, offset], wave_number)
        return total
    result = lax.map(row_block, jnp.arange(row_blocks, dtype=jnp.int32))
    return result.reshape(NROWS, 2 * NEXC)
```

```python
import functools
import math

import jax
import jax.numpy as jnp
import numpy as np
from jax import lax
from jax.experimental import pallas as pl
from jax.experimental.pallas import tpu as pltpu
from jax.sharding import PartitionSpec as P

ORDERS = 3
SOFT = 0.05
FOUR_PI = 4.0 * math.pi
LANES = 128
MESH = pl.DeviceIdType.MESH
TN = (((0,), (0,)), ((), ()))
NT = (((1,), (1,)), ((), ()))


def fitted(function, terms):
    nodes = (np.cos((np.arange(terms) + 0.5) * np.pi / terms) + 1.0) / 8.0
    matrix = np.vander(nodes, terms, increasing=True)
    return [float(c) for c in np.linalg.solve(matrix, function(np.sqrt(nodes)))]


COS = fitted(lambda u: np.cos(2.0 * np.pi * u), 7)
SIN = fitted(lambda u: np.sin(2.0 * np.pi * u) / u, 7)


def horner(coefficients, y):
    total = coefficients[-1]
    for c in coefficients[-2::-1]:
        total = total * y + c
    return total


def cos_sin(turns):
    u = turns - jnp.round(turns)
    y = u * u
    return horner(COS, y), u * horner(SIN, y)


def times_i(value):
    half = value.shape[1] // 2
    swapped = jnp.concatenate([value[:, half:], value[:, :half]], 1)
    lane = lax.broadcasted_iota(jnp.int32, value.shape, 1)
    return jnp.where(lane < half, -swapped, swapped)


def split_two(value):
    high = value.astype(jnp.bfloat16)
    return high, (value - high.astype(jnp.float32)).astype(jnp.bfloat16)


def columns_of(rows):
    few, lanes = rows.shape
    pad = jnp.zeros((8 - few, lanes), jnp.float32)
    return jnp.concatenate([rows, pad], 0).T


def kernel(
    wave_hbm,
    order_hbm,
    tgt_hbm,
    tnode_hbm,
    tweight_hbm,
    geom_hbm,
    excite_hbm,
    snode_hbm,
    sweight_hbm,
    out_ref,
    node_all,
    weight_all,
    geom_all,
    excite_all,
    green_high,
    green_low,
    wave_ref,
    order_ref,
    tgt_ref,
    tnode_ref,
    tweight_ref,
    node_own,
    local,
    node_send,
    weight_send,
    geom_send,
    excite_send,
    recv,
    weight_recv,
    weight_pair,
    weight_back,
    pair_send,
    pair_recv,
):
    n_row = lax.axis_size("row")
    row = lax.axis_index("row")
    col = lax.axis_index("col")
    other = 1 - col
    band = node_all.shape[0]
    reach = (band - 1) // 2
    qn = node_all.shape[2]
    qpad = pl.cdiv(qn, LANES) * LANES
    step_nodes = qn // ORDERS
    per = excite_hbm.shape[0]
    blk = out_ref.shape[0]

    barrier = pltpu.get_barrier_semaphore()

    @pl.loop(1, n_row)
    def _(d):
        pl.semaphore_signal(
            barrier, inc=1, device_id={"row": lax.rem(row + d, n_row)}, device_id_type=MESH
        )

    pl.semaphore_signal(barrier, inc=1, device_id={"col": other}, device_id_type=MESH)

    loads = [
        pltpu.make_async_copy(here, there, local.at[index])
        for index, (here, there) in enumerate(
            (
                (wave_hbm, wave_ref),
                (tnode_hbm, tnode_ref),
                (order_hbm, order_ref),
                (tgt_hbm, tgt_ref),
                (tweight_hbm, tweight_ref),
            )
        )
    ]
    own_nodes = pltpu.make_async_copy(snode_hbm, node_own, local.at[len(loads)])
    own_nodes.start()
    for load in loads:
        load.start()

    def fill(slot):
        pltpu.make_async_copy(snode_hbm, node_all.at[slot], recv.at[0]).start()
        pltpu.make_async_copy(sweight_hbm, weight_all.at[col, slot], weight_recv.at[slot]).start()

    @pl.loop(0, band)
    def _(slot):
        block = row + slot - reach
        missing = jnp.logical_or(block < 0, block >= n_row)

        @pl.when(jnp.logical_or(missing, slot == reach))
        def _():
            fill(slot)

    pltpu.make_async_copy(geom_hbm, geom_all.at[col, row], recv.at[2]).start()
    pltpu.make_async_copy(excite_hbm, excite_all.at[col, row], recv.at[3]).start()

    def near_copies(slot):
        to = {"row": row + reach - slot}
        nodes = pltpu.make_async_remote_copy(
            src_ref=snode_hbm,
            dst_ref=node_all.at[slot],
            send_sem=node_send.at[slot],
            recv_sem=recv.at[0],
            device_id=to,
            device_id_type=MESH,
        )
        weights = pltpu.make_async_remote_copy(
            src_ref=sweight_hbm,
            dst_ref=weight_all.at[col, slot],
            send_sem=weight_send.at[slot],
            recv_sem=weight_recv.at[slot],
            device_id=to,
            device_id_type=MESH,
        )
        return nodes, weights

    def far_copies(d):
        to = {"row": lax.rem(row + d, n_row)}
        geoms = pltpu.make_async_remote_copy(
            src_ref=geom_hbm,
            dst_ref=geom_all.at[col, row],
            send_sem=geom_send.at[d],
            recv_sem=recv.at[2],
            device_id=to,
            device_id_type=MESH,
        )
        excites = pltpu.make_async_remote_copy(
            src_ref=excite_hbm,
            dst_ref=excite_all.at[col, row],
            send_sem=excite_send.at[d],
            recv_sem=recv.at[3],
            device_id=to,
            device_id_type=MESH,
        )
        return geoms, excites

    def for_near(act):
        @pl.loop(0, band)
        def _(slot):
            goal = row + reach - slot
            inside = jnp.logical_and(goal >= 0, goal < n_row)

            @pl.when(jnp.logical_and(inside, slot != reach))
            def _():
                act(slot)

    def weight_to_pair(slot, half):
        return pltpu.make_async_remote_copy(
            src_ref=weight_all.at[half, slot],
            dst_ref=weight_all.at[half, slot],
            send_sem=weight_pair.at[slot],
            recv_sem=weight_back.at[slot],
            device_id={"col": other},
            device_id_type=MESH,
        )

    def to_pair(index, buffer):
        return pltpu.make_async_remote_copy(
            src_ref=buffer.at[col],
            dst_ref=buffer.at[col],
            send_sem=pair_send.at[index],
            recv_sem=pair_recv.at[index],
            device_id={"col": other},
            device_id_type=MESH,
        )

    def from_pair(index, buffer):
        return pltpu.make_async_remote_copy(
            src_ref=buffer.at[other],
            dst_ref=buffer.at[other],
            send_sem=pair_send.at[index],
            recv_sem=pair_recv.at[index],
            device_id={"col": other},
            device_id_type=MESH,
        )

    for load in loads[:3]:
        load.wait()
    wave = wave_ref[0]
    per_turn = wave * (0.5 / math.pi)

    tnodes = tnode_ref[...]
    tnodes = jnp.where(col == 0, tnodes[:, :qn], tnodes[:, qn:])
    if qpad > qn:
        tnodes = jnp.concatenate([tnodes, jnp.zeros((3, qpad - qn), jnp.float32)], 1)
    tcols = columns_of(tnodes)[:qn]
    t_x, t_y, t_z = (jnp.broadcast_to(tcols[:, i : i + 1], (qn, LANES)) for i in range(3))

    point = lax.broadcasted_iota(jnp.int32, (qn, LANES), 0)

    def order_of(slot):
        block = row + slot - reach
        valid = jnp.logical_and(block >= 0, block < n_row)
        return jnp.where(valid, order_ref[col, slot] * step_nodes, 0)

    def green_of(slot, snodes):
        live = point < order_of(slot)
        if qpad > qn:
            snodes = jnp.concatenate([snodes, jnp.zeros((3, qpad - qn), jnp.float32)], 1)
        for part in range(qpad // LANES):
            here = slice(part * LANES, (part + 1) * LANES)
            d_x = t_x - snodes[0:1, here]
            d_y = t_y - snodes[1:2, here]
            d_z = t_z - snodes[2:3, here]
            squared = d_x * d_x + d_y * d_y + d_z * d_z + SOFT * SOFT
            inverse = lax.rsqrt(squared)
            cosine, sine = cos_sin(per_turn * (squared * inverse))
            inverse = jnp.where(live, inverse, 0.0)
            for index, value in enumerate((inverse * cosine, inverse * sine)):
                high, low = split_two(value)
                at = pl.multiple_of((2 * slot + index) * qpad + part * LANES, LANES)
                green_high[:, pl.ds(at, LANES)] = high
                green_low[:, pl.ds(at, LANES)] = low

    own_nodes.wait()
    green_of(reach, node_own[...])

    pl.semaphore_wait(barrier, n_row)

    for_near(lambda slot: near_copies(slot)[0].start())

    @pl.loop(1, n_row)
    def _(d):
        far_copies(d)[0].start()

    for_near(lambda slot: near_copies(slot)[1].start())

    @pl.loop(1, n_row)
    def _(d):
        far_copies(d)[1].start()

    pltpu.make_async_copy(node_all, node_all, recv.at[0]).wait()

    def green_some(begin, end):
        @pl.loop(begin, end)
        def _(slot):
            block = row + slot - reach
            needed = jnp.logical_and(block >= 0, block < n_row)

            @pl.when(jnp.logical_and(needed, slot != reach))
            def _():
                green_of(slot, node_all[slot])

            @pl.when(jnp.logical_not(needed))
            def _():
                at = pl.ds(pl.multiple_of(2 * slot * qpad, LANES), 2 * qpad)
                green_high[:, at] = jnp.zeros((qn, 2 * qpad), jnp.bfloat16)
                green_low[:, at] = jnp.zeros((qn, 2 * qpad), jnp.bfloat16)

    green_some(0, (band - 2))
    pltpu.make_async_copy(geom_all.at[col], geom_all.at[col], recv.at[2]).wait()
    to_pair(0, geom_all).start()

    @pl.loop(0, band)
    def _(slot):
        pltpu.make_async_copy(
            weight_all.at[col, slot], weight_all.at[col, slot], weight_recv.at[slot]
        ).wait()
        weight_to_pair(slot, col).start()

    pltpu.make_async_copy(excite_all.at[col], excite_all.at[col], recv.at[3]).wait()
    to_pair(1, excite_all).start()
    green_some((band - 2), band)
    from_pair(0, geom_all).wait_recv()

    loads[3].wait()
    begin = pl.multiple_of(col * blk, blk)
    gcols = columns_of(tgt_ref[:, pl.ds(begin, blk)])
    p_x, p_y, p_z, n_x, n_y, n_z = (gcols[:, i : i + 1] for i in range(6))
    pieces = LANES // per
    chunks = n_row // pieces

    def impedance(half, chunk):
        places = jnp.concatenate([geom_all[half, chunk * pieces + i] for i in range(pieces)], 1)
        d_x = p_x - places[0:1]
        d_y = p_y - places[1:2]
        d_z = p_z - places[2:3]
        squared = d_x * d_x + d_y * d_y + d_z * d_z + SOFT * SOFT
        inverse = lax.rsqrt(squared)
        radius = squared * inverse
        along = (n_x * d_x + n_y * d_y + n_z * d_z) * inverse
        scale = places[3:4] * (inverse * (1.0 / FOUR_PI))
        cosine, sine = cos_sin(per_turn * radius)
        green_re = scale * cosine
        green_im = scale * sine
        factor_re = 1.0 - along
        factor_im = -along / (wave * radius)
        kern_re = green_re * factor_re - green_im * factor_im
        kern_im = green_re * factor_im + green_im * factor_re
        return jnp.concatenate(
            [kern_re.astype(jnp.bfloat16), kern_im.astype(jnp.bfloat16)], 1
        )

    def both(rows):
        turned = times_i(rows.astype(jnp.float32)).astype(jnp.bfloat16)
        return jnp.concatenate([rows, turned], 0)

    from_pair(1, excite_all).wait_recv()

    def far_step(index, total):
        half, chunk = index // chunks, lax.rem(index, chunks)
        rows = excite_all[half, pl.ds(chunk * pieces, pieces)].reshape(LANES, blk)
        return total + jnp.dot(
            impedance(half, chunk), both(rows), preferred_element_type=jnp.float32
        )

    far = lax.fori_loop(0, 2 * chunks, far_step, jnp.zeros(out_ref.shape, jnp.float32))

    width = out_ref.shape[1]

    lane = lax.broadcasted_iota(jnp.int32, (2 * per, qpad), 1)
    applied, sources = [], []
    for slot in range(band):
        weight_to_pair(slot, other).wait_recv()
        live = lane < order_of(slot)
        basis = []
        for part in range(2):
            value = jnp.concatenate([weight_all[half, slot, part] for half in range(2)], 0)
            if qpad > qn:
                value = jnp.concatenate(
                    [value, jnp.zeros((2 * per, qpad - qn), jnp.bfloat16)], 1
                )
            basis.append(jnp.where(live, value.astype(jnp.float32), 0.0))
        stacked = jnp.concatenate(
            [
                jnp.concatenate([basis[0], -basis[1]], 1),
                jnp.concatenate([basis[1], basis[0]], 1),
            ],
            0,
        ).astype(jnp.bfloat16)
        here = slice(2 * slot * qpad, 2 * (slot + 1) * qpad)
        applied.append(
            lax.dot_general(green_high[:, here], stacked, NT, preferred_element_type=jnp.float32)
            + lax.dot_general(green_low[:, here], stacked, NT, preferred_element_type=jnp.float32)
        )
        source = jnp.clip(row + slot - reach, 0, n_row - 1)
        sources.append(both(jnp.concatenate([excite_all[half, source] for half in range(2)], 0)))
    high, low = split_two(jnp.concatenate(applied, 1))
    sources = jnp.concatenate(sources, 0)
    inner = jnp.dot(high, sources, preferred_element_type=jnp.float32) + jnp.dot(
        low, sources, preferred_element_type=jnp.float32
    )
    inner = inner * (1.0 / FOUR_PI)
    loads[4].wait()
    tests = jnp.concatenate(
        [tweight_ref[0, :, pl.ds(begin, blk)], tweight_ref[1, :, pl.ds(begin, blk)]], 0
    )
    high, low = split_two(jnp.concatenate([inner, times_i(inner)], 0))
    product = lax.dot_general(
        tests, jnp.concatenate([high, low], 1), TN, preferred_element_type=jnp.float32
    )
    out_ref[...] = far + (product[:, :width] + product[:, width:])

    for_near(lambda slot: [copy.wait_send() for copy in near_copies(slot)])

    @pl.loop(1, n_row)
    def _(d):
        for copy in far_copies(d):
            copy.wait_send()

    @pl.loop(0, band)
    def _(slot):
        weight_to_pair(slot, col).wait_send()

    for index, buffer in enumerate((geom_all, excite_all)):
        to_pair(index, buffer).wait_send()


def on_device(
    wavenumber,
    tgt_geom,
    src_geom,
    excite,
    tgt_nodes,
    src_nodes,
    tgt_weights,
    src_weights,
    near_order,
):
    n_row = lax.axis_size("row")
    band = near_order.shape[1]
    blk = tgt_geom.shape[1] // lax.axis_size("col")
    qn = src_nodes.shape[1]
    qpad = -(-qn // LANES) * LANES
    excite_rows = excite.T
    weight_rows = src_weights.transpose(0, 2, 1)
    vmem = pl.BlockSpec(memory_space=pltpu.VMEM)
    hbm = pl.BlockSpec(memory_space=pl.ANY)
    dma = pltpu.SemaphoreType.DMA
    return pl.pallas_call(
        kernel,
        out_shape=pltpu.VMEM((blk, excite.shape[0]), jnp.float32),
        in_specs=[hbm] * 9,
        out_specs=vmem,
        scratch_shapes=[
            pltpu.VMEM((band,) + src_nodes.shape, jnp.float32),
            pltpu.VMEM((2, band) + weight_rows.shape, jnp.bfloat16),
            pltpu.VMEM((2, n_row) + src_geom.shape, jnp.float32),
            pltpu.VMEM((2, n_row) + excite_rows.shape, jnp.bfloat16),
            pltpu.VMEM((qn, band * 2 * qpad), jnp.bfloat16),
            pltpu.VMEM((qn, band * 2 * qpad), jnp.bfloat16),
            pltpu.SMEM(wavenumber.shape, jnp.float32),
            pltpu.SMEM(near_order.shape, jnp.int32),
            pltpu.VMEM(tgt_geom.shape, jnp.float32),
            pltpu.VMEM(tgt_nodes.shape, jnp.float32),
            pltpu.VMEM(tgt_weights.shape, jnp.bfloat16),
            pltpu.VMEM(src_nodes.shape, jnp.float32),
            dma((6,)),
            dma((band,)),
            dma((band,)),
            dma((n_row,)),
            dma((n_row,)),
            dma((4,)),
            dma((band,)),
            dma((band,)),
            dma((band,)),
            dma((2,)),
            dma((2,)),
        ],
        compiler_params=pltpu.CompilerParams(collective_id=0, has_side_effects=True),
        name="slab",
    )(
        wavenumber,
        near_order,
        tgt_geom,
        tgt_nodes,
        tgt_weights,
        src_geom,
        excite_rows,
        src_nodes,
        weight_rows,
    )


def solution(mesh):
    return jax.shard_map(
        on_device,
        mesh=mesh,
        in_specs=(
            P("groups"),
            P(None, ("groups", "row")),
            P(None, ("groups", "row", "col")),
            P(None, ("groups", "row", "col")),
            P(None, ("groups", "row")),
            P(None, ("groups", "row")),
            P(None, None, ("groups", "row")),
            P(None, None, ("groups", "row", "col")),
            P(("groups", "row"), None),
        ),
        out_specs=P(("groups", "row", "col"), None),
        check_vma=False,
    )
```

```python
import math

import jax
import jax.numpy as jnp
import numpy as np
from jax import lax
from jax.experimental import pallas as pl
from jax.experimental.pallas import tpu as pltpu
from jax.sharding import PartitionSpec as P

ORDERS = 3
SOFT = 0.05
PI = math.pi
LANES = 128
ROWS = 8
PAIR = 2
MESH = pl.DeviceIdType.MESH
TN = (((0,), (0,)), ((), ()))


def fitted(function, terms):
    nodes = (np.cos((np.arange(terms) + 0.5) * np.pi / terms) + 1.0) / 8.0
    matrix = np.vander(nodes, terms, increasing=True)
    return [float(c) for c in np.linalg.solve(matrix, function(np.sqrt(nodes)))]


COS = fitted(lambda u: np.cos(2.0 * np.pi * u), 6)
SIN = fitted(lambda u: np.sin(2.0 * np.pi * u) / u, 6)


def horner(coefficients, y):
    total = coefficients[-1]
    for c in coefficients[-2::-1]:
        total = total * y + c
    return total


def wave_parts(squared):
    inverse = lax.rsqrt(squared)
    turns = squared * inverse
    u = turns - jnp.round(turns)
    y = u * u
    return inverse, horner(COS, y), u, horner(SIN, y)


def times_i(value):
    half = value.shape[1] // 2
    swapped = pltpu.roll(value, half, 1)
    lane = lax.broadcasted_iota(jnp.int32, value.shape, 1)
    return jnp.where(lane < half, -swapped, swapped)


def split_two(value):
    high = value.astype(jnp.bfloat16)
    return high, (value - high.astype(jnp.float32)).astype(jnp.bfloat16)


def columns_of(rows):
    few, lanes = rows.shape
    pad = jnp.zeros((ROWS - few, lanes), jnp.float32)
    return jnp.concatenate([rows, pad], 0).T


def kernel(
    wave_hbm,
    order_hbm,
    tgt_hbm,
    tnode_hbm,
    tweight_hbm,
    geom_hbm,
    excite_hbm,
    snode_hbm,
    sweight_hbm,
    out_ref,
    small_all,
    bulk_all,
    small_pack,
    bulk_pack,
    tnode_wide,
    tgt_wide,
    tests,
    green_high,
    green_low,
    moment,
    impedance,
    part_send,
    part_recv,
    wave_ref,
    order_ref,
    tgt_ref,
    tnode_ref,
    tweight_ref,
    geom_ref,
    excite_ref,
    snode_ref,
    sweight_ref,
    local,
    own,
    small_send,
    bulk_send,
    small_recv,
    bulk_recv,
    part_sem,
):
    n_row = lax.axis_size("row")
    row = lax.axis_index("row")
    col = lax.axis_index("col")
    home = lax.rem(row, 2)
    place = row // 2
    chips = n_row // 2
    reach = (order_hbm.shape[1] - 1) // 2
    qn = snode_hbm.shape[1]
    tail = qn - LANES
    step_nodes = qn // ORDERS
    per = excite_hbm.shape[0]
    blk, width = out_ref.shape
    near_pairs = moment.shape[0]
    first_pair = jnp.clip(
        (row - reach - col + 1) // 2 // PAIR, 0, chips // PAIR - near_pairs
    )
    mine = home == col

    barrier = pltpu.get_barrier_semaphore()
    upper = row >= chips

    def outward(index, count):
        return jnp.where(upper, index, count - 1 - index)

    @pl.loop(0, n_row)
    def _(index):
        index = outward(index, n_row)
        chip, core = 2 * (index // 2) + col, lax.rem(index, 2)

        @pl.when(jnp.logical_not(jnp.logical_and(chip == row, core == col)))
        def _():
            pl.semaphore_signal(
                barrier, inc=1, device_id={"row": chip, "col": core}, device_id_type=MESH
            )

    @pl.when(jnp.logical_not(mine))
    def _():
        pl.semaphore_signal(barrier, inc=1, device_id={"col": 1 - col}, device_id_type=MESH)

    loads = [
        pltpu.make_async_copy(here, there, local.at[index])
        for index, (here, there) in enumerate(
            (
                (snode_hbm, snode_ref),
                (geom_hbm, geom_ref),
                (excite_hbm, excite_ref),
                (sweight_hbm, sweight_ref),
                (wave_hbm, wave_ref),
                (tnode_hbm, tnode_ref),
                (tgt_hbm, tgt_ref),
                (order_hbm, order_ref),
                (tweight_hbm, tweight_ref),
            )
        )
    ]
    for load in loads:
        load.start()

    lane = lax.broadcasted_iota(jnp.int32, (1, LANES), 1)

    loads[0].wait()
    nodes = snode_ref[...]
    gap = jnp.zeros((nodes.shape[0], LANES - tail), jnp.float32)
    ends = nodes[:, LANES:]
    even, odd = jnp.concatenate([ends, gap], 1), jnp.concatenate([gap, ends], 1)
    ends = jnp.where(lax.rem(place, PAIR) == 0, even, odd)
    small_pack[0:3, :] = jnp.where(col == 0, nodes[:, :LANES], ends)
    loads[1].wait()
    pieces = LANES // (2 * per)
    spread = jnp.concatenate([geom_ref[...]] * (LANES // per), 1)
    begin = (2 * lax.rem(place, pieces) + col) * per
    inside = jnp.logical_and(lane >= begin, lane < begin + per)
    small_pack[3:4, :] = jnp.zeros((1, LANES), jnp.float32)
    small_pack[4:8, :] = jnp.where(inside, spread, 0.0)
    loads[2].wait()
    bulk_pack[0] = excite_ref[...]
    loads[3].wait()
    bulk_pack[1] = sweight_ref[0, :, :LANES]
    bulk_pack[2] = sweight_ref[1, :, :LANES]
    bulk_pack[3] = jnp.concatenate(
        [sweight_ref[part, :, LANES:].astype(jnp.float32) for part in range(2)], 1
    ).astype(jnp.bfloat16)

    @pl.when(mine)
    def _():
        pltpu.make_async_copy(small_pack, small_all.at[place, col], small_recv.at[place]).start()
        pltpu.make_async_copy(bulk_pack, bulk_all.at[place, col], bulk_recv.at[place]).start()

    def small_to(chip):
        return pltpu.make_async_remote_copy(
            src_ref=small_pack,
            dst_ref=small_all.at[place, col],
            send_sem=small_send.at[chip],
            recv_sem=small_recv.at[place],
            device_id={"row": chip, "col": home},
            device_id_type=MESH,
        )

    def bulk_to(chip):
        return pltpu.make_async_remote_copy(
            src_ref=bulk_pack,
            dst_ref=bulk_all.at[place, col],
            send_sem=bulk_send.at[chip],
            recv_sem=bulk_recv.at[place],
            device_id={"row": chip, "col": home},
            device_id_type=MESH,
        )

    def excite_to(chip):
        return pltpu.make_async_remote_copy(
            src_ref=bulk_pack.at[0],
            dst_ref=bulk_all.at[place, col, 0],
            send_sem=bulk_send.at[chip],
            recv_sem=bulk_recv.at[place],
            device_id={"row": chip, "col": home},
            device_id_type=MESH,
        )

    def is_near(chip):
        return jnp.logical_and(chip >= row - reach, chip <= row + reach)

    def for_others(act):
        @pl.loop(0, n_row)
        def _(index):
            chip = outward(index, n_row)

            @pl.when(jnp.logical_not(jnp.logical_and(mine, chip == row)))
            def _():
                act(chip)

    def bulk_act(chip, name):
        near = is_near(chip)

        @pl.when(near)
        def _():
            getattr(bulk_to(chip), name)()

        @pl.when(jnp.logical_not(near))
        def _():
            getattr(excite_to(chip), name)()

    def order_of(block, chip):
        offset = chip - row + reach
        valid = jnp.logical_and(offset >= 0, offset <= 2 * reach)
        value = order_ref[block, jnp.clip(offset, 0, 2 * reach)] * step_nodes
        return jnp.where(valid, value, 0)

    def turns_per_unit():
        return wave_ref[0] * (0.5 / PI)

    def prepare():
        rate = turns_per_unit()
        cols = columns_of(tnode_ref[...])
        origin = cols[0:1]
        cols = (cols - origin) * rate
        for block in range(2):
            for axis in range(3):
                tnode_wide[block, axis] = jnp.broadcast_to(
                    cols[block * qn : (block + 1) * qn, axis : axis + 1], (qn, LANES)
                )
        loads[6].wait()
        cols = columns_of(tgt_ref[...])
        for axis in range(6):
            line = cols[:, axis : axis + 1]
            if axis < 3:
                line = (line - origin[:, axis : axis + 1]) * rate
            tgt_wide[axis] = jnp.broadcast_to(line, (2 * blk, LANES))

        loads[8].wait()
        for block in range(2):
            at = slice(block * blk, (block + 1) * blk)
            tests[block] = jnp.concatenate([tweight_ref[0, :, at], tweight_ref[1, :, at]], 0).T

    def scaled(places):
        rate = turns_per_unit()
        first = tnode_ref[:, 0:1]
        return (places - first) * rate

    def green_of(chunk, places, limits):
        rate = turns_per_unit()
        soft = rate * rate * (SOFT * SOFT)
        places = scaled(places)
        s_x, s_y, s_z = (places[i : i + 1] for i in range(3))

        @pl.loop(0, 2)
        def _(block):
            limit, ahead = limits(block)
            for group in range(ORDERS):
                here = slice(group * step_nodes, (group + 1) * step_nodes)
                live = jnp.logical_and(ahead < limit, limit > group * step_nodes)
                scale = jnp.where(live, rate * (0.25 / PI), 0.0)
                d_x = tnode_wide[block, 0, here] - s_x
                d_y = tnode_wide[block, 1, here] - s_y
                d_z = tnode_wide[block, 2, here] - s_z
                squared = d_x * d_x + d_y * d_y + (d_z * d_z + soft)
                inverse, cosine, u, sine = wave_parts(squared)
                inverse = inverse * scale
                for part, value in enumerate((inverse * cosine, (inverse * u) * sine)):
                    high, low = split_two(value)
                    at = pl.multiple_of((2 * chunk + part) * LANES, LANES)
                    green_high[block, here, pl.ds(at, LANES)] = high
                    green_low[block, here, pl.ds(at, LANES)] = low

    def green_head(pair, slot, places):
        chip = 2 * ((first_pair + pair) * PAIR + slot) + col
        green_of(3 * pair + slot, places, lambda block: (order_of(block, chip), lane))

    def green_tail(pair, places):
        chip = 2 * (first_pair + pair) * PAIR + col

        def limits(block):
            limit = jnp.where(lane < tail, order_of(block, chip), order_of(block, chip + 2))
            return limit, LANES + jnp.where(lane < tail, lane, lane - tail)

        green_of(3 * pair + PAIR, places, limits)

    own_pair = place // PAIR - first_pair
    own_slot = lax.rem(place, PAIR)

    def green_own():
        @pl.when(mine)
        def _():
            green_head(own_pair, own_slot, snode_ref[:, :LANES])

    loads[4].wait()
    loads[5].wait()
    loads[7].wait()

    @pl.when(jnp.logical_not(upper))
    def _():
        prepare()
        green_own()

    pl.semaphore_wait(barrier, n_row)
    for_others(lambda chip: small_to(chip).start())
    for_others(lambda chip: bulk_act(chip, "start"))

    @pl.when(upper)
    def _():
        prepare()
        green_own()

    def wait_small(index):
        pltpu.make_async_copy(small_all.at[index], small_all.at[index], small_recv.at[index]).wait()

    def wait_bulk(index):
        near = is_near(2 * index + col)

        @pl.when(near)
        def _():
            pltpu.make_async_copy(bulk_all.at[index], bulk_all.at[index], bulk_recv.at[index]).wait()

        @pl.when(jnp.logical_not(near))
        def _():
            view = bulk_all.at[index, :, 0]
            pltpu.make_async_copy(view, view, bulk_recv.at[index]).wait()

    @pl.loop(0, near_pairs)
    def _(turn):
        pair = near_pairs - 1 - turn
        base = (first_pair + pair) * PAIR

        @pl.loop(0, PAIR)
        def _(slot):
            slot = PAIR - 1 - slot
            index = base + slot
            chip = 2 * index + col
            wait_small(index)

            @pl.when(jnp.logical_and(is_near(chip), chip != row))
            def _():
                green_head(pair, slot, small_all[index, 0, 0:3])

            @pl.when(jnp.logical_not(is_near(chip)))
            def _():
                at = pl.ds(pl.multiple_of((3 * pair + slot) * 2 * LANES, LANES), 2 * LANES)
                for block in range(2):
                    green_high[block, :, at] = jnp.zeros((qn, 2 * LANES), jnp.bfloat16)
                    green_low[block, :, at] = jnp.zeros((qn, 2 * LANES), jnp.bfloat16)

        green_tail(pair, small_all[base, 1, 0:3] + small_all[base + 1, 1, 0:3])

    for_rest_begin, for_rest_end = PAIR * first_pair, PAIR * (first_pair + near_pairs)

    def for_rest(act):
        if PAIR * near_pairs < chips:

            @pl.loop(0, chips)
            def _(index):
                @pl.when(jnp.logical_or(index < for_rest_begin, index >= for_rest_end))
                def _():
                    act(index)

    for_rest(wait_small)

    rate = turns_per_unit()
    soft = rate * rate * (SOFT * SOFT)

    @pl.loop(0, chips // pieces)
    def _(chunk):
        packed = small_all[pl.ds(chunk * pieces, pieces), :, 4:8, :].reshape(2 * pieces, 4, LANES)
        packed = jnp.sum(packed, 0)
        places = scaled(packed[0:3])
        area = packed[3:4] * (rate * (0.25 / PI))
        at = pl.multiple_of(chunk * 2 * LANES, LANES)
        for part in range(2 * blk // 64):
            here = slice(part * 64, (part + 1) * 64)
            d_x = tgt_wide[0, here] - places[0:1]
            d_y = tgt_wide[1, here] - places[1:2]
            d_z = tgt_wide[2, here] - places[2:3]
            squared = d_x * d_x + d_y * d_y + (d_z * d_z + soft)
            inverse, cosine, u, sine = wave_parts(squared)
            sine = u * sine
            along = (tgt_wide[3, here] * d_x + tgt_wide[4, here] * d_y + tgt_wide[5, here] * d_z) * inverse
            scale = area * inverse
            green_re = scale * cosine
            green_im = scale * sine
            factor_re = 1.0 - along
            factor_im = along * (inverse * (-0.5 / PI))
            impedance[here, pl.ds(at, LANES)] = (green_re * factor_re - green_im * factor_im).astype(jnp.bfloat16)
            impedance[here, pl.ds(at + LANES, LANES)] = (green_re * factor_im + green_im * factor_re).astype(jnp.bfloat16)

    def turned(rows):
        return times_i(rows.astype(jnp.float32)).astype(jnp.bfloat16)

    def put_moment(pair, begin, value):
        both = jnp.concatenate([value, times_i(value)], 0)
        high, low = split_two(both)
        count = value.shape[0]
        for part in range(2):
            at = pl.ds(pl.multiple_of(begin + part * LANES, tail), count)
            here = slice(part * count, (part + 1) * count)
            moment[pair, at, 0:width] = high[here]
            moment[pair, at, width:] = low[here]

    @pl.loop(0, near_pairs)
    def _(turn):
        pair = near_pairs - 1 - turn

        @pl.loop(0, PAIR)
        def _(slot):
            slot = PAIR - 1 - slot
            index = (first_pair + pair) * PAIR + slot
            wait_bulk(index)
            near = is_near(2 * index + col)
            head_at = slot * 2 * LANES
            tail_at = PAIR * 2 * LANES + slot * tail

            @pl.when(near)
            def _():
                rows = bulk_all[index, :, 0].reshape(2 * per, width)
                spun = turned(rows)
                heads = jnp.concatenate([bulk_all[index, half, part] for part in (1, 2) for half in range(2)], 0)
                value = lax.dot_general(
                    heads, jnp.concatenate([rows, spun], 0), TN, preferred_element_type=jnp.float32
                )
                put_moment(pair, head_at, value)
                ends = jnp.concatenate([bulk_all[index, half, 3] for half in range(2)], 0)
                value = lax.dot_general(
                    ends, jnp.concatenate([rows, spun], 1), TN, preferred_element_type=jnp.float32
                )
                put_moment(pair, tail_at, value[:tail, :width] + value[tail:, width:])

            @pl.when(jnp.logical_not(near))
            def _():
                put_moment(pair, head_at, jnp.zeros((LANES, width), jnp.float32))
                put_moment(pair, tail_at, jnp.zeros((tail, width), jnp.float32))

    for_rest(wait_bulk)

    def partial(block):
        def far_step(chunk, total):
            rows = bulk_all[pl.ds(chunk * pieces, pieces), :, 0].reshape(LANES, width)
            at = pl.multiple_of(chunk * 2 * LANES, LANES)
            begin = pl.multiple_of(block * blk, blk)
            return total + jnp.dot(
                impedance[pl.ds(begin, blk), pl.ds(at, 2 * LANES)],
                jnp.concatenate([rows, turned(rows)], 0),
                preferred_element_type=jnp.float32,
            )

        far = lax.fori_loop(0, chips // pieces, far_step, jnp.zeros((blk, width), jnp.float32))
        right = jnp.concatenate([moment[pair] for pair in range(near_pairs)], 0)
        inner = jnp.dot(green_high[block], right, preferred_element_type=jnp.float32)
        inner = inner[:, :width] + inner[:, width:]
        inner = inner + jnp.dot(green_low[block], right[:, :width], preferred_element_type=jnp.float32)
        high, low = split_two(jnp.concatenate([inner, times_i(inner)], 0))
        product = jnp.dot(
            tests[block], jnp.concatenate([high, low], 1), preferred_element_type=jnp.float32
        )
        return far + (product[:, :width] + product[:, width:])

    swap = pltpu.make_async_remote_copy(
        src_ref=part_send,
        dst_ref=part_recv,
        send_sem=part_sem.at[0],
        recv_sem=part_sem.at[1],
        device_id={"col": 1 - col},
        device_id_type=MESH,
    )
    part_send[...] = partial(1 - col)
    swap.start()
    result = partial(col)
    swap.wait_recv()
    out_ref[...] = result + part_recv[...]

    for_others(lambda chip: small_to(chip).wait_send())
    for_others(lambda chip: bulk_act(chip, "wait_send"))
    swap.wait_send()


def on_device(
    wavenumber,
    tgt_geom,
    src_geom,
    excite,
    tgt_nodes,
    src_nodes,
    tgt_weights,
    src_weights,
    near_order,
):
    n_row = lax.axis_size("row")
    chips = n_row // 2
    blk = tgt_geom.shape[1] // 2
    qn = src_nodes.shape[1]
    per, width = src_geom.shape[1], excite.shape[0]
    excite_rows = excite.T
    weight_rows = src_weights.transpose(0, 2, 1)
    near_pairs = min(3, chips // PAIR)
    depth = near_pairs * 3 * 2 * LANES
    hbm = pl.BlockSpec(memory_space=pl.ANY)
    dma = pltpu.SemaphoreType.DMA
    f32, bf16 = jnp.float32, jnp.bfloat16
    return pl.pallas_call(
        kernel,
        out_shape=pltpu.VMEM((blk, width), f32),
        in_specs=[hbm] * 9,
        out_specs=pl.BlockSpec(memory_space=pltpu.VMEM),
        scratch_shapes=[
            pltpu.VMEM((chips, 2, ROWS, LANES), f32),
            pltpu.VMEM((chips, 2, 4, per, LANES), bf16),
            pltpu.VMEM((ROWS, LANES), f32),
            pltpu.VMEM((4, per, LANES), bf16),
            pltpu.VMEM((2, 3, qn, LANES), f32),
            pltpu.VMEM((6, 2 * blk, LANES), f32),
            pltpu.VMEM((2, blk, 2 * qn), bf16),
            pltpu.VMEM((2, qn, depth), bf16),
            pltpu.VMEM((2, qn, depth), bf16),
            pltpu.VMEM((near_pairs, 3 * 2 * LANES, 2 * width), bf16),
            pltpu.VMEM((2 * blk, chips * 4 * per), bf16),
            pltpu.VMEM((blk, width), f32),
            pltpu.VMEM((blk, width), f32),
            pltpu.SMEM(wavenumber.shape, f32),
            pltpu.SMEM(near_order.shape, jnp.int32),
            pltpu.VMEM(tgt_geom.shape, f32),
            pltpu.VMEM(tgt_nodes.shape, f32),
            pltpu.VMEM(tgt_weights.shape, bf16),
            pltpu.VMEM(src_geom.shape, f32),
            pltpu.VMEM(excite_rows.shape, bf16),
            pltpu.VMEM(src_nodes.shape, f32),
            pltpu.VMEM(weight_rows.shape, bf16),
            dma((9,)),
            dma((2,)),
            dma((n_row,)),
            dma((n_row,)),
            dma((chips,)),
            dma((chips,)),
            dma((2,)),
        ],
        compiler_params=pltpu.CompilerParams(collective_id=0, has_side_effects=True),
        name="slab",
    )(
        wavenumber,
        near_order,
        tgt_geom,
        tgt_nodes,
        tgt_weights,
        src_geom,
        excite_rows,
        src_nodes,
        weight_rows,
    )


def solution(mesh):
    return jax.shard_map(
        on_device,
        mesh=mesh,
        in_specs=(
            P("groups"),
            P(None, ("groups", "row")),
            P(None, ("groups", "row", "col")),
            P(None, ("groups", "row", "col")),
            P(None, ("groups", "row")),
            P(None, ("groups", "row")),
            P(None, None, ("groups", "row")),
            P(None, None, ("groups", "row", "col")),
            P(("groups", "row"), None),
        ),
        out_specs=P(("groups", "row", "col"), None),
        check_vma=False,
    )
```

```python
import math

import jax
import jax.numpy as jnp
import numpy as np
from jax import lax
from jax.experimental import pallas as pl
from jax.experimental.pallas import tpu as pltpu
from jax.sharding import PartitionSpec as P

ORDERS = 3
SOFT = 0.05
PI = math.pi
LANES = 128
ROWS = 8
MESH = pl.DeviceIdType.MESH
TN = (((0,), (0,)), ((), ()))


def fitted(function, terms):
    nodes = (np.cos((np.arange(terms) + 0.5) * np.pi / terms) + 1.0) / 8.0
    matrix = np.vander(nodes, terms, increasing=True)
    return [float(c) for c in np.linalg.solve(matrix, function(np.sqrt(nodes)))]


COS = fitted(lambda u: np.cos(2.0 * np.pi * u), 6)
SIN = fitted(lambda u: np.sin(2.0 * np.pi * u) / u, 6)


def horner(coefficients, y):
    total = coefficients[-1]
    for c in coefficients[-2::-1]:
        total = total * y + c
    return total


def wave_parts(squared):
    inverse = lax.rsqrt(squared)
    turns = squared * inverse
    u = turns - jnp.round(turns)
    y = u * u
    return inverse, horner(COS, y), u, horner(SIN, y)


def plus_i(first, second):
    half = second.shape[1] // 2
    swapped = pltpu.roll(second, half, 1)
    lane = lax.broadcasted_iota(jnp.int32, second.shape, 1)
    return first + jnp.where(lane < half, -swapped, swapped)


def split_two(value):
    high = value.astype(jnp.bfloat16)
    return high, (value - high.astype(jnp.float32)).astype(jnp.bfloat16)


def columns_of(rows):
    few, lanes = rows.shape
    pad = jnp.zeros((ROWS - few, lanes), jnp.float32)
    return jnp.concatenate([rows, pad], 0).T


def kernel(
    wave_hbm,
    order_hbm,
    tgt_hbm,
    tnode_hbm,
    tweight_hbm,
    geom_hbm,
    excite_hbm,
    snode_hbm,
    sweight_hbm,
    out_ref,
    node_all,
    bulk_all,
    bulk_pack,
    tnode_wide,
    tgt_wide,
    tests,
    green_high,
    green_low,
    moment,
    impedance,
    far_send,
    far_recv,
    far_own,
    wave_ref,
    order_ref,
    tgt_ref,
    tnode_ref,
    tweight_ref,
    geom_ref,
    excite_ref,
    snode_ref,
    sweight_ref,
    local,
    node_send,
    node_recv,
    bulk_send,
    bulk_recv,
    moment_send,
    moment_recv,
    far_sem,
):
    n_row = lax.axis_size("row")
    row = lax.axis_index("row")
    col = lax.axis_index("col")
    home = lax.rem(row, 2)
    place = row // 2
    chips = n_row // 2
    band = node_all.shape[0]
    reach = (band - 1) // 2
    qn = snode_hbm.shape[1]
    tail = qn - LANES
    step_nodes = qn // ORDERS
    per = excite_hbm.shape[0]
    blk, width = out_ref.shape
    near_pairs = moment.shape[0]
    first_pair = jnp.clip((row - reach + band - 1) // 2 - (band - 1) // 2, 0, chips - near_pairs)
    mine = home == col
    upper = row >= chips
    lane = lax.broadcasted_iota(jnp.int32, (1, LANES), 1)

    def outward(index, count):
        return jnp.where(upper, index, count - 1 - index)

    barrier = pltpu.get_barrier_semaphore()

    def greet(chip, core):
        pl.semaphore_signal(
            barrier, inc=1, device_id={"row": chip, "col": core}, device_id_type=MESH
        )

    @pl.loop(0, n_row)
    def _(index):
        chip = outward(index, n_row)

        @pl.when(chip != row)
        def _():
            greet(chip, col)

        @pl.when(jnp.logical_or(lax.rem(chip, 2) == col, chip == row))
        def _():
            greet(chip, 1 - col)

    loads = [
        pltpu.make_async_copy(here, there, local.at[index])
        for index, (here, there) in enumerate(
            (
                (geom_hbm, geom_ref),
                (excite_hbm, excite_ref),
                (snode_hbm, snode_ref),
                (sweight_hbm, sweight_ref),
                (wave_hbm, wave_ref),
                (tnode_hbm, tnode_ref),
                (tgt_hbm, tgt_ref),
                (order_hbm, order_ref),
                (tweight_hbm, tweight_ref),
            )
        )
    ]
    for load in loads:
        load.start()

    loads[0].wait()
    pieces = LANES // (2 * per)
    spread = jnp.concatenate([geom_ref[...]] * (LANES // per), 1)
    begin = (2 * lax.rem(place, pieces) + col) * per
    inside = jnp.logical_and(lane >= begin, lane < begin + per)
    spread = jnp.where(inside, spread, 0.0)
    first = spread.astype(jnp.bfloat16).astype(jnp.float32)
    second = (spread - first).astype(jnp.bfloat16).astype(jnp.float32)
    third = (spread - first) - second
    rest = jnp.zeros((per - 12, LANES), jnp.float32)
    bulk_pack[1] = jnp.concatenate([first, second, third, rest], 0).astype(jnp.bfloat16)
    loads[1].wait()
    bulk_pack[0] = excite_ref[...]
    loads[2].wait()
    nodes = snode_ref[...]
    gap = jnp.zeros((nodes.shape[0], LANES - tail), jnp.float32)
    even = lax.rem(row, 2) == 0
    node_all[reach, 0:3] = jnp.where(even, nodes[:, :LANES], nodes[:, qn - LANES :])
    node_all[reach, 4:7] = jnp.where(
        even,
        jnp.concatenate([nodes[:, LANES:], gap], 1),
        jnp.concatenate([gap, nodes[:, :tail]], 1),
    )
    node_all[reach, 3:4] = jnp.zeros((1, LANES), jnp.float32)
    node_all[reach, 7:8] = jnp.zeros((1, LANES), jnp.float32)
    loads[3].wait()
    bulk_pack[2] = sweight_ref[0, :, :LANES]
    bulk_pack[3] = jnp.concatenate(
        [sweight_ref[0, :, LANES:].astype(jnp.float32), sweight_ref[1, :, :tail].astype(jnp.float32)], 1
    ).astype(jnp.bfloat16)
    bulk_pack[4] = sweight_ref[1, :, tail:]

    @pl.when(mine)
    def _():
        pltpu.make_async_copy(bulk_pack, bulk_all.at[place, col], bulk_recv.at[place]).start()

    def node_to(chip):
        slot = row - chip + reach
        return pltpu.make_async_remote_copy(
            src_ref=node_all.at[reach],
            dst_ref=node_all.at[slot],
            send_sem=node_send.at[slot],
            recv_sem=node_recv.at[slot],
            device_id={"row": chip},
            device_id_type=MESH,
        )

    def bulk_to(chip, planes):
        return pltpu.make_async_remote_copy(
            src_ref=bulk_pack.at[pl.ds(0, planes)],
            dst_ref=bulk_all.at[place, col, pl.ds(0, planes)],
            send_sem=bulk_send.at[chip],
            recv_sem=bulk_recv.at[place],
            device_id={"row": chip, "col": home},
            device_id_type=MESH,
        )

    def is_near(chip):
        return jnp.logical_and(chip >= row - reach, chip <= row + reach)

    def for_sends(name):
        @pl.loop(0, n_row)
        def _(index):
            chip = outward(index, n_row)
            near = is_near(chip)

            @pl.when(jnp.logical_and(near, chip != row))
            def _():
                getattr(node_to(chip), name)()

            @pl.when(jnp.logical_and(near, jnp.logical_not(jnp.logical_and(mine, chip == row))))
            def _():
                getattr(bulk_to(chip, 5), name)()

            @pl.when(jnp.logical_not(near))
            def _():
                getattr(bulk_to(chip, 2), name)()

    def order_of(chip):
        offset = jnp.clip(chip - row + reach, 0, 2 * reach)
        return jnp.where(is_near(chip), order_ref[col, offset] * step_nodes, 0)

    def turns_per_unit():
        return wave_ref[0] * (0.5 / PI)

    def scaled(places):
        return (places - tnode_ref[:, 0:1]) * turns_per_unit()

    def prepare():
        rate = turns_per_unit()
        begin = pl.multiple_of(col * blk, blk)
        cols = columns_of(tnode_ref[...])
        origin = cols[0:1]
        cols = jnp.where(col == 0, cols[:qn], cols[qn:])
        cols = (cols - origin) * rate
        for axis in range(3):
            tnode_wide[axis] = jnp.broadcast_to(cols[:, axis : axis + 1], (qn, LANES))
        loads[6].wait()
        cols = columns_of(tgt_ref[...])
        for axis in range(6):
            line = cols[:, axis : axis + 1]
            if axis < 3:
                line = (line - origin[:, axis : axis + 1]) * rate
            tgt_wide[axis] = jnp.broadcast_to(line, (2 * blk, LANES))
        loads[8].wait()
        for part in range(2):
            tests[part * blk : (part + 1) * blk] = tweight_ref[part, :, pl.ds(begin, blk)].T
        for pair in range(near_pairs):
            for core in range(2):

                @pl.when(jnp.logical_not(is_near(2 * (first_pair + pair) + core)))
                def _():
                    moment[pair, core * qn : (core + 1) * qn] = jnp.zeros((qn, 2 * width), jnp.bfloat16)
                    at = (3 * pair + 2 * core) * LANES
                    green_high[:, at : at + LANES] = jnp.zeros((2 * qn, LANES), jnp.bfloat16)
                    green_low[:, at : at + LANES] = jnp.zeros((2 * qn, LANES), jnp.bfloat16)

    def green_of(chunk, places, limit, ahead):
        rate = turns_per_unit()
        soft = rate * rate * (SOFT * SOFT)
        places = scaled(places)
        s_x, s_y, s_z = (places[i : i + 1] for i in range(3))
        at = pl.ds(pl.multiple_of(chunk * LANES, LANES), LANES)
        for group in range(ORDERS):
            here = slice(group * step_nodes, (group + 1) * step_nodes)
            live = jnp.logical_and(ahead < limit, limit > group * step_nodes)
            scale = jnp.where(live, rate * (0.25 / PI), 0.0)
            d_x = tnode_wide[0, here] - s_x
            d_y = tnode_wide[1, here] - s_y
            d_z = tnode_wide[2, here] - s_z
            squared = d_x * d_x + d_y * d_y + (d_z * d_z + soft)
            inverse, cosine, u, sine = wave_parts(squared)
            inverse = inverse * scale
            for part, value in enumerate((inverse * cosine, (inverse * u) * sine)):
                high, low = split_two(value)
                to = slice(part * qn + group * step_nodes, part * qn + (group + 1) * step_nodes)
                green_high[to, at] = high
                green_low[to, at] = low

    def green_head(pair, core, places):
        limit = order_of(2 * (first_pair + pair) + core)
        green_of(3 * pair + 2 * core, places, limit, lane + core * tail)

    def slot_of(chip):
        return jnp.clip(chip - row + reach, 0, band - 1)

    def green_middle(pair):
        chip = 2 * (first_pair + pair)
        places = jnp.zeros((3, LANES), jnp.float32)
        for core in range(2):
            value = node_all[slot_of(chip + core), 4:7]
            places = places + jnp.where(is_near(chip + core), value, 0.0)
        limit = jnp.where(lane < tail, order_of(chip), order_of(chip + 1))
        green_of(3 * pair + 1, places, limit, jnp.where(lane < tail, lane + LANES, lane - tail))

    def green_own():
        green_head(place - first_pair, home, node_all[reach, 0:3])

    def green_pair(pair):
        @pl.loop(0, 2)
        def _(core):
            chip = 2 * (first_pair + pair) + core
            slot = slot_of(chip)

            @pl.when(jnp.logical_and(is_near(chip), chip != row))
            def _():
                view = node_all.at[slot]
                pltpu.make_async_copy(view, view, node_recv.at[slot]).wait()
                green_head(pair, core, node_all[slot, 0:3])

        green_middle(pair)

    def pair_live(pair):
        chip = 2 * (first_pair + pair)
        return jnp.logical_or(is_near(chip), is_near(chip + 1))

    def green_some(begin, end):
        @pl.loop(begin, end)
        def _(turn):
            pair = near_pairs - 1 - turn

            @pl.when(pair_live(pair))
            def _():
                green_pair(pair)

            @pl.when(jnp.logical_not(pair_live(pair)))
            def _():
                at = pl.ds(pl.multiple_of((3 * pair + 1) * LANES, LANES), LANES)
                green_high[:, at] = jnp.zeros((2 * qn, LANES), jnp.bfloat16)
                green_low[:, at] = jnp.zeros((2 * qn, LANES), jnp.bfloat16)

    loads[4].wait()
    loads[5].wait()
    loads[7].wait()

    @pl.when(jnp.logical_not(upper))
    def _():
        prepare()
        green_own()

    pl.semaphore_wait(barrier, jnp.where(mine, n_row, 2 * n_row - 1))
    for_sends("start")

    @pl.when(upper)
    def _():
        prepare()
        green_own()

    green_some(0, near_pairs - 1)

    def wait_bulk(index):
        near = is_near(2 * index + col)
        for planes, go in ((5, near), (2, jnp.logical_not(near))):

            @pl.when(go)
            def _():
                view = bulk_all.at[index, :, pl.ds(0, planes)]
                pltpu.make_async_copy(view, view, bulk_recv.at[index]).wait()

    @pl.loop(0, near_pairs)
    def _(turn):
        wait_bulk(first_pair + near_pairs - 1 - turn)

    for pair in range(near_pairs):
        index = first_pair + pair
        rows = bulk_all[index, :, 0].reshape(2 * per, width)
        weights = jnp.concatenate(
            [bulk_all[index, :, 2 + part].reshape(2 * per, LANES) for part in range(3)], 1
        )
        both = lax.dot_general(weights, rows, TN, preferred_element_type=jnp.float32)
        value = plus_i(both[:qn], both[qn:])
        value = jnp.where(is_near(2 * index + col), value, 0.0)
        high, low = split_two(value)
        at = pl.ds(pl.multiple_of(col * qn, tail), qn)
        moment[pair, at, 0:width] = high
        moment[pair, at, width:] = low

    def moment_to(pair, core):
        view = moment.at[pair, pl.ds(pl.multiple_of(core * qn, tail), qn)]
        return pltpu.make_async_remote_copy(
            src_ref=view,
            dst_ref=view,
            send_sem=moment_send.at[pair],
            recv_sem=moment_recv.at[pair],
            device_id={"col": 1 - col},
            device_id_type=MESH,
        )

    def for_moments(core, name):
        @pl.loop(0, near_pairs)
        def _(pair):
            @pl.when(is_near(2 * (first_pair + pair) + core))
            def _():
                getattr(moment_to(pair, core), name)()

    for_moments(col, "start")

    if near_pairs < chips:

        @pl.loop(0, chips)
        def _(index):
            @pl.when(jnp.logical_or(index < first_pair, index >= first_pair + near_pairs))
            def _():
                wait_bulk(index)

    rate = turns_per_unit()
    soft = rate * rate * (SOFT * SOFT)

    @pl.loop(0, chips // pieces)
    def _(chunk):
        packed = bulk_all[pl.ds(chunk * pieces, pieces), :, 1].reshape(2 * pieces, per, LANES)
        packed = jnp.sum(packed.astype(jnp.float32), 0)
        packed = packed[0:4] + packed[4:8] + packed[8:12]
        places = scaled(packed[0:3])
        area = packed[3:4] * (rate * (0.25 / PI))
        rows = bulk_all[pl.ds(chunk * pieces, pieces), :, 0].reshape(LANES, width)

        def impedance_of(block, total):
            begin = pl.multiple_of(block * blk, blk)
            for part in range(2):
                here = pl.ds(begin + part * (blk // 2), blk // 2)
                d_x = tgt_wide[0, here] - places[0:1]
                d_y = tgt_wide[1, here] - places[1:2]
                d_z = tgt_wide[2, here] - places[2:3]
                squared = d_x * d_x + d_y * d_y + (d_z * d_z + soft)
                inverse, cosine, u, sine = wave_parts(squared)
                sine = u * sine
                along = tgt_wide[3, here] * d_x + tgt_wide[4, here] * d_y + tgt_wide[5, here] * d_z
                along = along * inverse
                scale = area * inverse
                green_re = scale * cosine
                green_im = scale * sine
                factor_re = 1.0 - along
                factor_im = along * (inverse * (-0.5 / PI))
                at = part * (blk // 2)
                impedance[at : at + blk // 2] = (
                    green_re * factor_re - green_im * factor_im
                ).astype(jnp.bfloat16)
                impedance[blk + at : blk + at + blk // 2] = (
                    green_re * factor_im + green_im * factor_re
                ).astype(jnp.bfloat16)
            both = jnp.dot(impedance[...], rows, preferred_element_type=jnp.float32)
            fresh = plus_i(both[:blk], both[blk:])
            total[...] = jnp.where(chunk == 0, fresh, total[...] + fresh)

        impedance_of(1 - col, far_send)
        impedance_of(col, far_own)

    swap = pltpu.make_async_remote_copy(
        src_ref=far_send,
        dst_ref=far_recv,
        send_sem=far_sem.at[0],
        recv_sem=far_sem.at[1],
        device_id={"col": 1 - col},
        device_id_type=MESH,
    )
    swap.start()

    green_some(near_pairs - 1, near_pairs)

    for_moments(1 - col, "wait_recv")
    right = moment[...].reshape(near_pairs * 2 * qn, 2 * width)
    both = jnp.dot(green_high[...], right, preferred_element_type=jnp.float32)
    both = both[:, :width] + both[:, width:]
    both = both + jnp.dot(green_low[...], right[:, :width], preferred_element_type=jnp.float32)
    high, low = split_two(plus_i(both[:qn], both[qn:]))
    both = jnp.dot(tests[...], jnp.concatenate([high, low], 1), preferred_element_type=jnp.float32)
    both = both[:, :width] + both[:, width:]
    near = plus_i(both[:blk], both[blk:])
    swap.wait_recv()
    out_ref[...] = (far_own[...] + far_recv[...]) + near

    for_sends("wait_send")
    for_moments(col, "wait_send")
    swap.wait_send()


def on_device(
    wavenumber,
    tgt_geom,
    src_geom,
    excite,
    tgt_nodes,
    src_nodes,
    tgt_weights,
    src_weights,
    near_order,
):
    n_row = lax.axis_size("row")
    chips = n_row // 2
    band = near_order.shape[1]
    blk = tgt_geom.shape[1] // 2
    qn = src_nodes.shape[1]
    per, width = src_geom.shape[1], excite.shape[0]
    excite_rows = excite.T
    weight_rows = src_weights.transpose(0, 2, 1)
    near_pairs = min(band // 2 + 1, chips)
    depth = near_pairs * 2 * qn
    hbm = pl.BlockSpec(memory_space=pl.ANY)
    dma = pltpu.SemaphoreType.DMA
    f32, bf16 = jnp.float32, jnp.bfloat16
    return pl.pallas_call(
        kernel,
        out_shape=pltpu.VMEM((blk, width), f32),
        in_specs=[hbm] * 9,
        out_specs=pl.BlockSpec(memory_space=pltpu.VMEM),
        scratch_shapes=[
            pltpu.VMEM((band, ROWS, LANES), f32),
            pltpu.VMEM((chips, 2, 5, per, LANES), bf16),
            pltpu.VMEM((5, per, LANES), bf16),
            pltpu.VMEM((3, qn, LANES), f32),
            pltpu.VMEM((6, 2 * blk, LANES), f32),
            pltpu.VMEM((2 * blk, qn), bf16),
            pltpu.VMEM((2 * qn, depth), bf16),
            pltpu.VMEM((2 * qn, depth), bf16),
            pltpu.VMEM((near_pairs, 2 * qn, 2 * width), bf16),
            pltpu.VMEM((2 * blk, LANES), bf16),
            pltpu.VMEM((blk, width), f32),
            pltpu.VMEM((blk, width), f32),
            pltpu.VMEM((blk, width), f32),
            pltpu.SMEM(wavenumber.shape, f32),
            pltpu.SMEM(near_order.shape, jnp.int32),
            pltpu.VMEM(tgt_geom.shape, f32),
            pltpu.VMEM(tgt_nodes.shape, f32),
            pltpu.VMEM(tgt_weights.shape, bf16),
            pltpu.VMEM(src_geom.shape, f32),
            pltpu.VMEM(excite_rows.shape, bf16),
            pltpu.VMEM(src_nodes.shape, f32),
            pltpu.VMEM(weight_rows.shape, bf16),
            dma((9,)),
            dma((band,)),
            dma((band,)),
            dma((n_row,)),
            dma((chips,)),
            dma((near_pairs,)),
            dma((near_pairs,)),
            dma((2,)),
        ],
        compiler_params=pltpu.CompilerParams(collective_id=0, has_side_effects=True),
        name="slab",
    )(
        wavenumber,
        near_order,
        tgt_geom,
        tgt_nodes,
        tgt_weights,
        src_geom,
        excite_rows,
        src_nodes,
        weight_rows,
    )


def solution(mesh):
    return jax.shard_map(
        on_device,
        mesh=mesh,
        in_specs=(
            P("groups"),
            P(None, ("groups", "row")),
            P(None, ("groups", "row", "col")),
            P(None, ("groups", "row", "col")),
            P(None, ("groups", "row")),
            P(None, ("groups", "row")),
            P(None, None, ("groups", "row")),
            P(None, None, ("groups", "row", "col")),
            P(("groups", "row"), None),
        ),
        out_specs=P(("groups", "row", "col"), None),
        check_vma=False,
    )
```

```python
import math

import jax
import jax.numpy as jnp
import numpy as np
from jax import lax
from jax.experimental import pallas as pl
from jax.experimental.pallas import tpu as pltpu
from jax.sharding import PartitionSpec as P

ORDERS = 3
SOFT = 0.05
PI = math.pi
LANES = 128
ROWS = 8
MESH = pl.DeviceIdType.MESH
TN = (((0,), (0,)), ((), ()))


def fitted(function, terms):
    nodes = (np.cos((np.arange(terms) + 0.5) * np.pi / terms) + 1.0) / 8.0
    matrix = np.vander(nodes, terms, increasing=True)
    return [float(c) for c in np.linalg.solve(matrix, function(np.sqrt(nodes)))]


COS = fitted(lambda u: np.cos(2.0 * np.pi * u), 6)
SIN = fitted(lambda u: np.sin(2.0 * np.pi * u) / u, 6)


def horner(coefficients, y):
    total = coefficients[-1]
    for c in coefficients[-2::-1]:
        total = total * y + c
    return total


def wave_parts(squared):
    inverse = lax.rsqrt(squared)
    turns = squared * inverse
    u = turns - jnp.round(turns)
    y = u * u
    return inverse, horner(COS, y), u, horner(SIN, y)


def plus_i(first, second):
    half = second.shape[1] // 2
    swapped = pltpu.roll(second, half, 1)
    lane = lax.broadcasted_iota(jnp.int32, second.shape, 1)
    return first + jnp.where(lane < half, -swapped, swapped)


def split_two(value):
    high = value.astype(jnp.bfloat16)
    return high, (value - high.astype(jnp.float32)).astype(jnp.bfloat16)


def columns_of(rows):
    few, lanes = rows.shape
    pad = jnp.zeros((ROWS - few, lanes), jnp.float32)
    return jnp.concatenate([rows, pad], 0).T


def kernel(
    wave_hbm,
    order_hbm,
    tgt_hbm,
    tnode_hbm,
    tweight_hbm,
    geom_hbm,
    excite_hbm,
    snode_hbm,
    sweight_hbm,
    out_ref,
    small_all,
    bulk_all,
    small_pack,
    bulk_pack,
    tnode_wide,
    tgt_wide,
    origin,
    scale_all,
    tests,
    green_high,
    green_low,
    moment,
    impedance,
    part_send,
    part_recv,
    wave_ref,
    order_ref,
    tgt_ref,
    tnode_ref,
    tweight_ref,
    geom_ref,
    excite_ref,
    snode_ref,
    sweight_ref,
    local,
    small_send,
    bulk_send,
    small_recv,
    bulk_recv,
    part_sem,
):
    n_row = lax.axis_size("row")
    row = lax.axis_index("row")
    col = lax.axis_index("col")
    home = lax.rem(row, 2)
    place = row // 2
    chips = n_row // 2
    reach = (order_hbm.shape[1] - 1) // 2
    qn = snode_hbm.shape[1]
    tail = qn - LANES
    step_nodes = qn // ORDERS
    per = excite_hbm.shape[0]
    blk, width = out_ref.shape
    near_pairs = moment.shape[0]
    first_pair = jnp.clip(
        (row - reach - col + 1 + 4 * reach) // 4 - reach, 0, chips // 2 - near_pairs
    )
    mine = home == col
    upper = row >= chips
    lane = lax.broadcasted_iota(jnp.int32, (1, LANES), 1)

    def outward(index, count):
        return jnp.where(upper, index, count - 1 - index)

    barrier = pltpu.get_barrier_semaphore()

    @pl.loop(0, n_row)
    def _(index):
        index = outward(index, n_row)
        chip, core = 2 * (index // 2) + col, lax.rem(index, 2)

        @pl.when(jnp.logical_not(jnp.logical_and(chip == row, core == col)))
        def _():
            pl.semaphore_signal(
                barrier, inc=1, device_id={"row": chip, "col": core}, device_id_type=MESH
            )

    @pl.when(jnp.logical_not(mine))
    def _():
        pl.semaphore_signal(barrier, inc=1, device_id={"col": 1 - col}, device_id_type=MESH)

    loads = [
        pltpu.make_async_copy(here, there, local.at[index])
        for index, (here, there) in enumerate(
            (
                (snode_hbm, snode_ref),
                (geom_hbm, geom_ref),
                (excite_hbm, excite_ref),
                (sweight_hbm, sweight_ref),
                (wave_hbm, wave_ref),
                (tnode_hbm, tnode_ref),
                (tgt_hbm, tgt_ref),
                (order_hbm, order_ref),
                (tweight_hbm, tweight_ref),
            )
        )
    ]
    for load in loads:
        load.start()

    def heads_of(nodes):
        return jnp.where(lax.rem(place, 2) == 0, nodes[:, :LANES], nodes[:, tail:])

    loads[0].wait()
    nodes = snode_ref[...]
    gap = jnp.zeros((nodes.shape[0], LANES - tail), jnp.float32)
    ends = jnp.where(
        lax.rem(place, 2) == 0,
        jnp.concatenate([nodes[:, LANES:], gap], 1),
        jnp.concatenate([gap, nodes[:, :tail]], 1),
    )
    small_pack[0:3, :] = jnp.where(col == 0, heads_of(nodes), ends)
    loads[1].wait()
    pieces = LANES // (2 * per)
    spread = jnp.concatenate([geom_ref[...]] * (LANES // per), 1)
    begin = (2 * lax.rem(place, pieces) + col) * per
    inside = jnp.logical_and(lane >= begin, lane < begin + per)
    small_pack[3:4, :] = jnp.zeros((1, LANES), jnp.float32)
    small_pack[4:8, :] = jnp.where(inside, spread, 0.0)

    @pl.when(mine)
    def _():
        pltpu.make_async_copy(small_pack, small_all.at[place, col], small_recv.at[place]).start()

    def pack_bulk():
        loads[2].wait()
        bulk_pack[0] = excite_ref[...]
        loads[3].wait()
        bulk_pack[1] = sweight_ref[0, :, :LANES]
        bulk_pack[2] = jnp.concatenate(
            [sweight_ref[0, :, LANES:].astype(jnp.float32), sweight_ref[1, :, :tail].astype(jnp.float32)], 1
        ).astype(jnp.bfloat16)
        bulk_pack[3] = sweight_ref[1, :, tail:]

        @pl.when(mine)
        def _():
            pltpu.make_async_copy(bulk_pack, bulk_all.at[place, col], bulk_recv.at[place]).start()

    def small_to(chip):
        return pltpu.make_async_remote_copy(
            src_ref=small_pack,
            dst_ref=small_all.at[place, col],
            send_sem=small_send.at[chip],
            recv_sem=small_recv.at[place],
            device_id={"row": chip, "col": home},
            device_id_type=MESH,
        )

    def bulk_to(chip, planes):
        return pltpu.make_async_remote_copy(
            src_ref=bulk_pack.at[pl.ds(0, planes)],
            dst_ref=bulk_all.at[place, col, pl.ds(0, planes)],
            send_sem=bulk_send.at[chip],
            recv_sem=bulk_recv.at[place],
            device_id={"row": chip, "col": home},
            device_id_type=MESH,
        )

    def is_near(chip):
        return jnp.logical_and(chip >= row - reach, chip <= row + reach)

    def for_others(act, begin, end):
        @pl.loop(begin, end)
        def _(chip):
            @pl.when(jnp.logical_not(jnp.logical_and(mine, chip == row)))
            def _():
                act(chip)

    def small_act(name):
        return lambda chip: getattr(small_to(chip), name)()

    def bulk_act(name):
        def act(chip):
            near = is_near(chip)

            @pl.when(near)
            def _():
                getattr(bulk_to(chip, 4), name)()

            @pl.when(jnp.logical_not(near))
            def _():
                getattr(bulk_to(chip, 1), name)()

        return act

    def order_of(block, chip):
        offset = jnp.clip(chip - row + reach, 0, 2 * reach)
        return jnp.where(is_near(chip), order_ref[block, offset] * step_nodes, 0)

    def chip_of(pair, slot):
        return 4 * (first_pair + pair) + 2 * slot + col

    def prepare():
        loads[4].wait()
        loads[5].wait()
        loads[7].wait()
        rate = wave_ref[0] * (0.5 / PI)
        origin[0:3] = jnp.broadcast_to(tnode_ref[:, 0:1], (3, LANES))
        cols = columns_of(tnode_ref[...])
        first = cols[0:1]
        cols = (cols - first) * rate
        for block in range(2):
            for axis in range(3):
                tnode_wide[block, axis] = jnp.broadcast_to(
                    cols[block * qn : (block + 1) * qn, axis : axis + 1], (qn, LANES)
                )

        @pl.loop(0, near_pairs)
        def _(pair):
            for block in range(2):
                even, odd = (order_of(block, chip_of(pair, slot)) for slot in range(2))
                middle = jnp.where(lane < tail, even, odd)
                for part, (limit, ahead) in enumerate(
                    (
                        (even, lane),
                        (middle, jnp.where(lane < tail, lane + LANES, lane - tail)),
                        (odd, lane + tail),
                    )
                ):
                    for group in range(ORDERS):
                        live = jnp.logical_and(ahead < limit, limit > group * step_nodes)
                        value = jnp.where(live, rate * (0.25 / PI), 0.0)
                        at = (3 * pair + part) * 2 + block
                        scale_all[at, group] = jnp.broadcast_to(value, (ROWS, LANES))

            for slot in range(2):

                @pl.when(jnp.logical_not(is_near(chip_of(pair, slot))))
                def _():
                    at = pl.ds(pl.multiple_of((3 * pair + 2 * slot) * LANES, LANES), LANES)
                    for block in range(2):
                        green_high[block, :, at] = jnp.zeros((2 * qn, LANES), jnp.bfloat16)
                        green_low[block, :, at] = jnp.zeros((2 * qn, LANES), jnp.bfloat16)

            @pl.when(jnp.logical_not(pair_live(pair)))
            def _():
                at = pl.ds(pl.multiple_of((3 * pair + 1) * LANES, LANES), LANES)
                for block in range(2):
                    green_high[block, :, at] = jnp.zeros((2 * qn, LANES), jnp.bfloat16)
                    green_low[block, :, at] = jnp.zeros((2 * qn, LANES), jnp.bfloat16)

        @pl.when(mine)
        def _():
            own = place - 2 * first_pair
            green_of(3 * (own // 2) + 2 * lax.rem(own, 2), heads_of(snode_ref[...]))

        loads[6].wait()
        cols = columns_of(tgt_ref[...])
        for axis in range(6):
            line = cols[:, axis : axis + 1]
            if axis < 3:
                line = (line - first[:, axis : axis + 1]) * rate
            tgt_wide[axis] = jnp.broadcast_to(line, (2 * blk, LANES))
        loads[8].wait()
        for block in range(2):
            at = slice(block * blk, (block + 1) * blk)
            for part in range(2):
                tests[block, part * blk : (part + 1) * blk] = tweight_ref[part, :, at].T

    def pair_live(pair):
        return jnp.logical_or(is_near(chip_of(pair, 0)), is_near(chip_of(pair, 1)))

    def scaled(places):
        rate = wave_ref[0] * (0.5 / PI)
        return (places - origin[0:3]) * rate, rate * rate * (SOFT * SOFT)

    def green_of(chunk, places):
        places, soft = scaled(places)
        s_x, s_y, s_z = (jnp.broadcast_to(places[i : i + 1], (step_nodes, LANES)) for i in range(3))
        at = pl.ds(pl.multiple_of(chunk * LANES, LANES), LANES)

        @pl.loop(0, 2)
        def _(block):
            for group in range(ORDERS):
                here = slice(group * step_nodes, (group + 1) * step_nodes)
                scale = jnp.broadcast_to(scale_all[chunk * 2 + block, group, 0:1], (step_nodes, LANES))
                d_x = tnode_wide[block, 0, here] - s_x
                d_y = tnode_wide[block, 1, here] - s_y
                d_z = tnode_wide[block, 2, here] - s_z
                squared = d_x * d_x + d_y * d_y + (d_z * d_z + soft)
                inverse, cosine, u, sine = wave_parts(squared)
                inverse = inverse * scale
                for part, value in enumerate((inverse * cosine, (inverse * u) * sine)):
                    high, low = split_two(value)
                    to = slice(part * qn + group * step_nodes, part * qn + (group + 1) * step_nodes)
                    green_high[block, to, at] = high
                    green_low[block, to, at] = low

    urgent = n_row // 4

    @pl.when(jnp.logical_not(upper))
    def _():
        pack_bulk()
        prepare()

    pl.semaphore_wait(barrier, n_row)
    for_others(small_act("start"), 0, n_row)

    @pl.when(upper)
    def _():
        pack_bulk()

    for_others(bulk_act("start"), 0, urgent)

    @pl.when(upper)
    def _():
        prepare()

    for_others(bulk_act("start"), urgent, n_row)

    def wait_small(index):
        view = small_all.at[index]
        pltpu.make_async_copy(view, view, small_recv.at[index]).wait()

    def wait_bulk(index):
        near = is_near(2 * index + col)
        for planes, go in ((4, near), (1, jnp.logical_not(near))):

            @pl.when(go)
            def _():
                view = bulk_all.at[index, :, pl.ds(0, planes)]
                pltpu.make_async_copy(view, view, bulk_recv.at[index]).wait()

    @pl.loop(0, near_pairs)
    def _(turn):
        pair = near_pairs - 1 - turn
        base = 2 * (first_pair + pair)

        @pl.loop(0, 2)
        def _(slot):
            slot = 1 - slot
            wait_small(base + slot)
            chip = chip_of(pair, slot)

            @pl.when(jnp.logical_and(is_near(chip), chip != row))
            def _():
                green_of(3 * pair + 2 * slot, small_all[base + slot, 0, 0:3])

        @pl.when(pair_live(pair))
        def _():
            green_of(3 * pair + 1, small_all[base, 1, 0:3] + small_all[base + 1, 1, 0:3])

    def for_rest(act):
        if 2 * near_pairs < chips:

            @pl.loop(0, chips)
            def _(index):
                @pl.when(jnp.logical_or(index < 2 * first_pair, index >= 2 * (first_pair + near_pairs)))
                def _():
                    act(index)

    for_rest(wait_small)

    def impedance_of(chunk):
        packed = small_all[pl.ds(chunk * pieces, pieces), :, 4:8, :].reshape(2 * pieces, 4, LANES)
        packed = jnp.sum(packed, 0)
        places, soft = scaled(packed[0:3])
        area = packed[3:4] * (wave_ref[0] * (0.125 / PI / PI))
        at = pl.ds(pl.multiple_of(chunk * LANES, LANES), LANES)
        for part in range(4):
            block, half = part // 2, part % 2
            count = blk // 2
            here = slice(part * count, (part + 1) * count)
            d_x = tgt_wide[0, here] - places[0:1]
            d_y = tgt_wide[1, here] - places[1:2]
            d_z = tgt_wide[2, here] - places[2:3]
            squared = d_x * d_x + d_y * d_y + (d_z * d_z + soft)
            inverse, cosine, u, sine = wave_parts(squared)
            sine = u * sine
            along = tgt_wide[3, here] * d_x + tgt_wide[4, here] * d_y + tgt_wide[5, here] * d_z
            along = along * inverse
            scale = area * inverse
            green_re = scale * cosine
            green_im = scale * sine
            factor_re = 1.0 - along
            factor_im = along * (inverse * (-0.5 / PI))
            for side, value in enumerate(
                (
                    green_re * factor_re - green_im * factor_im,
                    green_re * factor_im + green_im * factor_re,
                )
            ):
                to = slice(side * blk + half * count, side * blk + (half + 1) * count)
                impedance[block, to, at] = value.astype(jnp.bfloat16)

    @pl.loop(0, chips // pieces)
    def _(chunk):
        impedance_of(chunk)

    @pl.loop(0, near_pairs)
    def _(pair):
        wait_bulk(2 * (first_pair + pair))
        wait_bulk(2 * (first_pair + pair) + 1)

    for slot in range(2 * near_pairs):
        index = 2 * first_pair + slot
        rows = bulk_all[index, :, 0].reshape(2 * per, width)
        weights = jnp.concatenate(
            [bulk_all[index, :, 1 + part].reshape(2 * per, LANES) for part in range(3)], 1
        )
        both = lax.dot_general(weights, rows, TN, preferred_element_type=jnp.float32)
        value = plus_i(both[:qn], both[qn:])
        value = jnp.where(is_near(2 * index + col), value, 0.0)
        high, low = split_two(value)
        at = slice((slot % 2) * qn, (slot % 2 + 1) * qn)
        moment[slot // 2, at, 0:width] = high
        moment[slot // 2, at, width:] = low

    for_rest(wait_bulk)

    def partial(block):
        def far_step(chunk, total):
            rows = bulk_all[pl.ds(chunk * pieces, pieces), :, 0].reshape(LANES, width)
            at = pl.ds(pl.multiple_of(chunk * LANES, LANES), LANES)
            return total + jnp.dot(impedance[block, :, at], rows, preferred_element_type=jnp.float32)

        right = moment[...].reshape(near_pairs * 2 * qn, 2 * width)
        both = jnp.dot(green_high[block], right, preferred_element_type=jnp.float32)
        both = both[:, :width] + both[:, width:]
        both = both + jnp.dot(green_low[block], right[:, :width], preferred_element_type=jnp.float32)
        high, low = split_two(plus_i(both[:qn], both[qn:]))
        product = jnp.dot(tests[block], jnp.concatenate([high, low], 1), preferred_element_type=jnp.float32)
        both = product[:, :width] + product[:, width:]
        if chips == pieces:
            both = far_step(0, both)
        else:
            both = lax.fori_loop(0, chips // pieces, far_step, both)
        return plus_i(both[:blk], both[blk:])

    swap = pltpu.make_async_remote_copy(
        src_ref=part_send,
        dst_ref=part_recv,
        send_sem=part_sem.at[0],
        recv_sem=part_sem.at[1],
        device_id={"col": 1 - col},
        device_id_type=MESH,
    )
    part_send[...] = partial(1 - col)
    swap.start()
    out_ref[...] = partial(col)
    for_others(small_act("wait_send"), 0, n_row)
    for_others(bulk_act("wait_send"), 0, n_row)
    swap.wait_recv()
    out_ref[...] += part_recv[...]
    swap.wait_send()


def on_device(
    wavenumber,
    tgt_geom,
    src_geom,
    excite,
    tgt_nodes,
    src_nodes,
    tgt_weights,
    src_weights,
    near_order,
):
    n_row = lax.axis_size("row")
    chips = n_row // 2
    blk = tgt_geom.shape[1] // 2
    qn = src_nodes.shape[1]
    per, width = src_geom.shape[1], excite.shape[0]
    excite_rows = excite.T
    weight_rows = src_weights.transpose(0, 2, 1)
    reach = (near_order.shape[1] - 1) // 2
    near_pairs = min(reach // 2 + 1, chips // 2)
    depth = near_pairs * 2 * qn
    hbm = pl.BlockSpec(memory_space=pl.ANY)
    dma = pltpu.SemaphoreType.DMA
    f32, bf16 = jnp.float32, jnp.bfloat16
    return pl.pallas_call(
        kernel,
        out_shape=pltpu.VMEM((blk, width), f32),
        in_specs=[hbm] * 9,
        out_specs=pl.BlockSpec(memory_space=pltpu.VMEM),
        scratch_shapes=[
            pltpu.VMEM((chips, 2, ROWS, LANES), f32),
            pltpu.VMEM((chips, 2, 4, per, LANES), bf16),
            pltpu.VMEM((ROWS, LANES), f32),
            pltpu.VMEM((4, per, LANES), bf16),
            pltpu.VMEM((2, 3, qn, LANES), f32),
            pltpu.VMEM((6, 2 * blk, LANES), f32),
            pltpu.VMEM((ROWS, LANES), f32),
            pltpu.VMEM((near_pairs * 6, ORDERS, ROWS, LANES), f32),
            pltpu.VMEM((2, 2 * blk, qn), bf16),
            pltpu.VMEM((2, 2 * qn, depth), bf16),
            pltpu.VMEM((2, 2 * qn, depth), bf16),
            pltpu.VMEM((near_pairs, 2 * qn, 2 * width), bf16),
            pltpu.VMEM((2, 2 * blk, chips * 2 * per), bf16),
            pltpu.VMEM((blk, width), f32),
            pltpu.VMEM((blk, width), f32),
            pltpu.SMEM(wavenumber.shape, f32),
            pltpu.SMEM(near_order.shape, jnp.int32),
            pltpu.VMEM(tgt_geom.shape, f32),
            pltpu.VMEM(tgt_nodes.shape, f32),
            pltpu.VMEM(tgt_weights.shape, bf16),
            pltpu.VMEM(src_geom.shape, f32),
            pltpu.VMEM(excite_rows.shape, bf16),
            pltpu.VMEM(src_nodes.shape, f32),
            pltpu.VMEM(weight_rows.shape, bf16),
            dma((9,)),
            dma((n_row,)),
            dma((n_row,)),
            dma((chips,)),
            dma((chips,)),
            dma((2,)),
        ],
        compiler_params=pltpu.CompilerParams(collective_id=0, has_side_effects=True),
        name="slab",
    )(
        wavenumber,
        near_order,
        tgt_geom,
        tgt_nodes,
        tgt_weights,
        src_geom,
        excite_rows,
        src_nodes,
        weight_rows,
    )


def solution(mesh):
    return jax.shard_map(
        on_device,
        mesh=mesh,
        in_specs=(
            P("groups"),
            P(None, ("groups", "row")),
            P(None, ("groups", "row", "col")),
            P(None, ("groups", "row", "col")),
            P(None, ("groups", "row")),
            P(None, ("groups", "row")),
            P(None, None, ("groups", "row")),
            P(None, None, ("groups", "row", "col")),
            P(("groups", "row"), None),
        ),
        out_specs=P(("groups", "row", "col"), None),
        check_vma=False,
    )
```

```python
import math

import jax
import jax.numpy as jnp
import numpy as np
from jax import lax
from jax.experimental import pallas as pl
from jax.experimental.pallas import tpu as pltpu
from jax.sharding import PartitionSpec as P

ORDERS = 3
SOFT = 0.05
PI = math.pi
LANES = 128
ROWS = 8
MESH = pl.DeviceIdType.MESH
TN = (((0,), (0,)), ((), ()))


def fitted(function, terms):
    nodes = (np.cos((np.arange(terms) + 0.5) * np.pi / terms) + 1.0) / 8.0
    matrix = np.vander(nodes, terms, increasing=True)
    return [float(c) for c in np.linalg.solve(matrix, function(np.sqrt(nodes)))]


COS = fitted(lambda u: np.cos(2.0 * np.pi * u), 6)
SIN = fitted(lambda u: np.sin(2.0 * np.pi * u) / u, 6)


def horner(coefficients, y):
    total = coefficients[-1]
    for c in coefficients[-2::-1]:
        total = total * y + c
    return total


def wave_parts(squared):
    inverse = lax.rsqrt(squared)
    turns = squared * inverse
    u = turns - jnp.round(turns)
    y = u * u
    return inverse, horner(COS, y), u, horner(SIN, y)


def plus_i(first, second):
    half = second.shape[1] // 2
    swapped = pltpu.roll(second, half, 1)
    lane = lax.broadcasted_iota(jnp.int32, second.shape, 1)
    return first + jnp.where(lane < half, -swapped, swapped)


def split_two(value):
    high = value.astype(jnp.bfloat16)
    return high, (value - high.astype(jnp.float32)).astype(jnp.bfloat16)


def columns_of(rows):
    few, lanes = rows.shape
    pad = jnp.zeros((ROWS - few, lanes), jnp.float32)
    return jnp.concatenate([rows, pad], 0).T


def kernel(
    wave_hbm,
    order_hbm,
    tgt_hbm,
    tnode_hbm,
    tweight_hbm,
    geom_hbm,
    excite_hbm,
    snode_hbm,
    sweight_hbm,
    out_ref,
    small_all,
    bulk_all,
    small_pack,
    bulk_pack,
    tnode_wide,
    tgt_wide,
    origin,
    scale_all,
    tests,
    green_high,
    green_low,
    moment,
    impedance,
    part_send,
    part_recv,
    wave_ref,
    order_ref,
    tgt_ref,
    tnode_ref,
    tweight_ref,
    geom_ref,
    excite_ref,
    snode_ref,
    sweight_ref,
    local,
    small_send,
    bulk_send,
    small_recv,
    bulk_recv,
    part_sem,
    ready,
):
    n_row = lax.axis_size("row")
    row = lax.axis_index("row")
    col = lax.axis_index("col")
    home = lax.rem(row, 2)
    place = row // 2
    chips = n_row // 2
    reach = (order_hbm.shape[1] - 1) // 2
    qn = snode_hbm.shape[1]
    tail = qn - LANES
    step_nodes = qn // ORDERS
    per = excite_hbm.shape[0]
    blk, width = out_ref.shape
    near_pairs = moment.shape[0]
    first_pair = jnp.clip(
        (row - reach - col + 1 + 4 * reach) // 4 - reach, 0, chips // 2 - near_pairs
    )
    mine = home == col
    lane = lax.broadcasted_iota(jnp.int32, (1, LANES), 1)

    loads = [
        pltpu.make_async_copy(here, there, local.at[index])
        for index, (here, there) in enumerate(
            (
                (snode_hbm, snode_ref),
                (geom_hbm, geom_ref),
                (excite_hbm, excite_ref),
                (sweight_hbm, sweight_ref),
                (wave_hbm, wave_ref),
                (tnode_hbm, tnode_ref),
                (tgt_hbm, tgt_ref),
                (order_hbm, order_ref),
                (tweight_hbm, tweight_ref),
            )
        )
    ]
    for load in loads:
        load.start()

    barrier = pltpu.get_barrier_semaphore()

    @pl.loop(2 * row + col + 1, 2 * n_row)
    def _(index):
        pl.semaphore_signal(
            barrier,
            inc=1,
            device_id={"row": index // 2, "col": lax.rem(index, 2)},
            device_id_type=MESH,
        )

    def heads_of(nodes):
        return jnp.where(lax.rem(place, 2) == 0, nodes[:, :LANES], nodes[:, tail:])

    loads[0].wait()
    nodes = snode_ref[...]
    gap = jnp.zeros((nodes.shape[0], LANES - tail), jnp.float32)
    ends = jnp.where(
        lax.rem(place, 2) == 0,
        jnp.concatenate([nodes[:, LANES:], gap], 1),
        jnp.concatenate([gap, nodes[:, :tail]], 1),
    )
    small_pack[0:3, :] = jnp.where(col == 0, heads_of(nodes), ends)
    loads[1].wait()
    pieces = LANES // (2 * per)
    spread = jnp.concatenate([geom_ref[...]] * (LANES // per), 1)
    begin = (2 * lax.rem(place, pieces) + col) * per
    inside = jnp.logical_and(lane >= begin, lane < begin + per)
    small_pack[3:4, :] = jnp.zeros((1, LANES), jnp.float32)
    small_pack[4:8, :] = jnp.where(inside, spread, 0.0)

    @pl.when(mine)
    def _():
        pltpu.make_async_copy(small_pack, small_all.at[place, col], small_recv.at[place]).start()

    def pack_bulk():
        loads[2].wait()
        bulk_pack[0] = excite_ref[...]
        loads[3].wait()
        bulk_pack[1] = sweight_ref[0, :, :LANES]
        bulk_pack[2] = jnp.concatenate(
            [sweight_ref[0, :, LANES:].astype(jnp.float32), sweight_ref[1, :, :tail].astype(jnp.float32)], 1
        ).astype(jnp.bfloat16)
        bulk_pack[3] = sweight_ref[1, :, tail:]

        @pl.when(mine)
        def _():
            pltpu.make_async_copy(bulk_pack, bulk_all.at[place, col], bulk_recv.at[place]).start()

    def small_to(chip):
        return pltpu.make_async_remote_copy(
            src_ref=small_pack,
            dst_ref=small_all.at[place, col],
            send_sem=small_send.at[chip],
            recv_sem=small_recv.at[place],
            device_id={"row": chip, "col": home},
            device_id_type=MESH,
        )

    def bulk_to(chip, planes):
        return pltpu.make_async_remote_copy(
            src_ref=bulk_pack.at[pl.ds(0, planes)],
            dst_ref=bulk_all.at[place, col, pl.ds(0, planes)],
            send_sem=bulk_send.at[chip],
            recv_sem=bulk_recv.at[place],
            device_id={"row": chip, "col": home},
            device_id_type=MESH,
        )

    def is_near(chip):
        return jnp.logical_and(chip >= row - reach, chip <= row + reach)

    lower_end = row + jnp.where(home < col, 1, 0)
    higher_begin = row + jnp.where(home > col, 0, 1)

    def for_others(act, begin, end):
        @pl.loop(begin, end)
        def _(chip):
            @pl.when(jnp.logical_not(jnp.logical_and(mine, chip == row)))
            def _():
                act(chip)

    def tell(chip, core, slot):
        pl.semaphore_signal(
            ready.at[slot], inc=1, device_id={"row": chip, "col": core}, device_id_type=MESH
        )

    def tell_lower():
        @pl.loop(0, row // 2 + 1)
        def _(index):
            chip = 2 * index + col
            for core in range(2):

                @pl.when(2 * chip + core < 2 * row + col)
                def _():
                    tell(chip, core, row)

        @pl.when(jnp.logical_and(col == 1, home == 0))
        def _():
            tell(row, 0, n_row)

    def send_higher(chip):
        pl.semaphore_wait(ready.at[chip], 1)
        small_to(chip).start()
        bulk_act("start")(chip)

    def small_act(name):
        return lambda chip: getattr(small_to(chip), name)()

    def bulk_act(name):
        def act(chip):
            near = is_near(chip)

            @pl.when(near)
            def _():
                getattr(bulk_to(chip, 4), name)()

            @pl.when(jnp.logical_not(near))
            def _():
                getattr(bulk_to(chip, 1), name)()

        return act

    def order_of(block, chip):
        offset = jnp.clip(chip - row + reach, 0, 2 * reach)
        return jnp.where(is_near(chip), order_ref[block, offset] * step_nodes, 0)

    def chip_of(pair, slot):
        return 4 * (first_pair + pair) + 2 * slot + col

    def prepare():
        loads[4].wait()
        loads[5].wait()
        loads[7].wait()
        rate = wave_ref[0] * (0.5 / PI)
        origin[0:3] = jnp.broadcast_to(tnode_ref[:, 0:1], (3, LANES))
        cols = columns_of(tnode_ref[...])
        first = cols[0:1]
        cols = (cols - first) * rate
        for block in range(2):
            for axis in range(3):
                tnode_wide[block, axis] = jnp.broadcast_to(
                    cols[block * qn : (block + 1) * qn, axis : axis + 1], (qn, LANES)
                )

        @pl.loop(0, near_pairs)
        def _(pair):
            for block in range(2):
                even, odd = (order_of(block, chip_of(pair, slot)) for slot in range(2))
                middle = jnp.where(lane < tail, even, odd)
                for part, (limit, ahead) in enumerate(
                    (
                        (even, lane),
                        (middle, jnp.where(lane < tail, lane + LANES, lane - tail)),
                        (odd, lane + tail),
                    )
                ):
                    for group in range(ORDERS):
                        live = jnp.logical_and(ahead < limit, limit > group * step_nodes)
                        value = jnp.where(live, rate * (0.25 / PI), 0.0)
                        at = (3 * pair + part) * 2 + block
                        scale_all[at, group] = jnp.broadcast_to(value, (ROWS, LANES))

            for slot in range(2):

                @pl.when(jnp.logical_not(is_near(chip_of(pair, slot))))
                def _():
                    at = pl.ds(pl.multiple_of((3 * pair + 2 * slot) * LANES, LANES), LANES)
                    for block in range(2):
                        green_high[block, :, at] = jnp.zeros((2 * qn, LANES), jnp.bfloat16)
                        green_low[block, :, at] = jnp.zeros((2 * qn, LANES), jnp.bfloat16)

            @pl.when(jnp.logical_not(pair_live(pair)))
            def _():
                at = pl.ds(pl.multiple_of((3 * pair + 1) * LANES, LANES), LANES)
                for block in range(2):
                    green_high[block, :, at] = jnp.zeros((2 * qn, LANES), jnp.bfloat16)
                    green_low[block, :, at] = jnp.zeros((2 * qn, LANES), jnp.bfloat16)

        @pl.when(mine)
        def _():
            own = place - 2 * first_pair
            green_of(3 * (own // 2) + 2 * lax.rem(own, 2), heads_of(snode_ref[...]))

        loads[6].wait()
        cols = columns_of(tgt_ref[...])
        for axis in range(6):
            line = cols[:, axis : axis + 1]
            if axis < 3:
                line = (line - first[:, axis : axis + 1]) * rate
            tgt_wide[axis] = jnp.broadcast_to(line, (2 * blk, LANES))
        loads[8].wait()
        for block in range(2):
            at = slice(block * blk, (block + 1) * blk)
            for part in range(2):
                tests[block, part * blk : (part + 1) * blk] = tweight_ref[part, :, at].T

    def pair_live(pair):
        return jnp.logical_or(is_near(chip_of(pair, 0)), is_near(chip_of(pair, 1)))

    def scaled(places):
        rate = wave_ref[0] * (0.5 / PI)
        return (places - origin[0:3]) * rate, rate * rate * (SOFT * SOFT)

    def green_of(chunk, places):
        places, soft = scaled(places)
        s_x, s_y, s_z = (jnp.broadcast_to(places[i : i + 1], (step_nodes, LANES)) for i in range(3))
        at = pl.ds(pl.multiple_of(chunk * LANES, LANES), LANES)

        @pl.loop(0, 2)
        def _(block):
            for group in range(ORDERS):
                here = slice(group * step_nodes, (group + 1) * step_nodes)
                scale = jnp.broadcast_to(scale_all[chunk * 2 + block, group, 0:1], (step_nodes, LANES))
                d_x = tnode_wide[block, 0, here] - s_x
                d_y = tnode_wide[block, 1, here] - s_y
                d_z = tnode_wide[block, 2, here] - s_z
                squared = d_x * d_x + d_y * d_y + (d_z * d_z + soft)
                inverse, cosine, u, sine = wave_parts(squared)
                inverse = inverse * scale
                for part, value in enumerate((inverse * cosine, (inverse * u) * sine)):
                    high, low = split_two(value)
                    to = slice(part * qn + group * step_nodes, part * qn + (group + 1) * step_nodes)
                    green_high[block, to, at] = high
                    green_low[block, to, at] = low

    @pl.when(2 * row + col > 0)
    def _():
        pl.semaphore_wait(barrier, 2 * row + col)

    tell_lower()
    for_others(small_act("start"), 0, lower_end)
    pack_bulk()
    for_others(bulk_act("start"), 0, lower_end)
    prepare()
    for_others(send_higher, higher_begin, n_row)

    @pl.when(jnp.logical_and(col == 0, home == 0))
    def _():
        pl.semaphore_wait(ready.at[n_row], 1)

    def wait_small(index):
        view = small_all.at[index]
        pltpu.make_async_copy(view, view, small_recv.at[index]).wait()

    def wait_bulk(index):
        near = is_near(2 * index + col)
        for planes, go in ((4, near), (1, jnp.logical_not(near))):

            @pl.when(go)
            def _():
                view = bulk_all.at[index, :, pl.ds(0, planes)]
                pltpu.make_async_copy(view, view, bulk_recv.at[index]).wait()

    @pl.loop(0, near_pairs)
    def _(turn):
        pair = near_pairs - 1 - turn
        base = 2 * (first_pair + pair)

        @pl.loop(0, 2)
        def _(slot):
            slot = 1 - slot
            wait_small(base + slot)
            chip = chip_of(pair, slot)

            @pl.when(jnp.logical_and(is_near(chip), chip != row))
            def _():
                green_of(3 * pair + 2 * slot, small_all[base + slot, 0, 0:3])

        @pl.when(pair_live(pair))
        def _():
            green_of(3 * pair + 1, small_all[base, 1, 0:3] + small_all[base + 1, 1, 0:3])

    def for_rest(act):
        if 2 * near_pairs < chips:

            @pl.loop(0, chips)
            def _(index):
                @pl.when(jnp.logical_or(index < 2 * first_pair, index >= 2 * (first_pair + near_pairs)))
                def _():
                    act(index)

    for_rest(wait_small)

    def impedance_of(chunk):
        packed = small_all[pl.ds(chunk * pieces, pieces), :, 4:8, :].reshape(2 * pieces, 4, LANES)
        packed = jnp.sum(packed, 0)
        places, soft = scaled(packed[0:3])
        area = packed[3:4] * (wave_ref[0] * (0.125 / PI / PI))
        at = pl.ds(pl.multiple_of(chunk * LANES, LANES), LANES)
        for part in range(4):
            block, half = part // 2, part % 2
            count = blk // 2
            here = slice(part * count, (part + 1) * count)
            d_x = tgt_wide[0, here] - places[0:1]
            d_y = tgt_wide[1, here] - places[1:2]
            d_z = tgt_wide[2, here] - places[2:3]
            squared = d_x * d_x + d_y * d_y + (d_z * d_z + soft)
            inverse, cosine, u, sine = wave_parts(squared)
            sine = u * sine
            along = tgt_wide[3, here] * d_x + tgt_wide[4, here] * d_y + tgt_wide[5, here] * d_z
            along = along * inverse
            scale = area * inverse
            green_re = scale * cosine
            green_im = scale * sine
            factor_re = 1.0 - along
            factor_im = along * (inverse * (-0.5 / PI))
            for side, value in enumerate(
                (
                    green_re * factor_re - green_im * factor_im,
                    green_re * factor_im + green_im * factor_re,
                )
            ):
                to = slice(side * blk + half * count, side * blk + (half + 1) * count)
                impedance[block, to, at] = value.astype(jnp.bfloat16)

    @pl.loop(0, chips // pieces)
    def _(chunk):
        impedance_of(chunk)

    @pl.loop(0, near_pairs)
    def _(pair):
        wait_bulk(2 * (first_pair + pair))
        wait_bulk(2 * (first_pair + pair) + 1)

    for slot in range(2 * near_pairs):
        index = 2 * first_pair + slot
        rows = bulk_all[index, :, 0].reshape(2 * per, width)
        weights = jnp.concatenate(
            [bulk_all[index, :, 1 + part].reshape(2 * per, LANES) for part in range(3)], 1
        )
        both = lax.dot_general(weights, rows, TN, preferred_element_type=jnp.float32)
        value = plus_i(both[:qn], both[qn:])
        value = jnp.where(is_near(2 * index + col), value, 0.0)
        high, low = split_two(value)
        at = slice((slot % 2) * qn, (slot % 2 + 1) * qn)
        moment[slot // 2, at, 0:width] = high
        moment[slot // 2, at, width:] = low

    for_rest(wait_bulk)

    def partial(block):
        def far_step(chunk, total):
            rows = bulk_all[pl.ds(chunk * pieces, pieces), :, 0].reshape(LANES, width)
            at = pl.ds(pl.multiple_of(chunk * LANES, LANES), LANES)
            return total + jnp.dot(impedance[block, :, at], rows, preferred_element_type=jnp.float32)

        right = moment[...].reshape(near_pairs * 2 * qn, 2 * width)
        both = jnp.dot(green_high[block], right, preferred_element_type=jnp.float32)
        both = both[:, :width] + both[:, width:]
        both = both + jnp.dot(green_low[block], right[:, :width], preferred_element_type=jnp.float32)
        high, low = split_two(plus_i(both[:qn], both[qn:]))
        product = jnp.dot(tests[block], jnp.concatenate([high, low], 1), preferred_element_type=jnp.float32)
        both = product[:, :width] + product[:, width:]
        if chips == pieces:
            both = far_step(0, both)
        else:
            both = lax.fori_loop(0, chips // pieces, far_step, both)
        return plus_i(both[:blk], both[blk:])

    swap = pltpu.make_async_remote_copy(
        src_ref=part_send,
        dst_ref=part_recv,
        send_sem=part_sem.at[0],
        recv_sem=part_sem.at[1],
        device_id={"col": 1 - col},
        device_id_type=MESH,
    )
    part_send[...] = partial(1 - col)
    swap.start()
    out_ref[...] = partial(col)
    for_others(small_act("wait_send"), 0, n_row)
    for_others(bulk_act("wait_send"), 0, n_row)
    swap.wait_recv()
    out_ref[...] += part_recv[...]
    swap.wait_send()


def on_device(
    wavenumber,
    tgt_geom,
    src_geom,
    excite,
    tgt_nodes,
    src_nodes,
    tgt_weights,
    src_weights,
    near_order,
):
    n_row = lax.axis_size("row")
    chips = n_row // 2
    blk = tgt_geom.shape[1] // 2
    qn = src_nodes.shape[1]
    per, width = src_geom.shape[1], excite.shape[0]
    excite_rows = excite.T
    weight_rows = src_weights.transpose(0, 2, 1)
    reach = (near_order.shape[1] - 1) // 2
    near_pairs = min(reach // 2 + 1, chips // 2)
    depth = near_pairs * 2 * qn
    hbm = pl.BlockSpec(memory_space=pl.ANY)
    dma = pltpu.SemaphoreType.DMA
    f32, bf16 = jnp.float32, jnp.bfloat16
    return pl.pallas_call(
        kernel,
        out_shape=pltpu.VMEM((blk, width), f32),
        in_specs=[hbm] * 9,
        out_specs=pl.BlockSpec(memory_space=pltpu.VMEM),
        scratch_shapes=[
            pltpu.VMEM((chips, 2, ROWS, LANES), f32),
            pltpu.VMEM((chips, 2, 4, per, LANES), bf16),
            pltpu.VMEM((ROWS, LANES), f32),
            pltpu.VMEM((4, per, LANES), bf16),
            pltpu.VMEM((2, 3, qn, LANES), f32),
            pltpu.VMEM((6, 2 * blk, LANES), f32),
            pltpu.VMEM((ROWS, LANES), f32),
            pltpu.VMEM((near_pairs * 6, ORDERS, ROWS, LANES), f32),
            pltpu.VMEM((2, 2 * blk, qn), bf16),
            pltpu.VMEM((2, 2 * qn, depth), bf16),
            pltpu.VMEM((2, 2 * qn, depth), bf16),
            pltpu.VMEM((near_pairs, 2 * qn, 2 * width), bf16),
            pltpu.VMEM((2, 2 * blk, chips * 2 * per), bf16),
            pltpu.VMEM((blk, width), f32),
            pltpu.VMEM((blk, width), f32),
            pltpu.SMEM(wavenumber.shape, f32),
            pltpu.SMEM(near_order.shape, jnp.int32),
            pltpu.VMEM(tgt_geom.shape, f32),
            pltpu.VMEM(tgt_nodes.shape, f32),
            pltpu.VMEM(tgt_weights.shape, bf16),
            pltpu.VMEM(src_geom.shape, f32),
            pltpu.VMEM(excite_rows.shape, bf16),
            pltpu.VMEM(src_nodes.shape, f32),
            pltpu.VMEM(weight_rows.shape, bf16),
            dma((9,)),
            dma((n_row,)),
            dma((n_row,)),
            dma((chips,)),
            dma((chips,)),
            dma((2,)),
            pltpu.SemaphoreType.REGULAR((n_row + 1,)),
        ],
        compiler_params=pltpu.CompilerParams(collective_id=0, has_side_effects=True),
        name="slab",
    )(
        wavenumber,
        near_order,
        tgt_geom,
        tgt_nodes,
        tgt_weights,
        src_geom,
        excite_rows,
        src_nodes,
        weight_rows,
    )


def solution(mesh):
    return jax.shard_map(
        on_device,
        mesh=mesh,
        in_specs=(
            P("groups"),
            P(None, ("groups", "row")),
            P(None, ("groups", "row", "col")),
            P(None, ("groups", "row", "col")),
            P(None, ("groups", "row")),
            P(None, ("groups", "row")),
            P(None, None, ("groups", "row")),
            P(None, None, ("groups", "row", "col")),
            P(("groups", "row"), None),
        ),
        out_specs=P(("groups", "row", "col"), None),
        check_vma=False,
    )
```

```python
import math

import jax
import jax.numpy as jnp
import numpy as np
from jax import lax
from jax.experimental import pallas as pl
from jax.experimental.pallas import tpu as pltpu
from jax.sharding import PartitionSpec as P

ORDERS = 3
SOFT = 0.05
PI = math.pi
LANES = 128
ROWS = 8
MESH = pl.DeviceIdType.MESH
TN = (((0,), (0,)), ((), ()))


def fitted(function, terms):
    nodes = (np.cos((np.arange(terms) + 0.5) * np.pi / terms) + 1.0) / 8.0
    matrix = np.vander(nodes, terms, increasing=True)
    return [float(c) for c in np.linalg.solve(matrix, function(np.sqrt(nodes)))]


COS = fitted(lambda u: np.cos(2.0 * np.pi * u), 6)
SIN = fitted(lambda u: np.sin(2.0 * np.pi * u) / u, 6)


def horner(coefficients, y):
    total = coefficients[-1]
    for c in coefficients[-2::-1]:
        total = total * y + c
    return total


def wave_parts(squared):
    inverse = lax.rsqrt(squared)
    turns = squared * inverse
    u = turns - jnp.round(turns)
    y = u * u
    return inverse, horner(COS, y), u, horner(SIN, y)


def plus_i(first, second):
    half = second.shape[1] // 2
    swapped = pltpu.roll(second, half, 1)
    lane = lax.broadcasted_iota(jnp.int32, second.shape, 1)
    return first + jnp.where(lane < half, -swapped, swapped)


def split_two(value):
    high = value.astype(jnp.bfloat16)
    return high, (value - high.astype(jnp.float32)).astype(jnp.bfloat16)


def columns_of(rows):
    few, lanes = rows.shape
    pad = jnp.zeros((ROWS - few, lanes), jnp.float32)
    return jnp.concatenate([rows, pad], 0).T


def kernel(
    wave_hbm,
    order_hbm,
    tgt_hbm,
    tnode_hbm,
    tweight_hbm,
    geom_hbm,
    excite_hbm,
    snode_hbm,
    sweight_hbm,
    out_ref,
    small_all,
    bulk_all,
    far_all,
    middle,
    small_pack,
    bulk_pack,
    tnode_wide,
    tgt_wide,
    origin,
    scale_all,
    tests,
    green_high,
    green_low,
    moment,
    impedance,
    part_send,
    part_recv,
    wave_ref,
    order_ref,
    tgt_ref,
    tnode_ref,
    tweight_ref,
    geom_ref,
    excite_ref,
    snode_ref,
    sweight_ref,
    local,
    small_send,
    bulk_send,
    small_recv,
    bulk_recv,
    part_sem,
    ready,
):
    n_row = lax.axis_size("row")
    row = lax.axis_index("row")
    col = lax.axis_index("col")
    home = lax.rem(row, 2)
    place = row // 2
    chips = n_row // 2
    reach = (order_hbm.shape[1] - 1) // 2
    qn = snode_hbm.shape[1]
    tail = qn - LANES
    step_nodes = qn // ORDERS
    per = excite_hbm.shape[0]
    blk, width = out_ref.shape
    near_pairs = moment.shape[0]
    first_pair = jnp.clip(
        (row - reach - col + 1 + 4 * reach) // 4 - reach, 0, chips // 2 - near_pairs
    )
    mine = home == col
    lane = lax.broadcasted_iota(jnp.int32, (1, LANES), 1)

    loads = [
        pltpu.make_async_copy(here, there, local.at[index])
        for index, (here, there) in enumerate(
            (
                (snode_hbm, snode_ref),
                (geom_hbm, geom_ref),
                (excite_hbm, excite_ref),
                (sweight_hbm, sweight_ref),
                (wave_hbm, wave_ref),
                (tnode_hbm, tnode_ref),
                (tgt_hbm, tgt_ref),
                (order_hbm, order_ref),
                (tweight_hbm, tweight_ref),
            )
        )
    ]
    for load in loads:
        load.start()

    barrier = pltpu.get_barrier_semaphore()

    @pl.loop(2 * row + col + 1, 2 * n_row)
    def _(index):
        pl.semaphore_signal(
            barrier,
            inc=1,
            device_id={"row": index // 2, "col": lax.rem(index, 2)},
            device_id_type=MESH,
        )

    def heads_of(nodes):
        return jnp.where(lax.rem(place, 2) == 0, nodes[:, :LANES], nodes[:, tail:])

    loads[0].wait()
    nodes = snode_ref[...]
    gap = jnp.zeros((nodes.shape[0], LANES - tail), jnp.float32)
    ends = jnp.where(
        lax.rem(place, 2) == 0,
        jnp.concatenate([nodes[:, LANES:], gap], 1),
        jnp.concatenate([gap, nodes[:, :tail]], 1),
    )
    small_pack[0:3, :] = jnp.where(col == 0, heads_of(nodes), ends)
    loads[1].wait()
    pieces = LANES // (2 * per)
    spread = jnp.concatenate([geom_ref[...]] * (LANES // per), 1)
    begin = (2 * lax.rem(place, pieces) + col) * per
    inside = jnp.logical_and(lane >= begin, lane < begin + per)
    small_pack[3:4, :] = jnp.zeros((1, LANES), jnp.float32)
    small_pack[4:8, :] = jnp.where(inside, spread, 0.0)

    @pl.when(mine)
    def _():
        pltpu.make_async_copy(small_pack, small_all.at[place, col], small_recv.at[place]).start()

    def pack_bulk():
        loads[2].wait()
        bulk_pack[0] = excite_ref[...]
        loads[3].wait()
        bulk_pack[1] = sweight_ref[0, :, :LANES]
        bulk_pack[2] = jnp.concatenate(
            [sweight_ref[0, :, LANES:].astype(jnp.float32), sweight_ref[1, :, :tail].astype(jnp.float32)], 1
        ).astype(jnp.bfloat16)
        bulk_pack[3] = sweight_ref[1, :, tail:]

        @pl.when(mine)
        def _():
            pltpu.make_async_copy(bulk_pack, bulk_all.at[place, col], bulk_recv.at[place]).start()

    def small_to(chip):
        return pltpu.make_async_remote_copy(
            src_ref=small_pack,
            dst_ref=small_all.at[place, col],
            send_sem=small_send.at[chip],
            recv_sem=small_recv.at[place],
            device_id={"row": chip, "col": home},
            device_id_type=MESH,
        )

    def bulk_to(chip, near):
        return pltpu.make_async_remote_copy(
            src_ref=bulk_pack if near else bulk_pack.at[0],
            dst_ref=bulk_all.at[place, col] if near else far_all.at[place, col],
            send_sem=bulk_send.at[chip],
            recv_sem=bulk_recv.at[place],
            device_id={"row": chip, "col": home},
            device_id_type=MESH,
        )

    def is_near(chip):
        return jnp.logical_and(chip >= row - reach, chip <= row + reach)

    lower_end = row + jnp.where(home < col, 1, 0)
    higher_begin = row + jnp.where(home > col, 0, 1)

    def for_others(act, begin, end):
        @pl.loop(begin, end)
        def _(chip):
            @pl.when(jnp.logical_not(jnp.logical_and(mine, chip == row)))
            def _():
                act(chip)

    def tell(chip, core, slot):
        pl.semaphore_signal(
            ready.at[slot], inc=1, device_id={"row": chip, "col": core}, device_id_type=MESH
        )

    def tell_lower():
        @pl.loop(0, row // 2 + 1)
        def _(index):
            chip = 2 * index + col
            for core in range(2):

                @pl.when(2 * chip + core < 2 * row + col)
                def _():
                    tell(chip, core, row)

        @pl.when(jnp.logical_and(col == 1, home == 0))
        def _():
            tell(row, 0, n_row)

    def send_higher(chip):
        pl.semaphore_wait(ready.at[chip], 1)
        small_to(chip).start()
        bulk_act("start")(chip)

    def small_act(name):
        return lambda chip: getattr(small_to(chip), name)()

    def bulk_act(name):
        def act(chip):
            near = is_near(chip)

            @pl.when(near)
            def _():
                getattr(bulk_to(chip, True), name)()

            @pl.when(jnp.logical_not(near))
            def _():
                getattr(bulk_to(chip, False), name)()

        return act

    def order_of(block, chip):
        offset = jnp.clip(chip - row + reach, 0, 2 * reach)
        return jnp.where(is_near(chip), order_ref[block, offset] * step_nodes, 0)

    def chip_of(pair, slot):
        return 4 * (first_pair + pair) + 2 * slot + col

    def prepare():
        loads[4].wait()
        loads[5].wait()
        loads[7].wait()
        rate = wave_ref[0] * (0.5 / PI)
        origin[0:3] = jnp.broadcast_to(tnode_ref[:, 0:1], (3, LANES))
        cols = columns_of(tnode_ref[...])
        first = cols[0:1]
        cols = (cols - first) * rate
        for block in range(2):
            for axis in range(3):
                tnode_wide[block, axis] = jnp.broadcast_to(
                    cols[block * qn : (block + 1) * qn, axis : axis + 1], (qn, LANES)
                )

        @pl.loop(0, near_pairs)
        def _(pair):
            for block in range(2):
                even, odd = (order_of(block, chip_of(pair, slot)) for slot in range(2))
                middle = jnp.where(lane < tail, even, odd)
                for part, (limit, ahead) in enumerate(
                    (
                        (even, lane),
                        (middle, jnp.where(lane < tail, lane + LANES, lane - tail)),
                        (odd, lane + tail),
                    )
                ):
                    for group in range(ORDERS):
                        live = jnp.logical_and(ahead < limit, limit > group * step_nodes)
                        value = jnp.where(live, rate * (0.25 / PI), 0.0)
                        at = (3 * pair + part) * 2 + block
                        scale_all[at, group] = jnp.broadcast_to(value, (ROWS, LANES))

            for slot in range(2):

                @pl.when(jnp.logical_not(is_near(chip_of(pair, slot))))
                def _():
                    at = pl.ds(pl.multiple_of((3 * pair + 2 * slot) * LANES, LANES), LANES)
                    for block in range(2):
                        green_high[block, :, at] = jnp.zeros((2 * qn, LANES), jnp.bfloat16)
                        green_low[block, :, at] = jnp.zeros((2 * qn, LANES), jnp.bfloat16)

            @pl.when(jnp.logical_not(pair_live(pair)))
            def _():
                at = pl.ds(pl.multiple_of((3 * pair + 1) * LANES, LANES), LANES)
                for block in range(2):
                    green_high[block, :, at] = jnp.zeros((2 * qn, LANES), jnp.bfloat16)
                    green_low[block, :, at] = jnp.zeros((2 * qn, LANES), jnp.bfloat16)

        @pl.when(mine)
        def _():
            own = place - 2 * first_pair
            green_of(3 * (own // 2) + 2 * lax.rem(own, 2), heads_of(snode_ref[...]))

        loads[6].wait()
        cols = columns_of(tgt_ref[...])
        for axis in range(6):
            line = cols[:, axis : axis + 1]
            if axis < 3:
                line = (line - first[:, axis : axis + 1]) * rate
            tgt_wide[axis] = jnp.broadcast_to(line, (2 * blk, LANES))
        loads[8].wait()
        for block in range(2):
            at = slice(block * blk, (block + 1) * blk)
            for part in range(2):
                tests[block, part * blk : (part + 1) * blk] = tweight_ref[part, :, at].T

    def pair_live(pair):
        return jnp.logical_or(is_near(chip_of(pair, 0)), is_near(chip_of(pair, 1)))

    def scaled(places):
        rate = wave_ref[0] * (0.5 / PI)
        return (places - origin[0:3]) * rate, rate * rate * (SOFT * SOFT)

    def green_of(chunk, places):
        places, soft = scaled(places)
        s_x, s_y, s_z = (jnp.broadcast_to(places[i : i + 1], (step_nodes, LANES)) for i in range(3))
        at = pl.ds(pl.multiple_of(chunk * LANES, LANES), LANES)

        @pl.loop(0, 2)
        def _(block):
            for group in range(ORDERS):
                here = slice(group * step_nodes, (group + 1) * step_nodes)
                scale = jnp.broadcast_to(scale_all[chunk * 2 + block, group, 0:1], (step_nodes, LANES))
                d_x = tnode_wide[block, 0, here] - s_x
                d_y = tnode_wide[block, 1, here] - s_y
                d_z = tnode_wide[block, 2, here] - s_z
                squared = d_x * d_x + d_y * d_y + (d_z * d_z + soft)
                inverse, cosine, u, sine = wave_parts(squared)
                inverse = inverse * scale
                for part, value in enumerate((inverse * cosine, (inverse * u) * sine)):
                    high, low = split_two(value)
                    to = slice(part * qn + group * step_nodes, part * qn + (group + 1) * step_nodes)
                    green_high[block, to, at] = high
                    green_low[block, to, at] = low

    @pl.when(2 * row + col > 0)
    def _():
        pl.semaphore_wait(barrier, 2 * row + col)

    tell_lower()
    for_others(small_act("start"), 0, lower_end)
    pack_bulk()
    for_others(bulk_act("start"), 0, lower_end)
    prepare()
    for_others(send_higher, higher_begin, n_row)

    @pl.when(jnp.logical_and(col == 0, home == 0))
    def _():
        pl.semaphore_wait(ready.at[n_row], 1)

    def wait_small(index):
        view = small_all.at[index]
        pltpu.make_async_copy(view, view, small_recv.at[index]).wait()

    def wait_bulk(index):
        near = is_near(2 * index + col)
        for view, go in ((bulk_all.at[index], near), (far_all.at[index], jnp.logical_not(near))):

            @pl.when(go)
            def _():
                pltpu.make_async_copy(view, view, bulk_recv.at[index]).wait()

    def inward(index, count):
        return jnp.where(row < chips, index, count - 1 - index)

    @pl.loop(0, near_pairs)
    def _(turn):
        pair = inward(turn, near_pairs)
        base = 2 * (first_pair + pair)
        middle[0:3] = jnp.zeros((3, LANES), jnp.float32)

        @pl.loop(0, 2)
        def _(slot):
            slot = inward(slot, 2)
            chip = chip_of(pair, slot)

            @pl.when(is_near(chip))
            def _():
                wait_small(base + slot)
                middle[0:3] += small_all[base + slot, 1, 0:3]

            @pl.when(jnp.logical_and(is_near(chip), chip != row))
            def _():
                green_of(3 * pair + 2 * slot, small_all[base + slot, 0, 0:3])

        @pl.when(pair_live(pair))
        def _():
            green_of(3 * pair + 1, middle[0:3])

    def for_chips(act, near):
        @pl.loop(0, chips)
        def _(index):
            go = is_near(2 * index + col)

            @pl.when(go if near else jnp.logical_not(go))
            def _():
                act(index)

    def impedance_of(chunk):
        packed = small_all[pl.ds(chunk * pieces, pieces), :, 4:8, :].reshape(2 * pieces, 4, LANES)
        packed = jnp.sum(packed, 0)
        places, soft = scaled(packed[0:3])
        area = packed[3:4] * (wave_ref[0] * (0.125 / PI / PI))
        at = pl.ds(pl.multiple_of(chunk * LANES, LANES), LANES)
        for part in range(4):
            block, half = part // 2, part % 2
            count = blk // 2
            here = slice(part * count, (part + 1) * count)
            d_x = tgt_wide[0, here] - places[0:1]
            d_y = tgt_wide[1, here] - places[1:2]
            d_z = tgt_wide[2, here] - places[2:3]
            squared = d_x * d_x + d_y * d_y + (d_z * d_z + soft)
            inverse, cosine, u, sine = wave_parts(squared)
            sine = u * sine
            along = tgt_wide[3, here] * d_x + tgt_wide[4, here] * d_y + tgt_wide[5, here] * d_z
            along = along * inverse
            scale = area * inverse
            green_re = scale * cosine
            green_im = scale * sine
            factor_re = 1.0 - along
            factor_im = along * (inverse * (-0.5 / PI))
            for side, value in enumerate(
                (
                    green_re * factor_re - green_im * factor_im,
                    green_re * factor_im + green_im * factor_re,
                )
            ):
                to = slice(side * blk + half * count, side * blk + (half + 1) * count)
                impedance[block, to, at] = value.astype(jnp.bfloat16)

    for_chips(wait_bulk, True)

    for slot in range(2 * near_pairs):
        index = 2 * first_pair + slot
        rows = bulk_all[index, :, 0].reshape(2 * per, width)
        weights = jnp.concatenate(
            [bulk_all[index, :, 1 + part].reshape(2 * per, LANES) for part in range(3)], 1
        )
        both = lax.dot_general(weights, rows, TN, preferred_element_type=jnp.float32)
        value = plus_i(both[:qn], both[qn:])
        value = jnp.where(is_near(2 * index + col), value, 0.0)
        high, low = split_two(value)
        at = slice((slot % 2) * qn, (slot % 2 + 1) * qn)
        moment[slot // 2, at, 0:width] = high
        moment[slot // 2, at, width:] = low

    def near_part(block):
        right = moment[...].reshape(near_pairs * 2 * qn, 2 * width)
        both = jnp.dot(green_high[block], right, preferred_element_type=jnp.float32)
        both = both[:, :width] + both[:, width:]
        both = both + jnp.dot(green_low[block], right[:, :width], preferred_element_type=jnp.float32)
        high, low = split_two(plus_i(both[:qn], both[qn:]))
        product = jnp.dot(tests[block], jnp.concatenate([high, low], 1), preferred_element_type=jnp.float32)
        return product[:, :width] + product[:, width:]

    def far_part(block, both):
        def far_step(chunk, total):
            rows = []
            for piece in range(pieces):
                index = chunk * pieces + piece
                rows.append(
                    jnp.where(is_near(2 * index + col), bulk_all[index, :, 0], far_all[index]).reshape(
                        2 * per, width
                    )
                )
            at = pl.ds(pl.multiple_of(chunk * LANES, LANES), LANES)
            return total + jnp.dot(
                impedance[block, :, at], jnp.concatenate(rows, 0), preferred_element_type=jnp.float32
            )

        if chips == pieces:
            both = far_step(0, both)
        else:
            both = lax.fori_loop(0, chips // pieces, far_step, both)
        return plus_i(both[:blk], both[blk:])

    swap = pltpu.make_async_remote_copy(
        src_ref=part_send,
        dst_ref=part_recv,
        send_sem=part_sem.at[0],
        recv_sem=part_sem.at[1],
        device_id={"col": 1 - col},
        device_id_type=MESH,
    )
    other = near_part(1 - col)
    for_chips(wait_small, False)
    for_chips(wait_bulk, False)

    @pl.loop(0, chips // pieces)
    def _(chunk):
        impedance_of(chunk)

    part_send[...] = far_part(1 - col, other)
    swap.start()
    out_ref[...] = far_part(col, near_part(col))
    for_others(small_act("wait_send"), 0, n_row)
    for_others(bulk_act("wait_send"), 0, n_row)
    swap.wait_recv()
    out_ref[...] += part_recv[...]
    swap.wait_send()


def on_device(
    wavenumber,
    tgt_geom,
    src_geom,
    excite,
    tgt_nodes,
    src_nodes,
    tgt_weights,
    src_weights,
    near_order,
):
    n_row = lax.axis_size("row")
    chips = n_row // 2
    blk = tgt_geom.shape[1] // 2
    qn = src_nodes.shape[1]
    per, width = src_geom.shape[1], excite.shape[0]
    excite_rows = excite.T
    weight_rows = src_weights.transpose(0, 2, 1)
    reach = (near_order.shape[1] - 1) // 2
    near_pairs = min(reach // 2 + 1, chips // 2)
    depth = near_pairs * 2 * qn
    hbm = pl.BlockSpec(memory_space=pl.ANY)
    dma = pltpu.SemaphoreType.DMA
    f32, bf16 = jnp.float32, jnp.bfloat16
    return pl.pallas_call(
        kernel,
        out_shape=pltpu.VMEM((blk, width), f32),
        in_specs=[hbm] * 9,
        out_specs=pl.BlockSpec(memory_space=pltpu.VMEM),
        scratch_shapes=[
            pltpu.VMEM((chips, 2, ROWS, LANES), f32),
            pltpu.VMEM((chips, 2, 4, per, LANES), bf16),
            pltpu.VMEM((chips, 2, per, LANES), bf16),
            pltpu.VMEM((ROWS, LANES), f32),
            pltpu.VMEM((ROWS, LANES), f32),
            pltpu.VMEM((4, per, LANES), bf16),
            pltpu.VMEM((2, 3, qn, LANES), f32),
            pltpu.VMEM((6, 2 * blk, LANES), f32),
            pltpu.VMEM((ROWS, LANES), f32),
            pltpu.VMEM((near_pairs * 6, ORDERS, ROWS, LANES), f32),
            pltpu.VMEM((2, 2 * blk, qn), bf16),
            pltpu.VMEM((2, 2 * qn, depth), bf16),
            pltpu.VMEM((2, 2 * qn, depth), bf16),
            pltpu.VMEM((near_pairs, 2 * qn, 2 * width), bf16),
            pltpu.VMEM((2, 2 * blk, chips * 2 * per), bf16),
            pltpu.VMEM((blk, width), f32),
            pltpu.VMEM((blk, width), f32),
            pltpu.SMEM(wavenumber.shape, f32),
            pltpu.SMEM(near_order.shape, jnp.int32),
            pltpu.VMEM(tgt_geom.shape, f32),
            pltpu.VMEM(tgt_nodes.shape, f32),
            pltpu.VMEM(tgt_weights.shape, bf16),
            pltpu.VMEM(src_geom.shape, f32),
            pltpu.VMEM(excite_rows.shape, bf16),
            pltpu.VMEM(src_nodes.shape, f32),
            pltpu.VMEM(weight_rows.shape, bf16),
            dma((9,)),
            dma((n_row,)),
            dma((n_row,)),
            dma((chips,)),
            dma((chips,)),
            dma((2,)),
            pltpu.SemaphoreType.REGULAR((n_row + 1,)),
        ],
        compiler_params=pltpu.CompilerParams(collective_id=0, has_side_effects=True),
        name="slab",
    )(
        wavenumber,
        near_order,
        tgt_geom,
        tgt_nodes,
        tgt_weights,
        src_geom,
        excite_rows,
        src_nodes,
        weight_rows,
    )


def solution(mesh):
    return jax.shard_map(
        on_device,
        mesh=mesh,
        in_specs=(
            P("groups"),
            P(None, ("groups", "row")),
            P(None, ("groups", "row", "col")),
            P(None, ("groups", "row", "col")),
            P(None, ("groups", "row")),
            P(None, ("groups", "row")),
            P(None, None, ("groups", "row")),
            P(None, None, ("groups", "row", "col")),
            P(("groups", "row"), None),
        ),
        out_specs=P(("groups", "row", "col"), None),
        check_vma=False,
    )
```

```python
import math

import jax
import jax.numpy as jnp
import numpy as np
from jax import lax
from jax.experimental import pallas as pl
from jax.experimental.pallas import tpu as pltpu
from jax.sharding import PartitionSpec as P

ORDERS = 3
SOFT = 0.05
PI = math.pi
LANES = 128
ROWS = 8
MESH = pl.DeviceIdType.MESH
TN = (((0,), (0,)), ((), ()))


def fitted(function, terms):
    nodes = (np.cos((np.arange(terms) + 0.5) * np.pi / terms) + 1.0) / 8.0
    matrix = np.vander(nodes, terms, increasing=True)
    return [float(c) for c in np.linalg.solve(matrix, function(np.sqrt(nodes)))]


COS = fitted(lambda u: np.cos(2.0 * np.pi * u), 6)
SIN = fitted(lambda u: np.sin(2.0 * np.pi * u) / u, 6)


def horner(coefficients, y):
    total = coefficients[-1]
    for c in coefficients[-2::-1]:
        total = total * y + c
    return total


def wave_parts(squared):
    inverse = lax.rsqrt(squared)
    turns = squared * inverse
    u = turns - jnp.round(turns)
    y = u * u
    return inverse, horner(COS, y), u, horner(SIN, y)


def plus_i(first, second):
    half = second.shape[1] // 2
    swapped = pltpu.roll(second, half, 1)
    lane = lax.broadcasted_iota(jnp.int32, second.shape, 1)
    return first + jnp.where(lane < half, -swapped, swapped)


def split_two(value):
    high = value.astype(jnp.bfloat16)
    return high, (value - high.astype(jnp.float32)).astype(jnp.bfloat16)


def columns_of(rows):
    few, lanes = rows.shape
    pad = jnp.zeros((ROWS - few, lanes), jnp.float32)
    return jnp.concatenate([rows, pad], 0).T


def kernel(
    wave_hbm,
    order_hbm,
    tgt_hbm,
    tnode_hbm,
    tweight_hbm,
    geom_hbm,
    excite_hbm,
    snode_hbm,
    sweight_hbm,
    out_ref,
    small_all,
    bulk_all,
    far_all,
    middle,
    small_pack,
    bulk_pack,
    tnode_wide,
    tgt_wide,
    origin,
    scale_all,
    tests,
    green_high,
    green_low,
    moment,
    impedance,
    part_send,
    part_recv,
    wave_ref,
    order_ref,
    tgt_ref,
    tnode_ref,
    tweight_ref,
    geom_ref,
    excite_ref,
    snode_ref,
    sweight_ref,
    local,
    small_send,
    bulk_send,
    small_recv,
    bulk_recv,
    part_sem,
    ready,
):
    n_row = lax.axis_size("row")
    row = lax.axis_index("row")
    col = lax.axis_index("col")
    home = lax.rem(row, 2)
    place = row // 2
    chips = n_row // 2
    reach = (order_hbm.shape[1] - 1) // 2
    qn = snode_hbm.shape[1]
    tail = qn - LANES
    step_nodes = qn // ORDERS
    per = excite_hbm.shape[0]
    blk, width = out_ref.shape
    near_pairs = moment.shape[0]
    first_pair = jnp.clip(
        (row - reach - col + 1 + 4 * reach) // 4 - reach, 0, chips // 2 - near_pairs
    )
    mine = home == col
    lane = lax.broadcasted_iota(jnp.int32, (1, LANES), 1)

    loads = [
        pltpu.make_async_copy(here, there, local.at[index])
        for index, (here, there) in enumerate(
            (
                (snode_hbm, snode_ref),
                (geom_hbm, geom_ref),
                (excite_hbm, excite_ref),
                (sweight_hbm, sweight_ref),
                (wave_hbm, wave_ref),
                (tnode_hbm, tnode_ref),
                (tgt_hbm, tgt_ref),
                (order_hbm, order_ref),
                (tweight_hbm, tweight_ref),
            )
        )
    ]
    for load in loads:
        load.start()

    barrier = pltpu.get_barrier_semaphore()

    @pl.loop(2 * row + col + 1, 2 * n_row)
    def _(index):
        pl.semaphore_signal(
            barrier,
            inc=1,
            device_id={"row": index // 2, "col": lax.rem(index, 2)},
            device_id_type=MESH,
        )

    def heads_of(nodes):
        return jnp.where(lax.rem(place, 2) == 0, nodes[:, :LANES], nodes[:, tail:])

    loads[0].wait()
    nodes = snode_ref[...]
    gap = jnp.zeros((nodes.shape[0], LANES - tail), jnp.float32)
    ends = jnp.where(
        lax.rem(place, 2) == 0,
        jnp.concatenate([nodes[:, LANES:], gap], 1),
        jnp.concatenate([gap, nodes[:, :tail]], 1),
    )
    small_pack[0:3, :] = jnp.where(col == 0, heads_of(nodes), ends)
    loads[1].wait()
    pieces = LANES // (2 * per)
    spread = jnp.concatenate([geom_ref[...]] * (LANES // per), 1)
    begin = (2 * lax.rem(place, pieces) + col) * per
    inside = jnp.logical_and(lane >= begin, lane < begin + per)
    small_pack[3:4, :] = jnp.zeros((1, LANES), jnp.float32)
    small_pack[4:8, :] = jnp.where(inside, spread, 0.0)

    @pl.when(mine)
    def _():
        pltpu.make_async_copy(small_pack, small_all.at[place, col], small_recv.at[place]).start()

    def pack_bulk():
        loads[2].wait()
        bulk_pack[0] = excite_ref[...]
        loads[3].wait()
        bulk_pack[1] = sweight_ref[0, :, :LANES]
        bulk_pack[2] = jnp.concatenate(
            [sweight_ref[0, :, LANES:].astype(jnp.float32), sweight_ref[1, :, :tail].astype(jnp.float32)], 1
        ).astype(jnp.bfloat16)
        bulk_pack[3] = sweight_ref[1, :, tail:]

        @pl.when(mine)
        def _():
            pltpu.make_async_copy(bulk_pack, bulk_all.at[place, col], bulk_recv.at[place]).start()

    def small_to(chip):
        return pltpu.make_async_remote_copy(
            src_ref=small_pack,
            dst_ref=small_all.at[place, col],
            send_sem=small_send.at[chip],
            recv_sem=small_recv.at[place],
            device_id={"row": chip, "col": home},
            device_id_type=MESH,
        )

    def bulk_to(chip, near):
        return pltpu.make_async_remote_copy(
            src_ref=bulk_pack if near else bulk_pack.at[0],
            dst_ref=bulk_all.at[place, col] if near else far_all.at[place, col],
            send_sem=bulk_send.at[chip],
            recv_sem=bulk_recv.at[place],
            device_id={"row": chip, "col": home},
            device_id_type=MESH,
        )

    def is_near(chip):
        return jnp.logical_and(chip >= row - reach, chip <= row + reach)

    lower_end = row + jnp.where(home < col, 1, 0)
    higher_begin = row + jnp.where(home > col, 0, 1)

    def for_others(act, begin, end):
        @pl.loop(begin, end)
        def _(chip):
            @pl.when(jnp.logical_not(jnp.logical_and(mine, chip == row)))
            def _():
                act(chip)

    def tell(chip, core, slot):
        pl.semaphore_signal(
            ready.at[slot], inc=1, device_id={"row": chip, "col": core}, device_id_type=MESH
        )

    def tell_lower():
        @pl.loop(0, row // 2 + 1)
        def _(index):
            chip = 2 * index + col
            for core in range(2):

                @pl.when(2 * chip + core < 2 * row + col)
                def _():
                    tell(chip, core, row)

        @pl.when(jnp.logical_and(col == 1, home == 0))
        def _():
            tell(row, 0, n_row)

    def send_higher(chip):
        pl.semaphore_wait(ready.at[chip], 1)
        small_to(chip).start()
        bulk_act("start")(chip)

    def small_act(name):
        return lambda chip: getattr(small_to(chip), name)()

    def bulk_act(name):
        def act(chip):
            near = is_near(chip)

            @pl.when(near)
            def _():
                getattr(bulk_to(chip, True), name)()

            @pl.when(jnp.logical_not(near))
            def _():
                getattr(bulk_to(chip, False), name)()

        return act

    def order_of(block, chip):
        offset = jnp.clip(chip - row + reach, 0, 2 * reach)
        return jnp.where(is_near(chip), order_ref[block, offset] * step_nodes, 0)

    def chip_of(pair, slot):
        return 4 * (first_pair + pair) + 2 * slot + col

    def prepare():
        loads[4].wait()
        loads[5].wait()
        loads[7].wait()
        rate = wave_ref[0] * (0.5 / PI)
        origin[0:3] = jnp.broadcast_to(tnode_ref[:, 0:1], (3, LANES))
        cols = columns_of(tnode_ref[...])
        first = cols[0:1]
        cols = (cols - first) * rate
        for block in range(2):
            for axis in range(3):
                tnode_wide[block, axis] = jnp.broadcast_to(
                    cols[block * qn : (block + 1) * qn, axis : axis + 1], (qn, LANES)
                )

        @pl.loop(0, near_pairs)
        def _(pair):
            for block in range(2):
                even, odd = (order_of(block, chip_of(pair, slot)) for slot in range(2))
                middle = jnp.where(lane < tail, even, odd)
                for part, (limit, ahead) in enumerate(
                    (
                        (even, lane),
                        (middle, jnp.where(lane < tail, lane + LANES, lane - tail)),
                        (odd, lane + tail),
                    )
                ):
                    for group in range(ORDERS):
                        live = jnp.logical_and(ahead < limit, limit > group * step_nodes)
                        value = jnp.where(live, rate * (0.25 / PI), 0.0)
                        at = (3 * pair + part) * 2 + block
                        scale_all[at, group] = jnp.broadcast_to(value, (ROWS, LANES))

            for slot in range(2):

                @pl.when(jnp.logical_not(is_near(chip_of(pair, slot))))
                def _():
                    at = pl.ds(pl.multiple_of((3 * pair + 2 * slot) * LANES, LANES), LANES)
                    for block in range(2):
                        green_high[block, :, at] = jnp.zeros((2 * qn, LANES), jnp.bfloat16)
                        green_low[block, :, at] = jnp.zeros((2 * qn, LANES), jnp.bfloat16)

            @pl.when(jnp.logical_not(pair_live(pair)))
            def _():
                at = pl.ds(pl.multiple_of((3 * pair + 1) * LANES, LANES), LANES)
                for block in range(2):
                    green_high[block, :, at] = jnp.zeros((2 * qn, LANES), jnp.bfloat16)
                    green_low[block, :, at] = jnp.zeros((2 * qn, LANES), jnp.bfloat16)

        @pl.when(mine)
        def _():
            own = place - 2 * first_pair
            green_of(3 * (own // 2) + 2 * lax.rem(own, 2), heads_of(snode_ref[...]))

        loads[6].wait()
        cols = columns_of(tgt_ref[...])
        for axis in range(6):
            line = cols[:, axis : axis + 1]
            if axis < 3:
                line = (line - first[:, axis : axis + 1]) * rate
            tgt_wide[axis] = jnp.broadcast_to(line, (2 * blk, LANES))
        loads[8].wait()
        for block in range(2):
            at = slice(block * blk, (block + 1) * blk)
            for part in range(2):
                tests[block, part * blk : (part + 1) * blk] = tweight_ref[part, :, at].T

    def pair_live(pair):
        return jnp.logical_or(is_near(chip_of(pair, 0)), is_near(chip_of(pair, 1)))

    def scaled(places):
        rate = wave_ref[0] * (0.5 / PI)
        return (places - origin[0:3]) * rate, rate * rate * (SOFT * SOFT)

    def green_of(chunk, places):
        places, soft = scaled(places)
        s_x, s_y, s_z = (jnp.broadcast_to(places[i : i + 1], (step_nodes, LANES)) for i in range(3))
        at = pl.ds(pl.multiple_of(chunk * LANES, LANES), LANES)

        @pl.loop(0, 2)
        def _(block):
            for group in range(ORDERS):
                here = slice(group * step_nodes, (group + 1) * step_nodes)
                scale = jnp.broadcast_to(scale_all[chunk * 2 + block, group, 0:1], (step_nodes, LANES))
                d_x = tnode_wide[block, 0, here] - s_x
                d_y = tnode_wide[block, 1, here] - s_y
                d_z = tnode_wide[block, 2, here] - s_z
                squared = d_x * d_x + d_y * d_y + (d_z * d_z + soft)
                inverse, cosine, u, sine = wave_parts(squared)
                inverse = inverse * scale
                for part, value in enumerate((inverse * cosine, (inverse * u) * sine)):
                    high, low = split_two(value)
                    to = slice(part * qn + group * step_nodes, part * qn + (group + 1) * step_nodes)
                    green_high[block, to, at] = high
                    green_low[block, to, at] = low

    @pl.when(2 * row + col > 0)
    def _():
        pl.semaphore_wait(barrier, 2 * row + col)

    tell_lower()
    for_others(small_act("start"), 0, lower_end)
    pack_bulk()
    for_others(bulk_act("start"), 0, lower_end)
    prepare()
    for_others(send_higher, higher_begin, n_row)

    @pl.when(jnp.logical_and(col == 0, home == 0))
    def _():
        pl.semaphore_wait(ready.at[n_row], 1)

    def wait_small(index):
        view = small_all.at[index]
        pltpu.make_async_copy(view, view, small_recv.at[index]).wait()

    def wait_bulk(index):
        near = is_near(2 * index + col)
        for view, go in ((bulk_all.at[index], near), (far_all.at[index], jnp.logical_not(near))):

            @pl.when(go)
            def _():
                pltpu.make_async_copy(view, view, bulk_recv.at[index]).wait()

    def inward(index, count):
        return jnp.where(row < chips, index, count - 1 - index)

    @pl.loop(0, near_pairs)
    def _(turn):
        pair = inward(turn, near_pairs)
        base = 2 * (first_pair + pair)
        middle[0:3] = jnp.zeros((3, LANES), jnp.float32)

        @pl.loop(0, 2)
        def _(slot):
            slot = inward(slot, 2)
            chip = chip_of(pair, slot)

            @pl.when(is_near(chip))
            def _():
                wait_small(base + slot)
                middle[0:3] += small_all[base + slot, 1, 0:3]

            @pl.when(jnp.logical_and(is_near(chip), chip != row))
            def _():
                green_of(3 * pair + 2 * slot, small_all[base + slot, 0, 0:3])

        @pl.when(pair_live(pair))
        def _():
            green_of(3 * pair + 1, middle[0:3])

    def for_chips(act, near):
        @pl.loop(0, chips)
        def _(index):
            go = is_near(2 * index + col)

            @pl.when(go if near else jnp.logical_not(go))
            def _():
                act(index)

    def impedance_of(chunk):
        packed = small_all[pl.ds(chunk * pieces, pieces), :, 4:8, :].reshape(2 * pieces, 4, LANES)
        packed = jnp.sum(packed, 0)
        places, soft = scaled(packed[0:3])
        area = packed[3:4] * (wave_ref[0] * (0.125 / PI / PI))
        at = pl.ds(pl.multiple_of(chunk * LANES, LANES), LANES)
        for part in range(4):
            block, half = part // 2, part % 2
            count = blk // 2
            here = slice(part * count, (part + 1) * count)
            d_x = tgt_wide[0, here] - places[0:1]
            d_y = tgt_wide[1, here] - places[1:2]
            d_z = tgt_wide[2, here] - places[2:3]
            squared = d_x * d_x + d_y * d_y + (d_z * d_z + soft)
            inverse, cosine, u, sine = wave_parts(squared)
            sine = u * sine
            along = tgt_wide[3, here] * d_x + tgt_wide[4, here] * d_y + tgt_wide[5, here] * d_z
            along = along * inverse
            scale = area * inverse
            green_re = scale * cosine
            green_im = scale * sine
            factor_re = 1.0 - along
            factor_im = along * (inverse * (-0.5 / PI))
            for side, value in enumerate(
                (
                    green_re * factor_re - green_im * factor_im,
                    green_re * factor_im + green_im * factor_re,
                )
            ):
                to = slice(side * blk + half * count, side * blk + (half + 1) * count)
                impedance[block, to, at] = value.astype(jnp.bfloat16)

    for_chips(wait_small, False)

    @pl.loop(0, chips // pieces)
    def _(chunk):
        impedance_of(chunk)

    @pl.loop(0, chips)
    def _(index):
        wait_bulk(index)

    for slot in range(2 * near_pairs):
        index = 2 * first_pair + slot
        rows = bulk_all[index, :, 0].reshape(2 * per, width)
        weights = jnp.concatenate(
            [bulk_all[index, :, 1 + part].reshape(2 * per, LANES) for part in range(3)], 1
        )
        both = lax.dot_general(weights, rows, TN, preferred_element_type=jnp.float32)
        value = plus_i(both[:qn], both[qn:])
        value = jnp.where(is_near(2 * index + col), value, 0.0)
        high, low = split_two(value)
        at = slice((slot % 2) * qn, (slot % 2 + 1) * qn)
        moment[slot // 2, at, 0:width] = high
        moment[slot // 2, at, width:] = low

    def near_part(block):
        right = moment[...].reshape(near_pairs * 2 * qn, 2 * width)
        both = jnp.dot(green_high[block], right, preferred_element_type=jnp.float32)
        both = both[:, :width] + both[:, width:]
        both = both + jnp.dot(green_low[block], right[:, :width], preferred_element_type=jnp.float32)
        high, low = split_two(plus_i(both[:qn], both[qn:]))
        product = jnp.dot(tests[block], jnp.concatenate([high, low], 1), preferred_element_type=jnp.float32)
        return product[:, :width] + product[:, width:]

    def far_part(block, both):
        def far_step(chunk, total):
            rows = []
            for piece in range(pieces):
                index = chunk * pieces + piece
                rows.append(
                    jnp.where(is_near(2 * index + col), bulk_all[index, :, 0], far_all[index]).reshape(
                        2 * per, width
                    )
                )
            at = pl.ds(pl.multiple_of(chunk * LANES, LANES), LANES)
            return total + jnp.dot(
                impedance[block, :, at], jnp.concatenate(rows, 0), preferred_element_type=jnp.float32
            )

        if chips == pieces:
            both = far_step(0, both)
        else:
            both = lax.fori_loop(0, chips // pieces, far_step, both)
        return plus_i(both[:blk], both[blk:])

    swap = pltpu.make_async_remote_copy(
        src_ref=part_send,
        dst_ref=part_recv,
        send_sem=part_sem.at[0],
        recv_sem=part_sem.at[1],
        device_id={"col": 1 - col},
        device_id_type=MESH,
    )
    part_send[...] = far_part(1 - col, near_part(1 - col))
    swap.start()
    out_ref[...] = far_part(col, near_part(col))
    for_others(small_act("wait_send"), 0, n_row)
    for_others(bulk_act("wait_send"), 0, n_row)
    swap.wait_recv()
    out_ref[...] += part_recv[...]
    swap.wait_send()


def on_device(
    wavenumber,
    tgt_geom,
    src_geom,
    excite,
    tgt_nodes,
    src_nodes,
    tgt_weights,
    src_weights,
    near_order,
):
    n_row = lax.axis_size("row")
    chips = n_row // 2
    blk = tgt_geom.shape[1] // 2
    qn = src_nodes.shape[1]
    per, width = src_geom.shape[1], excite.shape[0]
    excite_rows = excite.T
    weight_rows = src_weights.transpose(0, 2, 1)
    reach = (near_order.shape[1] - 1) // 2
    near_pairs = min(reach // 2 + 1, chips // 2)
    depth = near_pairs * 2 * qn
    hbm = pl.BlockSpec(memory_space=pl.ANY)
    dma = pltpu.SemaphoreType.DMA
    f32, bf16 = jnp.float32, jnp.bfloat16
    return pl.pallas_call(
        kernel,
        out_shape=pltpu.VMEM((blk, width), f32),
        in_specs=[hbm] * 9,
        out_specs=pl.BlockSpec(memory_space=pltpu.VMEM),
        scratch_shapes=[
            pltpu.VMEM((chips, 2, ROWS, LANES), f32),
            pltpu.VMEM((chips, 2, 4, per, LANES), bf16),
            pltpu.VMEM((chips, 2, per, LANES), bf16),
            pltpu.VMEM((ROWS, LANES), f32),
            pltpu.VMEM((ROWS, LANES), f32),
            pltpu.VMEM((4, per, LANES), bf16),
            pltpu.VMEM((2, 3, qn, LANES), f32),
            pltpu.VMEM((6, 2 * blk, LANES), f32),
            pltpu.VMEM((ROWS, LANES), f32),
            pltpu.VMEM((near_pairs * 6, ORDERS, ROWS, LANES), f32),
            pltpu.VMEM((2, 2 * blk, qn), bf16),
            pltpu.VMEM((2, 2 * qn, depth), bf16),
            pltpu.VMEM((2, 2 * qn, depth), bf16),
            pltpu.VMEM((near_pairs, 2 * qn, 2 * width), bf16),
            pltpu.VMEM((2, 2 * blk, chips * 2 * per), bf16),
            pltpu.VMEM((blk, width), f32),
            pltpu.VMEM((blk, width), f32),
            pltpu.SMEM(wavenumber.shape, f32),
            pltpu.SMEM(near_order.shape, jnp.int32),
            pltpu.VMEM(tgt_geom.shape, f32),
            pltpu.VMEM(tgt_nodes.shape, f32),
            pltpu.VMEM(tgt_weights.shape, bf16),
            pltpu.VMEM(src_geom.shape, f32),
            pltpu.VMEM(excite_rows.shape, bf16),
            pltpu.VMEM(src_nodes.shape, f32),
            pltpu.VMEM(weight_rows.shape, bf16),
            dma((9,)),
            dma((n_row,)),
            dma((n_row,)),
            dma((chips,)),
            dma((chips,)),
            dma((2,)),
            pltpu.SemaphoreType.REGULAR((n_row + 1,)),
        ],
        compiler_params=pltpu.CompilerParams(collective_id=0, has_side_effects=True),
        name="slab",
    )(
        wavenumber,
        near_order,
        tgt_geom,
        tgt_nodes,
        tgt_weights,
        src_geom,
        excite_rows,
        src_nodes,
        weight_rows,
    )


def solution(mesh):
    return jax.shard_map(
        on_device,
        mesh=mesh,
        in_specs=(
            P("groups"),
            P(None, ("groups", "row")),
            P(None, ("groups", "row", "col")),
            P(None, ("groups", "row", "col")),
            P(None, ("groups", "row")),
            P(None, ("groups", "row")),
            P(None, None, ("groups", "row")),
            P(None, None, ("groups", "row", "col")),
            P(("groups", "row"), None),
        ),
        out_specs=P(("groups", "row", "col"), None),
        check_vma=False,
    )
```

```python
import math

import jax
import jax.numpy as jnp
import numpy as np
from jax import lax
from jax.experimental import pallas as pl
from jax.experimental.pallas import tpu as pltpu
from jax.sharding import PartitionSpec as P

ORDERS = 3
SOFT = 0.05
PI = math.pi
LANES = 128
ROWS = 8
MESH = pl.DeviceIdType.MESH
TN = (((0,), (0,)), ((), ()))


def fitted(function, terms):
    nodes = (np.cos((np.arange(terms) + 0.5) * np.pi / terms) + 1.0) / 8.0
    matrix = np.vander(nodes, terms, increasing=True)
    return [float(c) for c in np.linalg.solve(matrix, function(np.sqrt(nodes)))]


COS = fitted(lambda u: np.cos(2.0 * np.pi * u), 6)
SIN = fitted(lambda u: np.sin(2.0 * np.pi * u) / u, 6)


def horner(coefficients, y):
    total = coefficients[-1]
    for c in coefficients[-2::-1]:
        total = total * y + c
    return total


def wave_parts(squared):
    inverse = lax.rsqrt(squared)
    turns = squared * inverse
    u = turns - jnp.round(turns)
    y = u * u
    return inverse, horner(COS, y), u, horner(SIN, y)


def plus_i(first, second):
    half = second.shape[1] // 2
    swapped = pltpu.roll(second, half, 1)
    lane = lax.broadcasted_iota(jnp.int32, second.shape, 1)
    return first + jnp.where(lane < half, -swapped, swapped)


def split_two(value):
    high = value.astype(jnp.bfloat16)
    return high, (value - high.astype(jnp.float32)).astype(jnp.bfloat16)


def columns_of(rows):
    few, lanes = rows.shape
    pad = jnp.zeros((ROWS - few, lanes), jnp.float32)
    return jnp.concatenate([rows, pad], 0).T


def kernel(
    wave_hbm,
    order_hbm,
    tgt_hbm,
    tnode_hbm,
    tweight_hbm,
    geom_hbm,
    excite_hbm,
    snode_hbm,
    sweight_hbm,
    out_ref,
    small_all,
    bulk_all,
    far_all,
    middle,
    small_pack,
    bulk_pack,
    tnode_wide,
    tgt_wide,
    origin,
    scale_all,
    tests,
    green_high,
    green_low,
    moment,
    impedance,
    part_send,
    part_recv,
    wave_ref,
    order_ref,
    tgt_ref,
    tnode_ref,
    tweight_ref,
    geom_ref,
    excite_ref,
    snode_ref,
    sweight_ref,
    local,
    small_send,
    bulk_send,
    small_recv,
    bulk_recv,
    part_sem,
    ready,
):
    n_row = lax.axis_size("row")
    row = lax.axis_index("row")
    col = lax.axis_index("col")
    home = lax.rem(row, 2)
    place = row // 2
    chips = n_row // 2
    reach = (order_hbm.shape[1] - 1) // 2
    qn = snode_hbm.shape[1]
    tail = qn - LANES
    step_nodes = qn // ORDERS
    per = excite_hbm.shape[0]
    blk, width = out_ref.shape
    near_pairs = moment.shape[0]
    first_pair = jnp.clip(
        (row - reach - col + 1 + 4 * reach) // 4 - reach, 0, chips // 2 - near_pairs
    )
    mine = home == col
    lane = lax.broadcasted_iota(jnp.int32, (1, LANES), 1)

    loads = [
        pltpu.make_async_copy(here, there, local.at[index])
        for index, (here, there) in enumerate(
            (
                (snode_hbm, snode_ref),
                (geom_hbm, geom_ref),
                (excite_hbm, excite_ref),
                (sweight_hbm, sweight_ref),
                (wave_hbm, wave_ref),
                (tnode_hbm, tnode_ref),
                (tgt_hbm, tgt_ref),
                (order_hbm, order_ref),
                (tweight_hbm, tweight_ref),
            )
        )
    ]
    for load in loads:
        load.start()

    barrier = pltpu.get_barrier_semaphore()

    @pl.loop(2 * row + col + 1, 2 * n_row)
    def _(index):
        pl.semaphore_signal(
            barrier,
            inc=1,
            device_id={"row": index // 2, "col": lax.rem(index, 2)},
            device_id_type=MESH,
        )

    def heads_of(nodes):
        return jnp.where(lax.rem(place, 2) == 0, nodes[:, :LANES], nodes[:, tail:])

    loads[0].wait()
    nodes = snode_ref[...]
    gap = jnp.zeros((nodes.shape[0], LANES - tail), jnp.float32)
    ends = jnp.where(
        lax.rem(place, 2) == 0,
        jnp.concatenate([nodes[:, LANES:], gap], 1),
        jnp.concatenate([gap, nodes[:, :tail]], 1),
    )
    small_pack[0:3, :] = jnp.where(col == 0, heads_of(nodes), ends)
    loads[1].wait()
    pieces = LANES // (2 * per)
    spread = jnp.concatenate([geom_ref[...]] * (LANES // per), 1)
    begin = (2 * lax.rem(place, pieces) + col) * per
    inside = jnp.logical_and(lane >= begin, lane < begin + per)
    small_pack[3:4, :] = jnp.zeros((1, LANES), jnp.float32)
    small_pack[4:8, :] = jnp.where(inside, spread, 0.0)

    @pl.when(mine)
    def _():
        pltpu.make_async_copy(small_pack, small_all.at[place, col], small_recv.at[place]).start()

    def pack_bulk():
        loads[2].wait()
        bulk_pack[0] = excite_ref[...]
        loads[3].wait()
        bulk_pack[1] = sweight_ref[0, :, :LANES]
        bulk_pack[2] = jnp.concatenate(
            [sweight_ref[0, :, LANES:].astype(jnp.float32), sweight_ref[1, :, :tail].astype(jnp.float32)], 1
        ).astype(jnp.bfloat16)
        bulk_pack[3] = sweight_ref[1, :, tail:]

        @pl.when(mine)
        def _():
            pltpu.make_async_copy(bulk_pack, bulk_all.at[place, col], bulk_recv.at[place]).start()

    def small_to(chip):
        return pltpu.make_async_remote_copy(
            src_ref=small_pack,
            dst_ref=small_all.at[place, col],
            send_sem=small_send.at[chip],
            recv_sem=small_recv.at[place],
            device_id={"row": chip, "col": home},
            device_id_type=MESH,
        )

    def bulk_to(chip, near):
        return pltpu.make_async_remote_copy(
            src_ref=bulk_pack if near else bulk_pack.at[0],
            dst_ref=bulk_all.at[place, col] if near else far_all.at[place, col],
            send_sem=bulk_send.at[chip],
            recv_sem=bulk_recv.at[place],
            device_id={"row": chip, "col": home},
            device_id_type=MESH,
        )

    def is_near(chip):
        return jnp.logical_and(chip >= row - reach, chip <= row + reach)

    lower_end = row + jnp.where(home < col, 1, 0)
    higher_begin = row + jnp.where(home > col, 0, 1)

    def for_others(act, begin, end):
        @pl.loop(begin, end)
        def _(chip):
            @pl.when(jnp.logical_not(jnp.logical_and(mine, chip == row)))
            def _():
                act(chip)

    def tell(chip, core, slot):
        pl.semaphore_signal(
            ready.at[slot], inc=1, device_id={"row": chip, "col": core}, device_id_type=MESH
        )

    def tell_lower():
        @pl.loop(0, row // 2 + 1)
        def _(index):
            chip = 2 * index + col
            for core in range(2):

                @pl.when(2 * chip + core < 2 * row + col)
                def _():
                    tell(chip, core, row)

        @pl.when(jnp.logical_and(col == 1, home == 0))
        def _():
            tell(row, 0, n_row)

    def send_higher(chip):
        pl.semaphore_wait(ready.at[chip], 1)
        small_to(chip).start()
        bulk_act("start")(chip)

    def small_act(name):
        return lambda chip: getattr(small_to(chip), name)()

    def bulk_act(name):
        def act(chip):
            near = is_near(chip)

            @pl.when(near)
            def _():
                getattr(bulk_to(chip, True), name)()

            @pl.when(jnp.logical_not(near))
            def _():
                getattr(bulk_to(chip, False), name)()

        return act

    def order_of(block, chip):
        offset = jnp.clip(chip - row + reach, 0, 2 * reach)
        return jnp.where(is_near(chip), order_ref[block, offset] * step_nodes, 0)

    def chip_of(pair, slot):
        return 4 * (first_pair + pair) + 2 * slot + col

    def prepare():
        loads[4].wait()
        loads[5].wait()
        loads[7].wait()
        rate = wave_ref[0] * (0.5 / PI)
        origin[0:3] = jnp.broadcast_to(tnode_ref[:, 0:1], (3, LANES))
        cols = columns_of(tnode_ref[...])
        first = cols[0:1]
        cols = (cols - first) * rate
        for block in range(2):
            for axis in range(3):
                tnode_wide[block, axis] = jnp.broadcast_to(
                    cols[block * qn : (block + 1) * qn, axis : axis + 1], (qn, LANES)
                )

        @pl.loop(0, near_pairs)
        def _(pair):
            for block in range(2):
                even, odd = (order_of(block, chip_of(pair, slot)) for slot in range(2))
                middle = jnp.where(lane < tail, even, odd)
                for part, (limit, ahead) in enumerate(
                    (
                        (even, lane),
                        (middle, jnp.where(lane < tail, lane + LANES, lane - tail)),
                        (odd, lane + tail),
                    )
                ):
                    for group in range(ORDERS):
                        live = jnp.logical_and(ahead < limit, limit > group * step_nodes)
                        value = jnp.where(live, rate * (0.25 / PI), 0.0)
                        at = (3 * pair + part) * 2 + block
                        scale_all[at, group] = jnp.broadcast_to(value, (ROWS, LANES))

            for slot in range(2):

                @pl.when(jnp.logical_not(is_near(chip_of(pair, slot))))
                def _():
                    at = pl.ds(pl.multiple_of((3 * pair + 2 * slot) * LANES, LANES), LANES)
                    for block in range(2):
                        green_high[block, :, at] = jnp.zeros((2 * qn, LANES), jnp.bfloat16)
                        green_low[block, :, at] = jnp.zeros((2 * qn, LANES), jnp.bfloat16)

            @pl.when(jnp.logical_not(pair_live(pair)))
            def _():
                at = pl.ds(pl.multiple_of((3 * pair + 1) * LANES, LANES), LANES)
                for block in range(2):
                    green_high[block, :, at] = jnp.zeros((2 * qn, LANES), jnp.bfloat16)
                    green_low[block, :, at] = jnp.zeros((2 * qn, LANES), jnp.bfloat16)

        @pl.when(mine)
        def _():
            own = place - 2 * first_pair
            green_of(3 * (own // 2) + 2 * lax.rem(own, 2), heads_of(snode_ref[...]))

        loads[6].wait()
        cols = columns_of(tgt_ref[...])
        for axis in range(6):
            line = cols[:, axis : axis + 1]
            if axis < 3:
                line = (line - first[:, axis : axis + 1]) * rate
            tgt_wide[axis] = jnp.broadcast_to(line, (2 * blk, LANES))
        loads[8].wait()
        for block in range(2):
            at = slice(block * blk, (block + 1) * blk)
            for part in range(2):
                tests[block, part * blk : (part + 1) * blk] = tweight_ref[part, :, at].T

    def pair_live(pair):
        return jnp.logical_or(is_near(chip_of(pair, 0)), is_near(chip_of(pair, 1)))

    def scaled(places):
        rate = wave_ref[0] * (0.5 / PI)
        return (places - origin[0:3]) * rate, rate * rate * (SOFT * SOFT)

    def green_of(chunk, places):
        places, soft = scaled(places)
        s_x, s_y, s_z = (jnp.broadcast_to(places[i : i + 1], (step_nodes, LANES)) for i in range(3))
        at = pl.ds(pl.multiple_of(chunk * LANES, LANES), LANES)

        @pl.loop(0, 2)
        def _(block):
            for group in range(ORDERS):
                here = slice(group * step_nodes, (group + 1) * step_nodes)
                scale = jnp.broadcast_to(scale_all[chunk * 2 + block, group, 0:1], (step_nodes, LANES))
                d_x = tnode_wide[block, 0, here] - s_x
                d_y = tnode_wide[block, 1, here] - s_y
                d_z = tnode_wide[block, 2, here] - s_z
                squared = d_x * d_x + d_y * d_y + (d_z * d_z + soft)
                inverse, cosine, u, sine = wave_parts(squared)
                inverse = inverse * scale
                for part, value in enumerate((inverse * cosine, (inverse * u) * sine)):
                    high, low = split_two(value)
                    to = slice(part * qn + group * step_nodes, part * qn + (group + 1) * step_nodes)
                    green_high[block, to, at] = high
                    green_low[block, to, at] = low

    @pl.when(2 * row + col > 0)
    def _():
        pl.semaphore_wait(barrier, 2 * row + col)

    tell_lower()
    urgent = jnp.minimum(lower_end, 2)
    for_others(small_act("start"), 0, lower_end)
    pack_bulk()
    for_others(bulk_act("start"), 0, urgent)
    prepare()
    for_others(bulk_act("start"), urgent, lower_end)
    for_others(send_higher, higher_begin, n_row)

    @pl.when(jnp.logical_and(col == 0, home == 0))
    def _():
        pl.semaphore_wait(ready.at[n_row], 1)

    def wait_small(index):
        view = small_all.at[index]
        pltpu.make_async_copy(view, view, small_recv.at[index]).wait()

    def wait_bulk(index):
        near = is_near(2 * index + col)
        for view, go in ((bulk_all.at[index], near), (far_all.at[index], jnp.logical_not(near))):

            @pl.when(go)
            def _():
                pltpu.make_async_copy(view, view, bulk_recv.at[index]).wait()

    def inward(index, count):
        return jnp.where(row < chips, index, count - 1 - index)

    @pl.loop(0, near_pairs)
    def _(turn):
        pair = inward(turn, near_pairs)
        base = 2 * (first_pair + pair)
        middle[0:3] = jnp.zeros((3, LANES), jnp.float32)

        @pl.loop(0, 2)
        def _(slot):
            slot = inward(slot, 2)
            chip = chip_of(pair, slot)

            @pl.when(is_near(chip))
            def _():
                wait_small(base + slot)
                middle[0:3] += small_all[base + slot, 1, 0:3]

            @pl.when(jnp.logical_and(is_near(chip), chip != row))
            def _():
                green_of(3 * pair + 2 * slot, small_all[base + slot, 0, 0:3])

        @pl.when(pair_live(pair))
        def _():
            green_of(3 * pair + 1, middle[0:3])

    def for_chips(act, near):
        @pl.loop(0, chips)
        def _(index):
            go = is_near(2 * index + col)

            @pl.when(go if near else jnp.logical_not(go))
            def _():
                act(index)

    def impedance_of(chunk):
        packed = small_all[pl.ds(chunk * pieces, pieces), :, 4:8, :].reshape(2 * pieces, 4, LANES)
        packed = jnp.sum(packed, 0)
        places, soft = scaled(packed[0:3])
        area = packed[3:4] * (wave_ref[0] * (0.125 / PI / PI))
        at = pl.ds(pl.multiple_of(chunk * LANES, LANES), LANES)
        for part in range(4):
            block, half = part // 2, part % 2
            count = blk // 2
            here = slice(part * count, (part + 1) * count)
            d_x = tgt_wide[0, here] - places[0:1]
            d_y = tgt_wide[1, here] - places[1:2]
            d_z = tgt_wide[2, here] - places[2:3]
            squared = d_x * d_x + d_y * d_y + (d_z * d_z + soft)
            inverse, cosine, u, sine = wave_parts(squared)
            sine = u * sine
            along = tgt_wide[3, here] * d_x + tgt_wide[4, here] * d_y + tgt_wide[5, here] * d_z
            along = along * inverse
            scale = area * inverse
            green_re = scale * cosine
            green_im = scale * sine
            factor_re = 1.0 - along
            factor_im = along * (inverse * (-0.5 / PI))
            for side, value in enumerate(
                (
                    green_re * factor_re - green_im * factor_im,
                    green_re * factor_im + green_im * factor_re,
                )
            ):
                to = slice(side * blk + half * count, side * blk + (half + 1) * count)
                impedance[block, to, at] = value.astype(jnp.bfloat16)

    for_chips(wait_small, False)

    @pl.loop(0, chips // pieces)
    def _(chunk):
        impedance_of(chunk)

    @pl.loop(0, chips)
    def _(index):
        wait_bulk(index)

    for slot in range(2 * near_pairs):
        index = 2 * first_pair + slot
        rows = bulk_all[index, :, 0].reshape(2 * per, width)
        weights = jnp.concatenate(
            [bulk_all[index, :, 1 + part].reshape(2 * per, LANES) for part in range(3)], 1
        )
        both = lax.dot_general(weights, rows, TN, preferred_element_type=jnp.float32)
        value = plus_i(both[:qn], both[qn:])
        value = jnp.where(is_near(2 * index + col), value, 0.0)
        high, low = split_two(value)
        at = slice((slot % 2) * qn, (slot % 2 + 1) * qn)
        moment[slot // 2, at, 0:width] = high
        moment[slot // 2, at, width:] = low

    def near_part(block):
        right = moment[...].reshape(near_pairs * 2 * qn, 2 * width)
        both = jnp.dot(green_high[block], right, preferred_element_type=jnp.float32)
        both = both[:, :width] + both[:, width:]
        both = both + jnp.dot(green_low[block], right[:, :width], preferred_element_type=jnp.float32)
        high, low = split_two(plus_i(both[:qn], both[qn:]))
        product = jnp.dot(tests[block], jnp.concatenate([high, low], 1), preferred_element_type=jnp.float32)
        return product[:, :width] + product[:, width:]

    def far_part(block, both):
        def far_step(chunk, total):
            rows = []
            for piece in range(pieces):
                index = chunk * pieces + piece
                rows.append(
                    jnp.where(is_near(2 * index + col), bulk_all[index, :, 0], far_all[index]).reshape(
                        2 * per, width
                    )
                )
            at = pl.ds(pl.multiple_of(chunk * LANES, LANES), LANES)
            return total + jnp.dot(
                impedance[block, :, at], jnp.concatenate(rows, 0), preferred_element_type=jnp.float32
            )

        if chips == pieces:
            both = far_step(0, both)
        else:
            both = lax.fori_loop(0, chips // pieces, far_step, both)
        return plus_i(both[:blk], both[blk:])

    swap = pltpu.make_async_remote_copy(
        src_ref=part_send,
        dst_ref=part_recv,
        send_sem=part_sem.at[0],
        recv_sem=part_sem.at[1],
        device_id={"col": 1 - col},
        device_id_type=MESH,
    )
    part_send[...] = far_part(1 - col, near_part(1 - col))
    swap.start()
    out_ref[...] = far_part(col, near_part(col))
    for_others(small_act("wait_send"), 0, n_row)
    for_others(bulk_act("wait_send"), 0, n_row)
    swap.wait_recv()
    out_ref[...] += part_recv[...]
    swap.wait_send()


def on_device(
    wavenumber,
    tgt_geom,
    src_geom,
    excite,
    tgt_nodes,
    src_nodes,
    tgt_weights,
    src_weights,
    near_order,
):
    n_row = lax.axis_size("row")
    chips = n_row // 2
    blk = tgt_geom.shape[1] // 2
    qn = src_nodes.shape[1]
    per, width = src_geom.shape[1], excite.shape[0]
    excite_rows = excite.T
    weight_rows = src_weights.transpose(0, 2, 1)
    reach = (near_order.shape[1] - 1) // 2
    near_pairs = min(reach // 2 + 1, chips // 2)
    depth = near_pairs * 2 * qn
    hbm = pl.BlockSpec(memory_space=pl.ANY)
    dma = pltpu.SemaphoreType.DMA
    f32, bf16 = jnp.float32, jnp.bfloat16
    return pl.pallas_call(
        kernel,
        out_shape=pltpu.VMEM((blk, width), f32),
        in_specs=[hbm] * 9,
        out_specs=pl.BlockSpec(memory_space=pltpu.VMEM),
        scratch_shapes=[
            pltpu.VMEM((chips, 2, ROWS, LANES), f32),
            pltpu.VMEM((chips, 2, 4, per, LANES), bf16),
            pltpu.VMEM((chips, 2, per, LANES), bf16),
            pltpu.VMEM((ROWS, LANES), f32),
            pltpu.VMEM((ROWS, LANES), f32),
            pltpu.VMEM((4, per, LANES), bf16),
            pltpu.VMEM((2, 3, qn, LANES), f32),
            pltpu.VMEM((6, 2 * blk, LANES), f32),
            pltpu.VMEM((ROWS, LANES), f32),
            pltpu.VMEM((near_pairs * 6, ORDERS, ROWS, LANES), f32),
            pltpu.VMEM((2, 2 * blk, qn), bf16),
            pltpu.VMEM((2, 2 * qn, depth), bf16),
            pltpu.VMEM((2, 2 * qn, depth), bf16),
            pltpu.VMEM((near_pairs, 2 * qn, 2 * width), bf16),
            pltpu.VMEM((2, 2 * blk, chips * 2 * per), bf16),
            pltpu.VMEM((blk, width), f32),
            pltpu.VMEM((blk, width), f32),
            pltpu.SMEM(wavenumber.shape, f32),
            pltpu.SMEM(near_order.shape, jnp.int32),
            pltpu.VMEM(tgt_geom.shape, f32),
            pltpu.VMEM(tgt_nodes.shape, f32),
            pltpu.VMEM(tgt_weights.shape, bf16),
            pltpu.VMEM(src_geom.shape, f32),
            pltpu.VMEM(excite_rows.shape, bf16),
            pltpu.VMEM(src_nodes.shape, f32),
            pltpu.VMEM(weight_rows.shape, bf16),
            dma((9,)),
            dma((n_row,)),
            dma((n_row,)),
            dma((chips,)),
            dma((chips,)),
            dma((2,)),
            pltpu.SemaphoreType.REGULAR((n_row + 1,)),
        ],
        compiler_params=pltpu.CompilerParams(collective_id=0, has_side_effects=True),
        name="slab",
    )(
        wavenumber,
        near_order,
        tgt_geom,
        tgt_nodes,
        tgt_weights,
        src_geom,
        excite_rows,
        src_nodes,
        weight_rows,
    )


def solution(mesh):
    return jax.shard_map(
        on_device,
        mesh=mesh,
        in_specs=(
            P("groups"),
            P(None, ("groups", "row")),
            P(None, ("groups", "row", "col")),
            P(None, ("groups", "row", "col")),
            P(None, ("groups", "row")),
            P(None, ("groups", "row")),
            P(None, None, ("groups", "row")),
            P(None, None, ("groups", "row", "col")),
            P(("groups", "row"), None),
        ),
        out_specs=P(("groups", "row", "col"), None),
        check_vma=False,
    )
```

```python
import math

import jax
import jax.numpy as jnp
import numpy as np
from jax import lax
from jax.experimental import pallas as pl
from jax.experimental.pallas import tpu as pltpu
from jax.sharding import PartitionSpec as P

ORDERS = 3
SOFT = 0.05
PI = math.pi
LANES = 128
ROWS = 8
MESH = pl.DeviceIdType.MESH
TN = (((0,), (0,)), ((), ()))


def fitted(function, terms):
    nodes = (np.cos((np.arange(terms) + 0.5) * np.pi / terms) + 1.0) / 8.0
    matrix = np.vander(nodes, terms, increasing=True)
    return [float(c) for c in np.linalg.solve(matrix, function(np.sqrt(nodes)))]


COS = fitted(lambda u: np.cos(2.0 * np.pi * u), 6)
SIN = fitted(lambda u: np.sin(2.0 * np.pi * u) / u, 6)


def horner(coefficients, y):
    total = coefficients[-1]
    for c in coefficients[-2::-1]:
        total = total * y + c
    return total


def wave_parts(squared):
    inverse = lax.rsqrt(squared)
    turns = squared * inverse
    u = turns - jnp.round(turns)
    y = u * u
    return inverse, horner(COS, y), u, horner(SIN, y)


def plus_i(first, second):
    half = second.shape[1] // 2
    swapped = pltpu.roll(second, half, 1)
    lane = lax.broadcasted_iota(jnp.int32, second.shape, 1)
    return first + jnp.where(lane < half, -swapped, swapped)


def split_two(value):
    high = value.astype(jnp.bfloat16)
    return high, (value - high.astype(jnp.float32)).astype(jnp.bfloat16)


def columns_of(rows):
    few, lanes = rows.shape
    pad = jnp.zeros((ROWS - few, lanes), jnp.float32)
    return jnp.concatenate([rows, pad], 0).T


def kernel(
    wave_hbm,
    order_hbm,
    tgt_hbm,
    tnode_hbm,
    tweight_hbm,
    geom_hbm,
    excite_hbm,
    snode_hbm,
    sweight_hbm,
    out_ref,
    small_all,
    bulk_all,
    far_all,
    middle,
    small_pack,
    bulk_pack,
    tnode_wide,
    tgt_wide,
    origin,
    scale_all,
    tests,
    green_high,
    green_low,
    moment,
    impedance,
    part_send,
    part_recv,
    wave_ref,
    order_ref,
    tgt_ref,
    tnode_ref,
    tweight_ref,
    geom_ref,
    excite_ref,
    snode_ref,
    sweight_ref,
    local,
    small_send,
    bulk_send,
    small_recv,
    bulk_recv,
    part_sem,
    ready,
):
    n_row = lax.axis_size("row")
    row = lax.axis_index("row")
    col = lax.axis_index("col")
    home = lax.rem(row, 2)
    place = row // 2
    chips = n_row // 2
    reach = (order_hbm.shape[1] - 1) // 2
    qn = snode_hbm.shape[1]
    tail = qn - LANES
    step_nodes = qn // ORDERS
    per = excite_hbm.shape[0]
    blk, width = out_ref.shape
    near_pairs = moment.shape[0]
    first_pair = jnp.clip(
        (row - reach - col + 1 + 4 * reach) // 4 - reach, 0, chips // 2 - near_pairs
    )
    mine = home == col
    lane = lax.broadcasted_iota(jnp.int32, (1, LANES), 1)

    loads = [
        pltpu.make_async_copy(here, there, local.at[index])
        for index, (here, there) in enumerate(
            (
                (snode_hbm, snode_ref),
                (geom_hbm, geom_ref),
                (excite_hbm, excite_ref),
                (sweight_hbm, sweight_ref),
                (wave_hbm, wave_ref),
                (tnode_hbm, tnode_ref),
                (tgt_hbm, tgt_ref),
                (order_hbm, order_ref),
                (tweight_hbm, tweight_ref),
            )
        )
    ]
    for load in loads:
        load.start()

    barrier = pltpu.get_barrier_semaphore()

    @pl.loop(2 * row + col + 1, 2 * n_row)
    def _(index):
        pl.semaphore_signal(
            barrier,
            inc=1,
            device_id={"row": index // 2, "col": lax.rem(index, 2)},
            device_id_type=MESH,
        )

    def heads_of(nodes):
        return jnp.where(lax.rem(place, 2) == 0, nodes[:, :LANES], nodes[:, tail:])

    loads[0].wait()
    nodes = snode_ref[...]
    gap = jnp.zeros((nodes.shape[0], LANES - tail), jnp.float32)
    ends = jnp.where(
        lax.rem(place, 2) == 0,
        jnp.concatenate([nodes[:, LANES:], gap], 1),
        jnp.concatenate([gap, nodes[:, :tail]], 1),
    )
    small_pack[0:3, :] = jnp.where(col == 0, heads_of(nodes), ends)
    loads[1].wait()
    pieces = LANES // (2 * per)
    spread = jnp.concatenate([geom_ref[...]] * (LANES // per), 1)
    begin = (2 * lax.rem(place, pieces) + col) * per
    inside = jnp.logical_and(lane >= begin, lane < begin + per)
    small_pack[3:4, :] = jnp.zeros((1, LANES), jnp.float32)
    small_pack[4:8, :] = jnp.where(inside, spread, 0.0)

    @pl.when(mine)
    def _():
        pltpu.make_async_copy(small_pack, small_all.at[place, col], small_recv.at[place]).start()

    def pack_bulk():
        loads[2].wait()
        bulk_pack[0] = excite_ref[...]
        loads[3].wait()
        bulk_pack[1] = sweight_ref[0, :, :LANES]
        bulk_pack[2] = jnp.concatenate(
            [sweight_ref[0, :, LANES:].astype(jnp.float32), sweight_ref[1, :, :tail].astype(jnp.float32)], 1
        ).astype(jnp.bfloat16)
        bulk_pack[3] = sweight_ref[1, :, tail:]

        @pl.when(mine)
        def _():
            pltpu.make_async_copy(bulk_pack, bulk_all.at[place, col], bulk_recv.at[place]).start()

    def small_to(chip):
        return pltpu.make_async_remote_copy(
            src_ref=small_pack,
            dst_ref=small_all.at[place, col],
            send_sem=small_send.at[chip],
            recv_sem=small_recv.at[place],
            device_id={"row": chip, "col": home},
            device_id_type=MESH,
        )

    def bulk_to(chip, near):
        return pltpu.make_async_remote_copy(
            src_ref=bulk_pack if near else bulk_pack.at[0],
            dst_ref=bulk_all.at[place, col] if near else far_all.at[place, col],
            send_sem=bulk_send.at[chip],
            recv_sem=bulk_recv.at[place],
            device_id={"row": chip, "col": home},
            device_id_type=MESH,
        )

    def is_near(chip):
        return jnp.logical_and(chip >= row - reach, chip <= row + reach)

    lower_end = row + jnp.where(home < col, 1, 0)
    higher_begin = row + jnp.where(home > col, 0, 1)

    def for_others(act, begin, end):
        @pl.loop(begin, end)
        def _(chip):
            @pl.when(jnp.logical_not(jnp.logical_and(mine, chip == row)))
            def _():
                act(chip)

    def tell(chip, core, slot):
        pl.semaphore_signal(
            ready.at[slot], inc=1, device_id={"row": chip, "col": core}, device_id_type=MESH
        )

    def tell_lower():
        @pl.loop(0, row // 2 + 1)
        def _(index):
            chip = 2 * index + col
            for core in range(2):

                @pl.when(2 * chip + core < 2 * row + col)
                def _():
                    tell(chip, core, row)

        @pl.when(jnp.logical_and(col == 1, home == 0))
        def _():
            tell(row, 0, n_row)

    def send_higher(chip):
        pl.semaphore_wait(ready.at[chip], 1)
        small_to(chip).start()
        bulk_act("start")(chip)

    def small_act(name):
        return lambda chip: getattr(small_to(chip), name)()

    def bulk_act(name):
        def act(chip):
            near = is_near(chip)

            @pl.when(near)
            def _():
                getattr(bulk_to(chip, True), name)()

            @pl.when(jnp.logical_not(near))
            def _():
                getattr(bulk_to(chip, False), name)()

        return act

    def order_of(block, chip):
        offset = jnp.clip(chip - row + reach, 0, 2 * reach)
        return jnp.where(is_near(chip), order_ref[block, offset] * step_nodes, 0)

    def chip_of(pair, slot):
        return 4 * (first_pair + pair) + 2 * slot + col

    def prepare():
        loads[4].wait()
        loads[5].wait()
        loads[7].wait()
        rate = wave_ref[0] * (0.5 / PI)
        origin[0:3] = jnp.broadcast_to(tnode_ref[:, 0:1], (3, LANES))
        cols = columns_of(tnode_ref[...])
        first = cols[0:1]
        cols = (cols - first) * rate
        for block in range(2):
            for axis in range(3):
                tnode_wide[block, axis] = jnp.broadcast_to(
                    cols[block * qn : (block + 1) * qn, axis : axis + 1], (qn, LANES)
                )

        @pl.loop(0, near_pairs)
        def _(pair):
            for block in range(2):
                even, odd = (order_of(block, chip_of(pair, slot)) for slot in range(2))
                middle = jnp.where(lane < tail, even, odd)
                for part, (limit, ahead) in enumerate(
                    (
                        (even, lane),
                        (middle, jnp.where(lane < tail, lane + LANES, lane - tail)),
                        (odd, lane + tail),
                    )
                ):
                    for group in range(ORDERS):
                        live = jnp.logical_and(ahead < limit, limit > group * step_nodes)
                        value = jnp.where(live, rate * (0.25 / PI), 0.0)
                        at = (3 * pair + part) * 2 + block
                        scale_all[at, group] = jnp.broadcast_to(value, (ROWS, LANES))

            for slot in range(2):

                @pl.when(jnp.logical_not(is_near(chip_of(pair, slot))))
                def _():
                    at = pl.ds(pl.multiple_of((3 * pair + 2 * slot) * LANES, LANES), LANES)
                    for block in range(2):
                        green_high[block, :, at] = jnp.zeros((2 * qn, LANES), jnp.bfloat16)
                        green_low[block, :, at] = jnp.zeros((2 * qn, LANES), jnp.bfloat16)

            @pl.when(jnp.logical_not(pair_live(pair)))
            def _():
                at = pl.ds(pl.multiple_of((3 * pair + 1) * LANES, LANES), LANES)
                for block in range(2):
                    green_high[block, :, at] = jnp.zeros((2 * qn, LANES), jnp.bfloat16)
                    green_low[block, :, at] = jnp.zeros((2 * qn, LANES), jnp.bfloat16)

        @pl.when(mine)
        def _():
            own = place - 2 * first_pair
            green_of(3 * (own // 2) + 2 * lax.rem(own, 2), heads_of(snode_ref[...]))

        loads[6].wait()
        cols = columns_of(tgt_ref[...])
        for axis in range(6):
            line = cols[:, axis : axis + 1]
            if axis < 3:
                line = (line - first[:, axis : axis + 1]) * rate
            tgt_wide[axis] = jnp.broadcast_to(line, (2 * blk, LANES))
        loads[8].wait()
        for block in range(2):
            at = slice(block * blk, (block + 1) * blk)
            for part in range(2):
                tests[block, part * blk : (part + 1) * blk] = tweight_ref[part, :, at].T

    def pair_live(pair):
        return jnp.logical_or(is_near(chip_of(pair, 0)), is_near(chip_of(pair, 1)))

    def scaled(places):
        rate = wave_ref[0] * (0.5 / PI)
        return (places - origin[0:3]) * rate, rate * rate * (SOFT * SOFT)

    def green_of(chunk, places):
        places, soft = scaled(places)
        s_x, s_y, s_z = (jnp.broadcast_to(places[i : i + 1], (step_nodes, LANES)) for i in range(3))
        at = pl.ds(pl.multiple_of(chunk * LANES, LANES), LANES)

        @pl.loop(0, 2)
        def _(block):
            for group in range(ORDERS):
                here = slice(group * step_nodes, (group + 1) * step_nodes)
                scale = jnp.broadcast_to(scale_all[chunk * 2 + block, group, 0:1], (step_nodes, LANES))
                d_x = tnode_wide[block, 0, here] - s_x
                d_y = tnode_wide[block, 1, here] - s_y
                d_z = tnode_wide[block, 2, here] - s_z
                squared = d_x * d_x + d_y * d_y + (d_z * d_z + soft)
                inverse, cosine, u, sine = wave_parts(squared)
                inverse = inverse * scale
                for part, value in enumerate((inverse * cosine, (inverse * u) * sine)):
                    high, low = split_two(value)
                    to = slice(part * qn + group * step_nodes, part * qn + (group + 1) * step_nodes)
                    green_high[block, to, at] = high
                    green_low[block, to, at] = low

    pack_bulk()

    @pl.when(2 * row + col > 0)
    def _():
        pl.semaphore_wait(barrier, 2 * row + col)

    tell_lower()
    urgent = jnp.minimum(lower_end, jnp.maximum(row - reach, 2))

    def both_act(chip):
        small_to(chip).start()
        bulk_act("start")(chip)

    for_others(both_act, 0, urgent)
    for_others(small_act("start"), urgent, lower_end)
    prepare()
    for_others(bulk_act("start"), urgent, lower_end)
    split = jnp.where(row == 0, jnp.minimum(reach + 2, n_row), n_row)
    for_others(send_higher, higher_begin, split)

    def wait_small(index):
        view = small_all.at[index]
        pltpu.make_async_copy(view, view, small_recv.at[index]).wait()

    def wait_bulk(index):
        near = is_near(2 * index + col)
        for view, go in ((bulk_all.at[index], near), (far_all.at[index], jnp.logical_not(near))):

            @pl.when(go)
            def _():
                pltpu.make_async_copy(view, view, bulk_recv.at[index]).wait()

    def inward(index, count):
        return jnp.where(row < chips, index, count - 1 - index)

    def green_some(begin, end):
        @pl.loop(begin, end)
        def _(turn):
            pair = inward(turn, near_pairs)
            base = 2 * (first_pair + pair)
            middle[0:3] = jnp.zeros((3, LANES), jnp.float32)

            @pl.loop(0, 2)
            def _(slot):
                slot = inward(slot, 2)
                chip = chip_of(pair, slot)

                @pl.when(is_near(chip))
                def _():
                    wait_small(base + slot)
                    middle[0:3] += small_all[base + slot, 1, 0:3]

                @pl.when(jnp.logical_and(is_near(chip), chip != row))
                def _():
                    green_of(3 * pair + 2 * slot, small_all[base + slot, 0, 0:3])

            @pl.when(pair_live(pair))
            def _():
                green_of(3 * pair + 1, middle[0:3])

    done = jnp.where(row == 0, 1, 0)
    green_some(0, done)
    for_others(send_higher, split, n_row)

    @pl.when(jnp.logical_and(col == 0, home == 0))
    def _():
        pl.semaphore_wait(ready.at[n_row], 1)

    green_some(done, near_pairs)

    def for_chips(act, near):
        @pl.loop(0, chips)
        def _(index):
            go = is_near(2 * index + col)

            @pl.when(go if near else jnp.logical_not(go))
            def _():
                act(index)

    def impedance_of(chunk):
        packed = small_all[pl.ds(chunk * pieces, pieces), :, 4:8, :].reshape(2 * pieces, 4, LANES)
        packed = jnp.sum(packed, 0)
        places, soft = scaled(packed[0:3])
        area = packed[3:4] * (wave_ref[0] * (0.125 / PI / PI))
        at = pl.ds(pl.multiple_of(chunk * LANES, LANES), LANES)
        for part in range(4):
            block, half = part // 2, part % 2
            count = blk // 2
            here = slice(part * count, (part + 1) * count)
            d_x = tgt_wide[0, here] - places[0:1]
            d_y = tgt_wide[1, here] - places[1:2]
            d_z = tgt_wide[2, here] - places[2:3]
            squared = d_x * d_x + d_y * d_y + (d_z * d_z + soft)
            inverse, cosine, u, sine = wave_parts(squared)
            sine = u * sine
            along = tgt_wide[3, here] * d_x + tgt_wide[4, here] * d_y + tgt_wide[5, here] * d_z
            along = along * inverse
            scale = area * inverse
            green_re = scale * cosine
            green_im = scale * sine
            factor_re = 1.0 - along
            factor_im = along * (inverse * (-0.5 / PI))
            for side, value in enumerate(
                (
                    green_re * factor_re - green_im * factor_im,
                    green_re * factor_im + green_im * factor_re,
                )
            ):
                to = slice(side * blk + half * count, side * blk + (half + 1) * count)
                impedance[block, to, at] = value.astype(jnp.bfloat16)

    for_chips(wait_small, False)

    @pl.loop(0, chips // pieces)
    def _(chunk):
        impedance_of(chunk)

    @pl.loop(0, chips)
    def _(index):
        wait_bulk(index)

    for slot in range(2 * near_pairs):
        index = 2 * first_pair + slot
        rows = bulk_all[index, :, 0].reshape(2 * per, width)
        weights = jnp.concatenate(
            [bulk_all[index, :, 1 + part].reshape(2 * per, LANES) for part in range(3)], 1
        )
        both = lax.dot_general(weights, rows, TN, preferred_element_type=jnp.float32)
        value = plus_i(both[:qn], both[qn:])
        value = jnp.where(is_near(2 * index + col), value, 0.0)
        high, low = split_two(value)
        at = slice((slot % 2) * qn, (slot % 2 + 1) * qn)
        moment[slot // 2, at, 0:width] = high
        moment[slot // 2, at, width:] = low

    def near_part(block):
        right = moment[...].reshape(near_pairs * 2 * qn, 2 * width)
        both = jnp.dot(green_high[block], right, preferred_element_type=jnp.float32)
        both = both[:, :width] + both[:, width:]
        both = both + jnp.dot(green_low[block], right[:, :width], preferred_element_type=jnp.float32)
        high, low = split_two(plus_i(both[:qn], both[qn:]))
        product = jnp.dot(tests[block], jnp.concatenate([high, low], 1), preferred_element_type=jnp.float32)
        return product[:, :width] + product[:, width:]

    def far_part(block, both):
        def far_step(chunk, total):
            rows = []
            for piece in range(pieces):
                index = chunk * pieces + piece
                rows.append(
                    jnp.where(is_near(2 * index + col), bulk_all[index, :, 0], far_all[index]).reshape(
                        2 * per, width
                    )
                )
            at = pl.ds(pl.multiple_of(chunk * LANES, LANES), LANES)
            return total + jnp.dot(
                impedance[block, :, at], jnp.concatenate(rows, 0), preferred_element_type=jnp.float32
            )

        if chips == pieces:
            both = far_step(0, both)
        else:
            both = lax.fori_loop(0, chips // pieces, far_step, both)
        return plus_i(both[:blk], both[blk:])

    swap = pltpu.make_async_remote_copy(
        src_ref=part_send,
        dst_ref=part_recv,
        send_sem=part_sem.at[0],
        recv_sem=part_sem.at[1],
        device_id={"col": 1 - col},
        device_id_type=MESH,
    )
    part_send[...] = far_part(1 - col, near_part(1 - col))
    swap.start()
    out_ref[...] = far_part(col, near_part(col))
    for_others(small_act("wait_send"), 0, n_row)
    for_others(bulk_act("wait_send"), 0, n_row)
    swap.wait_recv()
    out_ref[...] += part_recv[...]
    swap.wait_send()


def on_device(
    wavenumber,
    tgt_geom,
    src_geom,
    excite,
    tgt_nodes,
    src_nodes,
    tgt_weights,
    src_weights,
    near_order,
):
    n_row = lax.axis_size("row")
    chips = n_row // 2
    blk = tgt_geom.shape[1] // 2
    qn = src_nodes.shape[1]
    per, width = src_geom.shape[1], excite.shape[0]
    excite_rows = excite.T
    weight_rows = src_weights.transpose(0, 2, 1)
    reach = (near_order.shape[1] - 1) // 2
    near_pairs = min(reach // 2 + 1, chips // 2)
    depth = near_pairs * 2 * qn
    hbm = pl.BlockSpec(memory_space=pl.ANY)
    dma = pltpu.SemaphoreType.DMA
    f32, bf16 = jnp.float32, jnp.bfloat16
    return pl.pallas_call(
        kernel,
        out_shape=pltpu.VMEM((blk, width), f32),
        in_specs=[hbm] * 9,
        out_specs=pl.BlockSpec(memory_space=pltpu.VMEM),
        scratch_shapes=[
            pltpu.VMEM((chips, 2, ROWS, LANES), f32),
            pltpu.VMEM((chips, 2, 4, per, LANES), bf16),
            pltpu.VMEM((chips, 2, per, LANES), bf16),
            pltpu.VMEM((ROWS, LANES), f32),
            pltpu.VMEM((ROWS, LANES), f32),
            pltpu.VMEM((4, per, LANES), bf16),
            pltpu.VMEM((2, 3, qn, LANES), f32),
            pltpu.VMEM((6, 2 * blk, LANES), f32),
            pltpu.VMEM((ROWS, LANES), f32),
            pltpu.VMEM((near_pairs * 6, ORDERS, ROWS, LANES), f32),
            pltpu.VMEM((2, 2 * blk, qn), bf16),
            pltpu.VMEM((2, 2 * qn, depth), bf16),
            pltpu.VMEM((2, 2 * qn, depth), bf16),
            pltpu.VMEM((near_pairs, 2 * qn, 2 * width), bf16),
            pltpu.VMEM((2, 2 * blk, chips * 2 * per), bf16),
            pltpu.VMEM((blk, width), f32),
            pltpu.VMEM((blk, width), f32),
            pltpu.SMEM(wavenumber.shape, f32),
            pltpu.SMEM(near_order.shape, jnp.int32),
            pltpu.VMEM(tgt_geom.shape, f32),
            pltpu.VMEM(tgt_nodes.shape, f32),
            pltpu.VMEM(tgt_weights.shape, bf16),
            pltpu.VMEM(src_geom.shape, f32),
            pltpu.VMEM(excite_rows.shape, bf16),
            pltpu.VMEM(src_nodes.shape, f32),
            pltpu.VMEM(weight_rows.shape, bf16),
            dma((9,)),
            dma((n_row,)),
            dma((n_row,)),
            dma((chips,)),
            dma((chips,)),
            dma((2,)),
            pltpu.SemaphoreType.REGULAR((n_row + 1,)),
        ],
        compiler_params=pltpu.CompilerParams(collective_id=0, has_side_effects=True),
        name="slab",
    )(
        wavenumber,
        near_order,
        tgt_geom,
        tgt_nodes,
        tgt_weights,
        src_geom,
        excite_rows,
        src_nodes,
        weight_rows,
    )


def solution(mesh):
    return jax.shard_map(
        on_device,
        mesh=mesh,
        in_specs=(
            P("groups"),
            P(None, ("groups", "row")),
            P(None, ("groups", "row", "col")),
            P(None, ("groups", "row", "col")),
            P(None, ("groups", "row")),
            P(None, ("groups", "row")),
            P(None, None, ("groups", "row")),
            P(None, None, ("groups", "row", "col")),
            P(("groups", "row"), None),
        ),
        out_specs=P(("groups", "row", "col"), None),
        check_vma=False,
    )
```

```python
import math

import jax
import jax.numpy as jnp
import numpy as np
from jax import lax
from jax.experimental import pallas as pl
from jax.experimental.pallas import tpu as pltpu
from jax.sharding import PartitionSpec as P

ORDERS = 3
SOFT = 0.05
PI = math.pi
LANES = 128
ROWS = 8
MESH = pl.DeviceIdType.MESH
TN = (((0,), (0,)), ((), ()))


def fitted(function, terms):
    nodes = (np.cos((np.arange(terms) + 0.5) * np.pi / terms) + 1.0) / 8.0
    matrix = np.vander(nodes, terms, increasing=True)
    return [float(c) for c in np.linalg.solve(matrix, function(np.sqrt(nodes)))]


HALF_COS = fitted(lambda u: math.sqrt(2.0) * np.cos(np.pi * u), 5)
HALF_SIN = fitted(lambda u: math.sqrt(2.0) * np.sin(np.pi * u) / u, 4)


def horner(coefficients, y):
    total = coefficients[-1]
    for c in coefficients[-2::-1]:
        total = total * y + c
    return total


def wave_parts(squared):
    inverse = lax.rsqrt(squared)
    turns = squared * inverse
    u = turns - jnp.round(turns)
    y = u * u
    half = u * horner(HALF_SIN, y)
    return inverse, 1.0 - half * half, half * horner(HALF_COS, y)


def plus_i(first, second):
    half = second.shape[1] // 2
    swapped = pltpu.roll(second, half, 1)
    lane = lax.broadcasted_iota(jnp.int32, second.shape, 1)
    return first + jnp.where(lane < half, -swapped, swapped)


def split_two(value):
    high = value.astype(jnp.bfloat16)
    return high, (value - high.astype(jnp.float32)).astype(jnp.bfloat16)


def columns_of(rows):
    few, lanes = rows.shape
    pad = jnp.zeros((ROWS - few, lanes), jnp.float32)
    return jnp.concatenate([rows, pad], 0).T


def kernel(
    wave_hbm,
    order_hbm,
    tgt_hbm,
    tnode_hbm,
    tweight_hbm,
    geom_hbm,
    excite_hbm,
    snode_hbm,
    sweight_hbm,
    out_ref,
    small_all,
    bulk_all,
    far_all,
    middle,
    small_pack,
    bulk_pack,
    tnode_wide,
    tgt_wide,
    origin,
    scale_all,
    tests,
    green_high,
    green_low,
    moment,
    impedance,
    part_send,
    part_recv,
    wave_ref,
    order_ref,
    tgt_ref,
    tnode_ref,
    tweight_ref,
    geom_ref,
    excite_ref,
    snode_ref,
    sweight_ref,
    local,
    small_send,
    bulk_send,
    small_recv,
    bulk_recv,
    part_sem,
    ready,
):
    n_row = lax.axis_size("row")
    row = lax.axis_index("row")
    col = lax.axis_index("col")
    home = lax.rem(row, 2)
    place = row // 2
    chips = n_row // 2
    reach = (order_hbm.shape[1] - 1) // 2
    qn = snode_hbm.shape[1]
    tail = qn - LANES
    step_nodes = qn // ORDERS
    per = excite_hbm.shape[0]
    blk, width = out_ref.shape
    near_pairs = moment.shape[0]
    first_pair = jnp.clip(
        (row - reach - col + 1 + 4 * reach) // 4 - reach, 0, chips // 2 - near_pairs
    )
    mine = home == col
    lane = lax.broadcasted_iota(jnp.int32, (1, LANES), 1)

    loads = [
        pltpu.make_async_copy(here, there, local.at[index])
        for index, (here, there) in enumerate(
            (
                (snode_hbm, snode_ref),
                (geom_hbm, geom_ref),
                (excite_hbm, excite_ref),
                (sweight_hbm, sweight_ref),
                (wave_hbm, wave_ref),
                (tnode_hbm, tnode_ref),
                (tgt_hbm, tgt_ref),
                (order_hbm, order_ref),
                (tweight_hbm, tweight_ref),
            )
        )
    ]
    for load in loads:
        load.start()

    barrier = pltpu.get_barrier_semaphore()

    @pl.loop(2 * row + col + 1, 2 * n_row)
    def _(index):
        pl.semaphore_signal(
            barrier,
            inc=1,
            device_id={"row": index // 2, "col": lax.rem(index, 2)},
            device_id_type=MESH,
        )

    def heads_of(nodes):
        return jnp.where(lax.rem(place, 2) == 0, nodes[:, :LANES], nodes[:, tail:])

    loads[0].wait()
    nodes = snode_ref[...]
    gap = jnp.zeros((nodes.shape[0], LANES - tail), jnp.float32)
    ends = jnp.where(
        lax.rem(place, 2) == 0,
        jnp.concatenate([nodes[:, LANES:], gap], 1),
        jnp.concatenate([gap, nodes[:, :tail]], 1),
    )
    small_pack[0:3, :] = jnp.where(col == 0, heads_of(nodes), ends)
    loads[1].wait()
    pieces = LANES // (2 * per)
    spread = jnp.concatenate([geom_ref[...]] * (LANES // per), 1)
    begin = (2 * lax.rem(place, pieces) + col) * per
    inside = jnp.logical_and(lane >= begin, lane < begin + per)
    small_pack[3:4, :] = jnp.zeros((1, LANES), jnp.float32)
    small_pack[4:8, :] = jnp.where(inside, spread, 0.0)

    @pl.when(mine)
    def _():
        pltpu.make_async_copy(small_pack, small_all.at[place, col], small_recv.at[place]).start()

    def pack_bulk():
        loads[2].wait()
        bulk_pack[0] = excite_ref[...]
        loads[3].wait()
        bulk_pack[1] = sweight_ref[0, :, :LANES]
        bulk_pack[2] = jnp.concatenate(
            [sweight_ref[0, :, LANES:].astype(jnp.float32), sweight_ref[1, :, :tail].astype(jnp.float32)], 1
        ).astype(jnp.bfloat16)
        bulk_pack[3] = sweight_ref[1, :, tail:]

        @pl.when(mine)
        def _():
            pltpu.make_async_copy(bulk_pack, bulk_all.at[place, col], bulk_recv.at[place]).start()

    def small_to(chip):
        return pltpu.make_async_remote_copy(
            src_ref=small_pack,
            dst_ref=small_all.at[place, col],
            send_sem=small_send.at[chip],
            recv_sem=small_recv.at[place],
            device_id={"row": chip, "col": home},
            device_id_type=MESH,
        )

    def bulk_to(chip, near):
        return pltpu.make_async_remote_copy(
            src_ref=bulk_pack if near else bulk_pack.at[0],
            dst_ref=bulk_all.at[place, col] if near else far_all.at[place, col],
            send_sem=bulk_send.at[chip],
            recv_sem=bulk_recv.at[place],
            device_id={"row": chip, "col": home},
            device_id_type=MESH,
        )

    def is_near(chip):
        return jnp.logical_and(chip >= row - reach, chip <= row + reach)

    lower_end = row + jnp.where(home < col, 1, 0)
    higher_begin = row + jnp.where(home > col, 0, 1)

    def for_others(act, begin, end):
        @pl.loop(begin, end)
        def _(chip):
            @pl.when(jnp.logical_not(jnp.logical_and(mine, chip == row)))
            def _():
                act(chip)

    def tell(chip, core, slot):
        pl.semaphore_signal(
            ready.at[slot], inc=1, device_id={"row": chip, "col": core}, device_id_type=MESH
        )

    def tell_lower():
        @pl.loop(0, row // 2 + 1)
        def _(index):
            chip = 2 * index + col
            for core in range(2):

                @pl.when(2 * chip + core < 2 * row + col)
                def _():
                    tell(chip, core, row)

        @pl.when(jnp.logical_and(col == 1, home == 0))
        def _():
            tell(row, 0, n_row)

    def send_higher(chip):
        pl.semaphore_wait(ready.at[chip], 1)
        small_to(chip).start()
        bulk_act("start")(chip)

    def small_act(name):
        return lambda chip: getattr(small_to(chip), name)()

    def bulk_act(name):
        def act(chip):
            near = is_near(chip)

            @pl.when(near)
            def _():
                getattr(bulk_to(chip, True), name)()

            @pl.when(jnp.logical_not(near))
            def _():
                getattr(bulk_to(chip, False), name)()

        return act

    def order_of(block, chip):
        offset = jnp.clip(chip - row + reach, 0, 2 * reach)
        return jnp.where(is_near(chip), order_ref[block, offset] * step_nodes, 0)

    def chip_of(pair, slot):
        return 4 * (first_pair + pair) + 2 * slot + col

    def prepare():
        loads[4].wait()
        loads[5].wait()
        loads[7].wait()
        rate = wave_ref[0] * (0.5 / PI)
        origin[0:3] = jnp.broadcast_to(tnode_ref[:, 0:1], (3, LANES))
        cols = columns_of(tnode_ref[...])
        first = cols[0:1]
        cols = (cols - first) * rate
        for block in range(2):
            for axis in range(3):
                tnode_wide[block, axis] = jnp.broadcast_to(
                    cols[block * qn : (block + 1) * qn, axis : axis + 1], (qn, LANES)
                )

        @pl.loop(0, near_pairs)
        def _(pair):
            for block in range(2):
                even, odd = (order_of(block, chip_of(pair, slot)) for slot in range(2))
                middle = jnp.where(lane < tail, even, odd)
                for part, (limit, ahead) in enumerate(
                    (
                        (even, lane),
                        (middle, jnp.where(lane < tail, lane + LANES, lane - tail)),
                        (odd, lane + tail),
                    )
                ):
                    for group in range(ORDERS):
                        live = jnp.logical_and(ahead < limit, limit > group * step_nodes)
                        value = jnp.where(live, rate * (0.25 / PI), 0.0)
                        at = (3 * pair + part) * 2 + block
                        scale_all[at, group] = jnp.broadcast_to(value, (ROWS, LANES))

            for slot in range(2):

                @pl.when(jnp.logical_not(is_near(chip_of(pair, slot))))
                def _():
                    at = pl.ds(pl.multiple_of((3 * pair + 2 * slot) * LANES, LANES), LANES)
                    for block in range(2):
                        green_high[block, :, at] = jnp.zeros((2 * qn, LANES), jnp.bfloat16)
                        green_low[block, :, at] = jnp.zeros((2 * qn, LANES), jnp.bfloat16)

            @pl.when(jnp.logical_not(pair_live(pair)))
            def _():
                at = pl.ds(pl.multiple_of((3 * pair + 1) * LANES, LANES), LANES)
                for block in range(2):
                    green_high[block, :, at] = jnp.zeros((2 * qn, LANES), jnp.bfloat16)
                    green_low[block, :, at] = jnp.zeros((2 * qn, LANES), jnp.bfloat16)

        @pl.when(mine)
        def _():
            own = place - 2 * first_pair
            green_of(3 * (own // 2) + 2 * lax.rem(own, 2), heads_of(snode_ref[...]))

        loads[6].wait()
        cols = columns_of(tgt_ref[...])
        for axis in range(6):
            line = cols[:, axis : axis + 1]
            if axis < 3:
                line = (line - first[:, axis : axis + 1]) * rate
            tgt_wide[axis] = jnp.broadcast_to(line, (2 * blk, LANES))
        loads[8].wait()
        for block in range(2):
            at = slice(block * blk, (block + 1) * blk)
            for part in range(2):
                tests[block, part * blk : (part + 1) * blk] = tweight_ref[part, :, at].T

    def pair_live(pair):
        return jnp.logical_or(is_near(chip_of(pair, 0)), is_near(chip_of(pair, 1)))

    def scaled(places):
        rate = wave_ref[0] * (0.5 / PI)
        return (places - origin[0:3]) * rate, rate * rate * (SOFT * SOFT)

    def green_of(chunk, places):
        places, soft = scaled(places)
        s_x, s_y, s_z = (jnp.broadcast_to(places[i : i + 1], (step_nodes, LANES)) for i in range(3))
        at = pl.ds(pl.multiple_of(chunk * LANES, LANES), LANES)

        @pl.loop(0, 2)
        def _(block):
            for group in range(ORDERS):
                here = slice(group * step_nodes, (group + 1) * step_nodes)
                scale = jnp.broadcast_to(scale_all[chunk * 2 + block, group, 0:1], (step_nodes, LANES))
                d_x = tnode_wide[block, 0, here] - s_x
                d_y = tnode_wide[block, 1, here] - s_y
                d_z = tnode_wide[block, 2, here] - s_z
                squared = d_x * d_x + d_y * d_y + (d_z * d_z + soft)
                inverse, cosine, sine = wave_parts(squared)
                inverse = inverse * scale
                for part, value in enumerate((inverse * cosine, inverse * sine)):
                    high, low = split_two(value)
                    to = slice(part * qn + group * step_nodes, part * qn + (group + 1) * step_nodes)
                    green_high[block, to, at] = high
                    green_low[block, to, at] = low

    pack_bulk()

    @pl.when(2 * row + col > 0)
    def _():
        pl.semaphore_wait(barrier, 2 * row + col)

    tell_lower()
    urgent = jnp.minimum(lower_end, jnp.maximum(row - reach, 2))

    def both_act(chip):
        small_to(chip).start()
        bulk_act("start")(chip)

    for_others(both_act, 0, urgent)
    for_others(small_act("start"), urgent, lower_end)
    prepare()
    for_others(bulk_act("start"), urgent, lower_end)
    split = jnp.where(row == 0, jnp.minimum(reach + 2, n_row), n_row)
    for_others(send_higher, higher_begin, split)

    def wait_small(index):
        view = small_all.at[index]
        pltpu.make_async_copy(view, view, small_recv.at[index]).wait()

    def wait_bulk(index):
        near = is_near(2 * index + col)
        for view, go in ((bulk_all.at[index], near), (far_all.at[index], jnp.logical_not(near))):

            @pl.when(go)
            def _():
                pltpu.make_async_copy(view, view, bulk_recv.at[index]).wait()

    def inward(index, count):
        return jnp.where(row < chips, index, count - 1 - index)

    def green_some(begin, end):
        @pl.loop(begin, end)
        def _(turn):
            pair = inward(turn, near_pairs)
            base = 2 * (first_pair + pair)
            middle[0:3] = jnp.zeros((3, LANES), jnp.float32)

            @pl.loop(0, 2)
            def _(slot):
                slot = inward(slot, 2)
                chip = chip_of(pair, slot)

                @pl.when(is_near(chip))
                def _():
                    wait_small(base + slot)
                    middle[0:3] += small_all[base + slot, 1, 0:3]

                @pl.when(jnp.logical_and(is_near(chip), chip != row))
                def _():
                    green_of(3 * pair + 2 * slot, small_all[base + slot, 0, 0:3])

            @pl.when(pair_live(pair))
            def _():
                green_of(3 * pair + 1, middle[0:3])

    done = jnp.where(row == 0, 1, 0)
    green_some(0, done)
    for_others(send_higher, split, n_row)

    @pl.when(jnp.logical_and(col == 0, home == 0))
    def _():
        pl.semaphore_wait(ready.at[n_row], 1)

    green_some(done, near_pairs)

    def for_chips(act, near):
        @pl.loop(0, chips)
        def _(index):
            go = is_near(2 * index + col)

            @pl.when(go if near else jnp.logical_not(go))
            def _():
                act(index)

    def impedance_of(chunk):
        packed = small_all[pl.ds(chunk * pieces, pieces), :, 4:8, :].reshape(2 * pieces, 4, LANES)
        packed = jnp.sum(packed, 0)
        places, soft = scaled(packed[0:3])
        area = packed[3:4] * (wave_ref[0] * (0.125 / PI / PI))
        at = pl.ds(pl.multiple_of(chunk * LANES, LANES), LANES)
        for part in range(4):
            block, half = part // 2, part % 2
            count = blk // 2
            here = slice(part * count, (part + 1) * count)
            d_x = tgt_wide[0, here] - places[0:1]
            d_y = tgt_wide[1, here] - places[1:2]
            d_z = tgt_wide[2, here] - places[2:3]
            squared = d_x * d_x + d_y * d_y + (d_z * d_z + soft)
            inverse, cosine, sine = wave_parts(squared)
            along = tgt_wide[3, here] * d_x + tgt_wide[4, here] * d_y + tgt_wide[5, here] * d_z
            along = along * inverse
            scale = area * inverse
            green_re = scale * cosine
            green_im = scale * sine
            factor_re = 1.0 - along
            factor_im = along * (inverse * (-0.5 / PI))
            for side, value in enumerate(
                (
                    green_re * factor_re - green_im * factor_im,
                    green_re * factor_im + green_im * factor_re,
                )
            ):
                to = slice(side * blk + half * count, side * blk + (half + 1) * count)
                impedance[block, to, at] = value.astype(jnp.bfloat16)

    for_chips(wait_small, False)

    @pl.loop(0, chips // pieces)
    def _(chunk):
        impedance_of(chunk)

    @pl.loop(0, chips)
    def _(index):
        wait_bulk(index)

    for slot in range(2 * near_pairs):
        index = 2 * first_pair + slot
        rows = bulk_all[index, :, 0].reshape(2 * per, width)
        weights = jnp.concatenate(
            [bulk_all[index, :, 1 + part].reshape(2 * per, LANES) for part in range(3)], 1
        )
        both = lax.dot_general(weights, rows, TN, preferred_element_type=jnp.float32)
        value = plus_i(both[:qn], both[qn:])
        value = jnp.where(is_near(2 * index + col), value, 0.0)
        high, low = split_two(value)
        at = slice((slot % 2) * qn, (slot % 2 + 1) * qn)
        moment[slot // 2, at, 0:width] = high
        moment[slot // 2, at, width:] = low

    def near_part(block):
        right = moment[...].reshape(near_pairs * 2 * qn, 2 * width)
        both = jnp.dot(green_high[block], right, preferred_element_type=jnp.float32)
        both = both[:, :width] + both[:, width:]
        both = both + jnp.dot(green_low[block], right[:, :width], preferred_element_type=jnp.float32)
        high, low = split_two(plus_i(both[:qn], both[qn:]))
        product = jnp.dot(tests[block], jnp.concatenate([high, low], 1), preferred_element_type=jnp.float32)
        return product[:, :width] + product[:, width:]

    def far_part(block, both):
        def far_step(chunk, total):
            rows = []
            for piece in range(pieces):
                index = chunk * pieces + piece
                rows.append(
                    jnp.where(is_near(2 * index + col), bulk_all[index, :, 0], far_all[index]).reshape(
                        2 * per, width
                    )
                )
            at = pl.ds(pl.multiple_of(chunk * LANES, LANES), LANES)
            return total + jnp.dot(
                impedance[block, :, at], jnp.concatenate(rows, 0), preferred_element_type=jnp.float32
            )

        if chips == pieces:
            both = far_step(0, both)
        else:
            both = lax.fori_loop(0, chips // pieces, far_step, both)
        return plus_i(both[:blk], both[blk:])

    swap = pltpu.make_async_remote_copy(
        src_ref=part_send,
        dst_ref=part_recv,
        send_sem=part_sem.at[0],
        recv_sem=part_sem.at[1],
        device_id={"col": 1 - col},
        device_id_type=MESH,
    )
    part_send[...] = far_part(1 - col, near_part(1 - col))
    swap.start()
    out_ref[...] = far_part(col, near_part(col))
    for_others(small_act("wait_send"), 0, n_row)
    for_others(bulk_act("wait_send"), 0, n_row)
    swap.wait_recv()
    out_ref[...] += part_recv[...]
    swap.wait_send()


def on_device(
    wavenumber,
    tgt_geom,
    src_geom,
    excite,
    tgt_nodes,
    src_nodes,
    tgt_weights,
    src_weights,
    near_order,
):
    n_row = lax.axis_size("row")
    chips = n_row // 2
    blk = tgt_geom.shape[1] // 2
    qn = src_nodes.shape[1]
    per, width = src_geom.shape[1], excite.shape[0]
    excite_rows = excite.T
    weight_rows = src_weights.transpose(0, 2, 1)
    reach = (near_order.shape[1] - 1) // 2
    near_pairs = min(reach // 2 + 1, chips // 2)
    depth = near_pairs * 2 * qn
    hbm = pl.BlockSpec(memory_space=pl.ANY)
    dma = pltpu.SemaphoreType.DMA
    f32, bf16 = jnp.float32, jnp.bfloat16
    return pl.pallas_call(
        kernel,
        out_shape=pltpu.VMEM((blk, width), f32),
        in_specs=[hbm] * 9,
        out_specs=pl.BlockSpec(memory_space=pltpu.VMEM),
        scratch_shapes=[
            pltpu.VMEM((chips, 2, ROWS, LANES), f32),
            pltpu.VMEM((chips, 2, 4, per, LANES), bf16),
            pltpu.VMEM((chips, 2, per, LANES), bf16),
            pltpu.VMEM((ROWS, LANES), f32),
            pltpu.VMEM((ROWS, LANES), f32),
            pltpu.VMEM((4, per, LANES), bf16),
            pltpu.VMEM((2, 3, qn, LANES), f32),
            pltpu.VMEM((6, 2 * blk, LANES), f32),
            pltpu.VMEM((ROWS, LANES), f32),
            pltpu.VMEM((near_pairs * 6, ORDERS, ROWS, LANES), f32),
            pltpu.VMEM((2, 2 * blk, qn), bf16),
            pltpu.VMEM((2, 2 * qn, depth), bf16),
            pltpu.VMEM((2, 2 * qn, depth), bf16),
            pltpu.VMEM((near_pairs, 2 * qn, 2 * width), bf16),
            pltpu.VMEM((2, 2 * blk, chips * 2 * per), bf16),
            pltpu.VMEM((blk, width), f32),
            pltpu.VMEM((blk, width), f32),
            pltpu.SMEM(wavenumber.shape, f32),
            pltpu.SMEM(near_order.shape, jnp.int32),
            pltpu.VMEM(tgt_geom.shape, f32),
            pltpu.VMEM(tgt_nodes.shape, f32),
            pltpu.VMEM(tgt_weights.shape, bf16),
            pltpu.VMEM(src_geom.shape, f32),
            pltpu.VMEM(excite_rows.shape, bf16),
            pltpu.VMEM(src_nodes.shape, f32),
            pltpu.VMEM(weight_rows.shape, bf16),
            dma((9,)),
            dma((n_row,)),
            dma((n_row,)),
            dma((chips,)),
            dma((chips,)),
            dma((2,)),
            pltpu.SemaphoreType.REGULAR((n_row + 1,)),
        ],
        compiler_params=pltpu.CompilerParams(collective_id=0, has_side_effects=True),
        name="slab",
    )(
        wavenumber,
        near_order,
        tgt_geom,
        tgt_nodes,
        tgt_weights,
        src_geom,
        excite_rows,
        src_nodes,
        weight_rows,
    )


def solution(mesh):
    return jax.shard_map(
        on_device,
        mesh=mesh,
        in_specs=(
            P("groups"),
            P(None, ("groups", "row")),
            P(None, ("groups", "row", "col")),
            P(None, ("groups", "row", "col")),
            P(None, ("groups", "row")),
            P(None, ("groups", "row")),
            P(None, None, ("groups", "row")),
            P(None, None, ("groups", "row", "col")),
            P(("groups", "row"), None),
        ),
        out_specs=P(("groups", "row", "col"), None),
        check_vma=False,
    )
```
